512 devices in a mesh: row: 32 (over z, y_hi, core), col: 16 (over y_lo, x).
Axes of the slice: x: 4, y: 8 (y_hi: 2, y_lo: 4; y = y_hi * 4 + y_lo), z: 8, core: 2. Of those that a mesh axis runs over, the one named last changes fastest.
Arguments:
- patches: bfloat16 [1024, 1024, 256], P('row', 'col'), may hold values from -6 to 6
- norm_gain: float32 [256], replicated, may hold values from 0.1 to 1.9
- w_first: bfloat16 [2, 4, 64, 64], replicated, may hold values from -0.5 to 0.5
- w_second: bfloat16 [2, 4, 64, 64], replicated, may hold values from -0.5 to 0.5
- depth_kernel: float32 [3, 3, 256], replicated, may hold values from -2 to 2
Outputs:
- mixed: bfloat16 [1024, 1024, 256], P('row', 'col')
The draws below stay inside these ranges and needn't reach their ends.
All inputs are finite; a program needn't handle non-finite values.
Results may differ from the reference program's by a relative error of at most 0.008.
Values may be sent and summed in bfloat16 or wider, within the bound.
No kernel may reach another device: no remote copies, remote signals or barrier semaphores. Data moves between devices by JAX's collectives and lax.ppermute only.
A program may use at most 64 MiB of HBM per device.

```python
import math
import jax
import jax.numpy as jnp
from jax import lax

BLOCK = 64
BLOCKS = 4
CH = 256
GRID_H = 1024
GRID_W = 1024


def level_of(rng, extent, split, low, top_value):
    level, own = 1.0, jax.random.fold_in(rng, 6)
    for position, shards_of in split:
        draws = jnp.exp(jax.random.uniform(jax.random.fold_in(own, position), (shards_of,), jnp.float32, low / len(split), top_value / len(split)))
        level = level * jnp.repeat(draws, extent[position] // shards_of).reshape([-1 if axis == position else 1 for axis in range(len(extent))])
    return level


def noise(stream_key, extent, scale, reach, pieces=(), kind=jnp.bfloat16):
    gain = level_of(stream_key, extent, pieces, -0.22, 0.18) if pieces else 1.0
    entries = jax.random.normal(stream_key, extent, jnp.float32) * scale * gain
    return jnp.minimum(jnp.maximum(entries, -reach), reach).astype(kind)


def setup_inputs(seed: int = 0) -> dict:
    key_of = jax.random.split(jax.random.key(seed), 6)
    return {
        "patches": noise(key_of[0], (GRID_H, GRID_W, CH), 1.0, 6.0, ((0, 32), (1, 16))),
        "norm_gain": jnp.clip(1.0 + 0.18 * jax.random.normal(key_of[1], (CH,), jnp.float32), 0.1, 1.9),
        "w_first": noise(key_of[2], (2, BLOCKS, BLOCK, BLOCK), (2 * BLOCK) ** -0.5, 0.5),
        "w_second": noise(key_of[3], (2, BLOCKS, BLOCK, BLOCK), (2 * BLOCK) ** -0.5, 0.5),
        "depth_kernel": noise(key_of[4], (3, 3, CH), 9 ** -0.5, 2.0, (), jnp.float32),
    }


def phase_table(first_idx, second_idx, length):
    product = first_idx[:, None] * second_idx[None, :] % length
    phase = product.astype(jnp.float32) * (2.0 * math.pi / length)
    return (jnp.cos(phase).astype(jnp.bfloat16), jnp.sin(phase).astype(jnp.bfloat16))

def shrink(values):
    level = 0.25
    return jnp.where(values > level, values - level, jnp.where(values < -level, values + level, 0.0 * values))

def reference(patches, norm_gain, w_first, w_second, depth_kernel):
    patch_grid_height, grid_w, chans = patches.shape
    half = grid_w // 2
    xf = patches.astype(jnp.float32)
    mean = lax.optimization_barrier(jnp.mean(xf, axis=-1, keepdims=True))
    var = lax.optimization_barrier(jnp.mean((xf - mean) ** 2, axis=-1, keepdims=True))
    normed = ((xf - mean) * lax.rsqrt(var + 1e-05) * norm_gain).astype(jnp.bfloat16)
    cos_w, sin_w = phase_table(jnp.arange(grid_w, dtype=jnp.int32), jnp.arange(half, dtype=jnp.int32), grid_w)
    cos_h, sin_h = phase_table(jnp.arange(patch_grid_height, dtype=jnp.int32), jnp.arange(patch_grid_height, dtype=jnp.int32), patch_grid_height)
    cosine_width_factor, sine_width_factor = (cos_w.astype(jnp.float32), sin_w.astype(jnp.float32))
    cosine_height_factor, sine_height_factor = (cos_h.astype(jnp.float32), sin_h.astype(jnp.float32))
    filter_coefficient = jnp.where(jnp.arange(half) == 0, 1.0, 2.0).astype(jnp.float32)
    width_factors = 1.0 / math.sqrt(grid_w)
    height_factors = 1.0 / math.sqrt(patch_grid_height)
    blocks = w_first.shape[1]
    width = w_first.shape[2]
    normed_blocks = normed.reshape(patch_grid_height, grid_w, blocks, width).transpose(2, 0, 1, 3)
    first_b = w_first.transpose(1, 0, 2, 3)
    second_b = w_second.transpose(1, 0, 2, 3)

    def one_block(packed):
        block, wa, wb = packed
        nb = block.astype(jnp.float32)
        wre = (jnp.einsum('hwc,wk->hkc', nb, cosine_width_factor) * width_factors).astype(jnp.bfloat16).astype(jnp.float32)
        wim = (-jnp.einsum('hwc,wk->hkc', nb, sine_width_factor) * width_factors).astype(jnp.bfloat16).astype(jnp.float32)
        zre = (height_factors * (jnp.einsum('qh,hkc->qkc', cosine_height_factor, wre) + jnp.einsum('qh,hkc->qkc', sine_height_factor, wim))).astype(jnp.bfloat16).astype(jnp.float32)
        zim = (height_factors * (jnp.einsum('qh,hkc->qkc', cosine_height_factor, wim) - jnp.einsum('qh,hkc->qkc', sine_height_factor, wre))).astype(jnp.bfloat16).astype(jnp.float32)
        a0, a1 = (wa[0].astype(jnp.float32), wa[1].astype(jnp.float32))
        b0, b1 = (wb[0].astype(jnp.float32), wb[1].astype(jnp.float32))
        hre = jnp.tanh(jnp.einsum('qkc,cd->qkd', zre, a0) - jnp.einsum('qkc,cd->qkd', zim, a1)).astype(jnp.bfloat16).astype(jnp.float32)
        him = jnp.tanh(jnp.einsum('qkc,cd->qkd', zre, a1) + jnp.einsum('qkc,cd->qkd', zim, a0)).astype(jnp.bfloat16).astype(jnp.float32)
        spectrum_real = shrink(jnp.einsum('qkc,cd->qkd', hre, b0) - jnp.einsum('qkc,cd->qkd', him, b1)).astype(jnp.bfloat16).astype(jnp.float32)
        spectrum_imaginary = shrink(jnp.einsum('qkc,cd->qkd', hre, b1) + jnp.einsum('qkc,cd->qkd', him, b0)).astype(jnp.bfloat16).astype(jnp.float32)
        value_real = (height_factors * (jnp.einsum('eu,ear->uar', cosine_height_factor, spectrum_real) - jnp.einsum('eu,ear->uar', sine_height_factor, spectrum_imaginary))).astype(jnp.bfloat16).astype(jnp.float32)
        value_imaginary = (height_factors * (jnp.einsum('eu,ear->uar', cosine_height_factor, spectrum_imaginary) + jnp.einsum('eu,ear->uar', sine_height_factor, spectrum_real))).astype(jnp.bfloat16).astype(jnp.float32)
        spectrum_values = width_factors * (jnp.einsum('osl,xs->oxl', value_real, cosine_width_factor * filter_coefficient) - jnp.einsum('osl,xs->oxl', value_imaginary, sine_width_factor * filter_coefficient))
        return spectrum_values.astype(jnp.bfloat16)
    spectral = lax.map(one_block, (normed_blocks, first_b, second_b))
    spectral = spectral.transpose(1, 2, 0, 3).reshape(patch_grid_height, grid_w, chans)
    nf = normed.astype(jnp.float32)
    conv = jnp.zeros((patch_grid_height, grid_w, chans), jnp.float32)
    for i in range(3):
        for j in range(3):
            conv = conv + jnp.roll(nf, (1 - i, 1 - j), axis=(0, 1)) * depth_kernel[i, j]
    return (xf + spectral.astype(jnp.float32) + conv).astype(jnp.bfloat16)
```

```python
import math

import jax
import jax.numpy as jnp
import numpy as np
from jax import lax
from jax.experimental import pallas as pl
from jax.experimental.pallas import tpu as pltpu
from jax.sharding import Mesh
from jax.sharding import PartitionSpec as P

TURN = 1024
CHUNKS = 2
F32 = jnp.float32
BF16 = jnp.bfloat16


def cos_of(idx):
    return jnp.cos((idx % TURN).astype(F32) * (2.0 * math.pi / TURN))


def sin_of(idx):
    return jnp.sin((idx % TURN).astype(F32) * (2.0 * math.pi / TURN))


def outer_table(e1, e2, f1, f2):
    e1, e2, f1, f2 = lax.optimization_barrier((e1, e2, f1, f2))
    out = e1[:, None, :] * f1[None] + e2[:, None, :] * f2[None]
    return out.astype(BF16).reshape(e1.shape[0] * f1.shape[0], e1.shape[1])


def phase_table(ia, ib, scale):
    return outer_table(cos_of(ia), sin_of(ia), cos_of(ib) * scale, -sin_of(ib) * scale)


def column(values):
    return jnp.asarray(values, jnp.int32)[:, None]


def split(idx, *sizes):
    out = []
    for s in reversed(sizes):
        out.append(idx % s)
        idx = idx // s
    return out[::-1]


def make_tables():
    lane = jnp.arange(1024, dtype=jnp.int32)[None, :]
    scale = 1.0 / 32.0
    a16 = jnp.arange(16, dtype=jnp.int32)[:, None]
    b64 = jnp.arange(64, dtype=jnp.int32)[:, None]
    pl_, ri, i = split(b64, 8, 2, 4)
    fwd_w = phase_table(32 * a16 * lane, (4 * pl_ + i) * lane + 256 * ri, scale)
    p, lri, li = split(lane, 128, 2, 4)
    k = 4 * p + li
    weight = jnp.where(k == 0, 1.0, 2.0).astype(F32) * scale
    inv_w = phase_table(64 * a16 * k, b64 * k + 256 * lri, weight)
    qhh, ro, qhl = split(a16, CHUNKS, 2, 8 // CHUNKS)
    qh = qhh * (8 // CHUNKS) + qhl
    bi, ql = split(b64, 4, 16)
    mask = jnp.where(bi == li, scale, 0.0).astype(F32)
    fwd_h = phase_table(128 * qh * p + 256 * (ro - lri), 8 * ql * p, mask)
    lqhh, lro, lqhl, lli, lql = split(lane, CHUNKS, 2, 8 // CHUNKS, 4, 16)
    lq0 = 16 * (lqhh * (8 // CHUNKS) + lqhl) + lql
    mask_t = jnp.where(i == lli, scale, 0.0).astype(F32)
    inv_h = phase_table(64 * a16 * lq0, 8 * pl_ * lq0 + 256 * (lro - ri), mask_t)
    t, gri, e = split(a16, 4, 2, 2)
    gro, gh8, gc = split(lane, 2, 8, 64)
    e1 = cos_of(128 * (2 * t + e) * gh8 - 256 * (gro - gri))
    eye = jnp.where(b64 == gc, 1.0, 0.0).astype(F32)
    e1, eye = lax.optimization_barrier((e1, eye))
    eight = (e1[:, None, :] * eye[None]).astype(BF16).reshape(1024, 1024)
    q0 = jnp.arange(128, dtype=jnp.int32)[:, None]
    h8 = jnp.arange(512, dtype=jnp.int32)[None, :] // 64
    return fwd_w, inv_w, fwd_h, inv_h, eight, cos_of(q0 * h8), sin_of(q0 * h8)


def first_layer(w0, w1):
    lane = jnp.arange(1024, dtype=jnp.int32)[None, :]
    ri, h8 = split(jnp.arange(16, dtype=jnp.int32)[:, None], 2, 8)
    t, ro, e, _ = split(lane, 4, 2, 2, 64)
    angle = 128 * (2 * t + e) * h8 + 256 * (ro - ri)
    return outer_table(
        cos_of(angle), sin_of(angle), jnp.tile(w0.astype(F32), (1, 16)), jnp.tile(w1.astype(F32), (1, 16))
    )


def second_layer(w0, w1):
    z = jnp.zeros_like(w0)
    b0 = jnp.block([[w0, z], [z, w0]])
    b1 = jnp.block([[w1, z], [z, w1]])
    return jnp.block([[b0, b1], [-b1, b0]])


def norm_kernel(x_ref, gain_ref, normed_ref, packed_ref):
    low = lax.broadcasted_iota(jnp.int32, (64, 128), 1) < 64

    def normed_row(h):
        xf = x_ref[h].astype(F32)
        mean = jnp.mean(xf, axis=-1, keepdims=True)
        d = xf - mean
        var = jnp.mean(d * d, axis=-1, keepdims=True)
        return d * lax.rsqrt(var + 1e-05) * gain_ref[...]

    for t in range(4):
        a, b = normed_row(2 * t), normed_row(2 * t + 1)
        normed_ref[2 * t] = a.astype(BF16)
        normed_ref[2 * t + 1] = b.astype(BF16)
        lanes = slice(128 * t, 128 * t + 128)
        for m in range(2):
            am, bm = a[:, 128 * m : 128 * m + 128], b[:, 128 * m : 128 * m + 128]
            ar, br = pltpu.roll(am, 64, 1), pltpu.roll(bm, 64, 1)
            packed_ref[2 * m, :, lanes] = jnp.where(low, am, br).astype(BF16)
            packed_ref[2 * m + 1, :, lanes] = jnp.where(low, ar, bm).astype(BF16)


def norm_and_pack(patches, gain):
    return pl.pallas_call(
        norm_kernel,
        grid=(4,),
        in_specs=[
            pl.BlockSpec((8, 64, 256), lambda g: (g, 0, 0)),
            pl.BlockSpec((1, 256), lambda g: (0, 0)),
        ],
        out_specs=[
            pl.BlockSpec((8, 64, 256), lambda g: (g, 0, 0)),
            pl.BlockSpec((4, 64, 512), lambda g: (g, 0, 0)),
        ],
        out_shape=[
            jax.ShapeDtypeStruct((32, 64, 256), BF16),
            jax.ShapeDtypeStruct((16, 64, 512), BF16),
        ],
        name="norm_pack",
    )(patches, gain.reshape(1, 256))


def final_kernel(base_ref, home_ref, out_ref):
    low = lax.broadcasted_iota(jnp.int32, (64, 128), 1) < 64
    for t in range(4):
        lanes = slice(128 * t, 128 * t + 128)
        for m in range(2):
            u = home_ref[2 * m, :, lanes].astype(F32)
            v = home_ref[2 * m + 1, :, lanes].astype(F32)
            even = jnp.where(low, u, pltpu.roll(v, 64, 1))
            odd = jnp.where(low, pltpu.roll(u, 64, 1), v)
            chans = slice(128 * m, 128 * m + 128)
            out_ref[2 * t, :, chans] = (base_ref[2 * t, :, chans] + even).astype(BF16)
            out_ref[2 * t + 1, :, chans] = (base_ref[2 * t + 1, :, chans] + odd).astype(BF16)


def unpack_and_add(base, home):
    return pl.pallas_call(
        final_kernel,
        grid=(4,),
        in_specs=[
            pl.BlockSpec((8, 64, 256), lambda g: (g, 0, 0)),
            pl.BlockSpec((4, 64, 512), lambda g: (g, 0, 0)),
        ],
        out_specs=pl.BlockSpec((8, 64, 256), lambda g: (g, 0, 0)),
        out_shape=jax.ShapeDtypeStruct((32, 64, 256), BF16),
        name="unpack_add",
    )(base, home)


def dot(a, b):
    return jnp.dot(a, b, preferred_element_type=F32)


def middle_kernel(
    z_any, fwd_any, first_any, eight_any, inv_any, second_ref, cos_ref, sin_ref, out_ref,
    z, fwd, first, eight, inv, held, sems,
):
    copies = []
    for n, (src, dst) in enumerate(
        ((z_any, z), (fwd_any, fwd), (first_any, first), (eight_any, eight), (inv_any, inv))
    ):
        copy = pltpu.make_async_copy(src, dst, sems.at[n])
        copy.start()
        copies.append(copy)
    copies[0].wait()
    copies[1].wait()
    rows = 512 // CHUNKS
    groups = 8 // CHUNKS
    for m in range(CHUNKS):
        u = dot(fwd[2 * rows * m : 2 * rows * (m + 1), :], z[...])
        shape = (groups, 4, 16, 512)
        ur, ui = u[:rows].reshape(shape), u[rows:].reshape(shape)
        c = cos_ref[16 * groups * m : 16 * groups * (m + 1), :].reshape(groups, 1, 16, 512)
        s = sin_ref[16 * groups * m : 16 * groups * (m + 1), :].reshape(groups, 1, 16, 512)
        vr = (ur * c + ui * s).astype(BF16).reshape(rows, 512)
        vi = (ui * c - ur * s).astype(BF16).reshape(rows, 512)
        if m == 0:
            copies[2].wait()
        hidden = jnp.tanh(dot(vr, first[:512, :]) + dot(vi, first[512:, :])).astype(BF16)
        parts = []
        for t in range(4):
            v = dot(hidden[:, 256 * t : 256 * t + 256], second_ref[...])
            v = jnp.where(v > 0.25, v - 0.25, jnp.where(v < -0.25, v + 0.25, 0.0 * v))
            parts.append(v.astype(BF16))
        if m == 0:
            copies[3].wait()
        y = dot(jnp.concatenate(parts, axis=1), eight[...])
        yr, yi = y[:, :512].reshape(shape), y[:, 512:].reshape(shape)
        held[2 * rows * m : 2 * rows * m + rows, :] = (yr * c - yi * s).astype(BF16).reshape(rows, 512)
        held[2 * rows * m + rows : 2 * rows * (m + 1), :] = (
            (yi * c + yr * s).astype(BF16).reshape(rows, 512)
        )
    copies[4].wait()
    for m in range(4):
        out_ref[256 * m : 256 * m + 256, :] = dot(inv[256 * m : 256 * m + 256, :], held[...]).astype(BF16)


def middle(z, fwd, first, eight, inv, second, cos, sin):
    anywhere = pl.BlockSpec(memory_space=pl.ANY)
    vmem = pl.BlockSpec(memory_space=pltpu.VMEM)
    return pl.pallas_call(
        middle_kernel,
        in_specs=[anywhere] * 5 + [vmem] * 3,
        out_specs=vmem,
        out_shape=jax.ShapeDtypeStruct((1024, 512), BF16),
        scratch_shapes=[
            pltpu.VMEM((1024, 512), BF16),
            pltpu.VMEM((1024, 1024), BF16),
            pltpu.VMEM((1024, 1024), BF16),
            pltpu.VMEM((1024, 1024), BF16),
            pltpu.VMEM((1024, 1024), BF16),
            pltpu.VMEM((1024, 512), BF16),
            pltpu.SemaphoreType.DMA((5,)),
        ],
        compiler_params=pltpu.CompilerParams(vmem_limit_bytes=40 * 1024 * 1024),
        name="filter_rows",
    )(z, fwd, first, eight, inv, second, cos, sin)


def with_halo(shard, sides, width):
    for axis, dim in sides:
        devices, length = (lax.axis_size(axis), shard.shape[dim])
        up = [(i, (i + 1) % devices) for i in range(devices)]
        down = [(j, i) for i, j in up]
        last = lax.slice_in_dim(shard, length - width, length, axis=dim)
        leading = lax.slice_in_dim(shard, 0, width, axis=dim)
        before = lax.ppermute(last, axis, up)
        after = lax.ppermute(leading, axis, down)
        shard = jnp.concatenate([before, shard, after], axis=dim)
    return shard


def local(patches, norm_gain, w_first, w_second, depth_kernel):
    rows_dev, cols_dev, chans = patches.shape
    normed, packed = norm_and_pack(patches, norm_gain)
    lines = lax.all_to_all(packed, ("yl", "x"), 0, 0, tiled=True).reshape(1024, 512)

    fwd_w, inv_w, fwd_h, inv_h, eight, cos, sin = make_tables()
    block = lax.axis_index("x")
    wf = lax.dynamic_index_in_dim(w_first, block, 1, keepdims=False)
    ws = lax.dynamic_index_in_dim(w_second, block, 1, keepdims=False)
    first = first_layer(wf[0], wf[1])
    second = second_layer(ws[0], ws[1])

    padded = with_halo(normed, (("row", 0), (("yl", "x"), 1)), 1)
    base = patches.astype(F32)
    for i in range(3):
        for j in range(3):
            base = base + padded[i : i + rows_dev, j : j + cols_dev] * depth_kernel[i, j]

    freqs = dot(fwd_w, lines).astype(BF16).reshape(128, 8, 512)
    whole = lax.all_to_all(freqs, ("row", "yl"), 0, 0, tiled=True).reshape(1024, 512)
    filtered = middle(whole, fwd_h, first, eight, inv_h, second, cos, sin)
    back = lax.all_to_all(filtered.reshape(128, 8, 512), ("row", "yl"), 0, 0, tiled=True)
    spectral = dot(inv_w, back.reshape(1024, 512)).astype(BF16).reshape(16, 64, 512)
    home = lax.all_to_all(spectral, ("yl", "x"), 0, 0, tiled=True)
    return unpack_and_add(base, home)


def solution(mesh):
    fine = Mesh(np.asarray(mesh.devices).reshape(32, 4, 4), ("row", "yl", "x"))
    return jax.shard_map(
        local,
        mesh=fine,
        in_specs=(P("row", ("yl", "x"), None), P(), P(), P(), P()),
        out_specs=P("row", ("yl", "x"), None),
        check_vma=False,
    )
```

```python
import functools
import math

import jax
import jax.numpy as jnp
import numpy as np
from jax import lax
from jax.experimental import pallas as pl
from jax.experimental.pallas import tpu as pltpu
from jax.sharding import Mesh
from jax.sharding import PartitionSpec as P

TURN = 1024
CHUNKS = 2
MIB = 1024 * 1024
F32 = jnp.float32
BF16 = jnp.bfloat16


def cos_of(idx):
    return jnp.cos((idx % TURN).astype(F32) * (2.0 * math.pi / TURN))


def sin_of(idx):
    return jnp.sin((idx % TURN).astype(F32) * (2.0 * math.pi / TURN))


def expand_kernel(steps, *refs):
    out_ref, half = refs[-1], (len(refs) - 1) // 2
    first = 0 if steps == 16 else steps * pl.program_id(0)

    def step(a, carry):
        v = None
        for e_ref, f_ref in zip(refs[:half], refs[half:-1]):
            term = e_ref[pl.ds(first + a, 1), :] * f_ref[...]
            v = term if v is None else v + term
        out_ref[pl.ds(pl.multiple_of(64 * a, 64), 64), :] = v.astype(BF16)
        return carry

    lax.fori_loop(0, steps, step, 0)


def outer_table(space, es, fs):
    whole = pl.BlockSpec(memory_space=pltpu.VMEM)
    stay = space == pltpu.VMEM
    return pl.pallas_call(
        functools.partial(expand_kernel, 16 if stay else 4),
        grid=(1,) if stay else (4,),
        in_specs=[whole] * (len(es) + len(fs)),
        out_specs=whole if stay else pl.BlockSpec((256, 1024), lambda g: (g, 0)),
        out_shape=space((1024, 1024), BF16),
        cost_estimate=pl.CostEstimate(flops=3 * 2**20, bytes_accessed=2**21, transcendentals=0),
        compiler_params=pltpu.CompilerParams(vmem_limit_bytes=4 * MIB),
        name="expand_table",
    )(*es, *fs)


def phase_table(space, ia, ib, scale):
    return outer_table(space, (cos_of(ia), sin_of(ia)), (cos_of(ib) * scale, -sin_of(ib) * scale))


def column(values):
    return jnp.asarray(values, jnp.int32)[:, None]


def split(idx, *sizes):
    out = []
    for s in reversed(sizes):
        out.append(idx % s)
        idx = idx // s
    return out[::-1]


def make_tables():
    lane = jnp.arange(1024, dtype=jnp.int32)[None, :]
    scale = 1.0 / 32.0
    a16 = jnp.arange(16, dtype=jnp.int32)[:, None]
    b64 = jnp.arange(64, dtype=jnp.int32)[:, None]
    pl_, ri, i = split(b64, 8, 2, 4)
    fwd_w = phase_table(pltpu.VMEM, 32 * a16 * lane, (4 * pl_ + i) * lane + 256 * ri, scale)
    p, lri, li = split(lane, 128, 2, 4)
    k = 4 * p + li
    weight = jnp.where(k == 0, 1.0, 2.0).astype(F32) * scale
    inv_w = phase_table(pltpu.VMEM, 64 * a16 * k, b64 * k + 256 * lri, weight)
    qhh, ro, qhl = split(a16, CHUNKS, 2, 8 // CHUNKS)
    qh = qhh * (8 // CHUNKS) + qhl
    bi, ql = split(b64, 4, 16)
    mask = jnp.where(bi == li, scale, 0.0).astype(F32)
    fwd_h = phase_table(pltpu.VMEM, 128 * qh * p + 256 * (ro - lri), 8 * ql * p, mask)
    lqhh, lro, lqhl, lli, lql = split(lane, CHUNKS, 2, 8 // CHUNKS, 4, 16)
    lq0 = 16 * (lqhh * (8 // CHUNKS) + lqhl) + lql
    mask_t = jnp.where(i == lli, scale, 0.0).astype(F32)
    inv_h = phase_table(pltpu.HBM, 64 * a16 * lq0, 8 * pl_ * lq0 + 256 * (lro - ri), mask_t)
    t, gri, e = split(a16, 4, 2, 2)
    gro, gh8, gc = split(lane, 2, 8, 64)
    e1 = cos_of(128 * (2 * t + e) * gh8 - 256 * (gro - gri))
    eye = jnp.where(b64 == gc, 1.0, 0.0).astype(F32)
    eight = outer_table(pltpu.HBM, (e1,), (eye,))
    q0 = jnp.arange(128, dtype=jnp.int32)[:, None]
    h8 = jnp.arange(512, dtype=jnp.int32)[None, :] // 64
    return fwd_w, inv_w, fwd_h, inv_h, eight, cos_of(q0 * h8), sin_of(q0 * h8)


def first_layer(w0, w1):
    lane = jnp.arange(1024, dtype=jnp.int32)[None, :]
    ri, h8 = split(jnp.arange(16, dtype=jnp.int32)[:, None], 2, 8)
    t, ro, e, _ = split(lane, 4, 2, 2, 64)
    angle = 128 * (2 * t + e) * h8 + 256 * (ro - ri)
    weights = (jnp.tile(w0.astype(F32), (1, 16)), jnp.tile(w1.astype(F32), (1, 16)))
    return outer_table(pltpu.HBM, (cos_of(angle), sin_of(angle)), weights)


def second_layer(w0, w1):
    z = jnp.zeros_like(w0)
    b0 = jnp.block([[w0, z], [z, w0]])
    b1 = jnp.block([[w1, z], [z, w1]])
    return jnp.block([[b0, b1], [-b1, b0]])


def low_half(rows):
    return lax.broadcasted_iota(jnp.int32, (rows, 128), 1) < 64


def swap(v):
    return pltpu.roll(v, 64, 1)


def norm_kernel(x_ref, gain_ref, packed_ref):
    low = low_half(64)
    ones = jnp.ones((256, 128), BF16)
    x = x_ref[...].reshape(512, 256)
    mean = dot(x, ones) * (1.0 / 256.0)
    d0, d1 = x[:, :128].astype(F32) - mean, x[:, 128:].astype(F32) - mean
    square = d0 * d0 + d1 * d1
    coarse = square.astype(BF16)
    fine = (square - coarse.astype(F32)).astype(BF16)
    var = dot(jnp.concatenate([coarse, fine], axis=1), ones) * (1.0 / 256.0)
    scale = lax.rsqrt(var + 1e-05)
    halves = (d0 * scale * gain_ref[:, :128], d1 * scale * gain_ref[:, 128:])
    for t in range(4):
        lanes = slice(128 * t, 128 * t + 128)
        for m in range(2):
            a = halves[m][128 * t : 128 * t + 64]
            b = halves[m][128 * t + 64 : 128 * t + 128]
            packed_ref[2 * m, :, lanes] = jnp.where(low, a, swap(b)).astype(BF16)
            packed_ref[2 * m + 1, :, lanes] = jnp.where(low, swap(a), b).astype(BF16)


def norm_and_pack(patches, gain):
    return pl.pallas_call(
        norm_kernel,
        grid=(4,),
        in_specs=[
            pl.BlockSpec((8, 64, 256), lambda g: (g, 0, 0)),
            pl.BlockSpec((1, 256), lambda g: (0, 0)),
        ],
        out_specs=pl.BlockSpec((4, 64, 512), lambda g: (g, 0, 0)),
        out_shape=pltpu.HBM((16, 64, 512), BF16),
        compiler_params=pltpu.CompilerParams(vmem_limit_bytes=12 * MIB),
        name="norm_pack",
    )(patches, gain.reshape(1, 256))


def final_kernel(x_ref, home_ref, out_ref):
    low = low_half(64)
    first = 4 * pl.program_id(0)
    for t in range(4):
        lanes = slice(128 * t, 128 * t + 128)
        for m in range(2):
            u = home_ref[first + 2 * m, :, lanes].astype(F32)
            v = home_ref[first + 2 * m + 1, :, lanes].astype(F32)
            chans = slice(128 * m, 128 * m + 128)
            even, odd = jnp.where(low, u, swap(v)), jnp.where(low, swap(u), v)
            out_ref[2 * t, :, chans] = (x_ref[2 * t, :, chans].astype(F32) + even).astype(BF16)
            out_ref[2 * t + 1, :, chans] = (x_ref[2 * t + 1, :, chans].astype(F32) + odd).astype(BF16)


def unpack_and_add(patches, home):
    return pl.pallas_call(
        final_kernel,
        grid=(4,),
        in_specs=[
            pl.BlockSpec((8, 64, 256), lambda g: (g, 0, 0)),
            pl.BlockSpec(memory_space=pltpu.VMEM),
        ],
        out_specs=pl.BlockSpec((8, 64, 256), lambda g: (g, 0, 0)),
        out_shape=jax.ShapeDtypeStruct((32, 64, 256), BF16),
        compiler_params=pltpu.CompilerParams(vmem_limit_bytes=8 * MIB),
        name="unpack_add",
    )(patches, resident(home))


def dot(a, b):
    return jnp.dot(a, b, preferred_element_type=F32)


def resident(v):
    return pltpu.with_memory_space_constraint(v, pltpu.VMEM)


def remaining(v):
    return pltpu.with_memory_space_constraint(v, pltpu.HBM)


def stream_dot(table, operand, extra, held, out, sems):
    copies = []
    for m in range(4):
        rows = slice(256 * m, 256 * m + 256)
        v = dot(table[rows, :], operand[...])
        if extra is not None:
            extra[m].wait()
            v = v + extra[4][rows, :]
        held[rows, :] = v.astype(BF16)
        copies.append(pltpu.make_async_copy(held.at[rows, :], out.at[rows, :], sems.at[m]))
        copies[-1].start()
    for copy in copies:
        copy.wait()


def columns_kernel(table_ref, x_ref, out_any, held, sems):
    stream_dot(table_ref, x_ref, None, held, out_any, sems)


def columns_add_kernel(table_ref, x_ref, extra_any, out_any, held, sems, extra, extra_sems):
    fetches = []
    for m in range(4):
        rows = slice(256 * m, 256 * m + 256)
        fetches.append(
            pltpu.make_async_copy(extra_any.at[rows, :], extra.at[rows, :], extra_sems.at[m])
        )
        fetches[-1].start()
    stream_dot(table_ref, x_ref, (*fetches, extra), held, out_any, sems)


def columns(table, x, *extra):
    scratch = [pltpu.VMEM((1024, 512), BF16), pltpu.SemaphoreType.DMA((4,))]
    if extra:
        scratch += [pltpu.VMEM((1024, 512), F32), pltpu.SemaphoreType.DMA((4,))]
    return pl.pallas_call(
        columns_add_kernel if extra else columns_kernel,
        in_specs=[pl.BlockSpec(memory_space=pltpu.VMEM)] * 2
        + [pl.BlockSpec(memory_space=pltpu.HBM)] * len(extra),
        out_specs=pl.BlockSpec(memory_space=pltpu.HBM),
        out_shape=pltpu.HBM((1024, 512), BF16),
        scratch_shapes=scratch,
        cost_estimate=pl.CostEstimate(flops=2**30, bytes_accessed=2**21, transcendentals=0),
        compiler_params=pltpu.CompilerParams(vmem_limit_bytes=12 * MIB),
        name="along_columns",
    )(resident(table), resident(x), *[remaining(e) for e in extra])


def stencil_kernel(x_ref, above_ref, below_ref, taps_ref, out_ref):
    low = low_half(512)

    def tile(t):
        return x_ref[:, 128 * t : 128 * t + 128].astype(F32)

    def between(t):
        if t < 0:
            other = above_ref[...].astype(F32)
            return jnp.concatenate(
                [
                    jnp.where(low, other, swap(tile(0)[:512])),
                    jnp.where(low, swap(other), swap(tile(0)[512:])),
                ],
                axis=0,
            )
        if t == 3:
            other = below_ref[...].astype(F32)
            return jnp.concatenate(
                [
                    jnp.where(low, swap(tile(3)[:512]), swap(other)),
                    jnp.where(low, swap(tile(3)[512:]), other),
                ],
                axis=0,
            )
        return jnp.where(low_half(1024), swap(tile(t)), swap(tile(t + 1)))

    for t in range(4):
        rows = (between(t - 1), tile(t), between(t))
        total = None
        for j in range(3):
            part = rows[0] * taps_ref[j : j + 1, :]
            part = part + rows[1] * taps_ref[3 + j : 4 + j, :]
            part = part + rows[2] * taps_ref[6 + j : 7 + j, :]
            if j != 1:
                part = pltpu.roll(part, 1 if j == 0 else 1023, 0)
            total = part if total is None else total + part
        out_ref[:, 128 * t : 128 * t + 128] = total


def stencil(x, above, below, taps):
    return pl.pallas_call(
        stencil_kernel,
        in_specs=[pl.BlockSpec(memory_space=pltpu.VMEM)] * 4,
        grid=(1,),
        out_specs=pl.BlockSpec((1024, 512), lambda g: (0, 0)),
        out_shape=pltpu.HBM((1024, 512), F32),
        cost_estimate=pl.CostEstimate(flops=2**24, bytes_accessed=2**22, transcendentals=0),
        compiler_params=pltpu.CompilerParams(vmem_limit_bytes=16 * MIB),
        name="stencil",
    )(resident(x), above, below, taps)


def middle_kernel(
    z, fwd, second_ref, cos_any, sin_any, first_any, eight_any, inv_any, out_any,
    cos_ref, sin_ref, first, eight, inv, held, done, sems, fetch_sems,
):
    fetches = []
    for n, (src, dst) in enumerate(
        (
            (cos_any, cos_ref),
            (sin_any, sin_ref),
            (first_any, first),
            (eight_any, eight),
            (inv_any, inv),
        )
    ):
        fetches.append(pltpu.make_async_copy(src, dst, fetch_sems.at[n]))
        fetches[-1].start()
    rows = 512 // CHUNKS
    groups = 8 // CHUNKS
    for m in range(CHUNKS):
        u = dot(fwd[2 * rows * m : 2 * rows * (m + 1), :], z[...])
        shape = (groups, 4, 16, 512)
        ur, ui = u[:rows].reshape(shape), u[rows:].reshape(shape)
        if m == 0:
            fetches[0].wait()
            fetches[1].wait()
        c = cos_ref[16 * groups * m : 16 * groups * (m + 1), :].reshape(groups, 1, 16, 512)
        s = sin_ref[16 * groups * m : 16 * groups * (m + 1), :].reshape(groups, 1, 16, 512)
        vr = (ur * c + ui * s).astype(BF16).reshape(rows, 512)
        vi = (ui * c - ur * s).astype(BF16).reshape(rows, 512)
        if m == 0:
            fetches[2].wait()
        hidden = jnp.tanh(dot(vr, first[:512, :]) + dot(vi, first[512:, :])).astype(BF16)
        parts = []
        for t in range(4):
            v = dot(hidden[:, 256 * t : 256 * t + 256], second_ref[...])
            v = jnp.where(v > 0.25, v - 0.25, jnp.where(v < -0.25, v + 0.25, 0.0 * v))
            parts.append(v.astype(BF16))
        if m == 0:
            fetches[3].wait()
        y = dot(jnp.concatenate(parts, axis=1), eight[...])
        yr, yi = y[:, :512].reshape(shape), y[:, 512:].reshape(shape)
        held[2 * rows * m : 2 * rows * m + rows, :] = (yr * c - yi * s).astype(BF16).reshape(rows, 512)
        held[2 * rows * m + rows : 2 * rows * (m + 1), :] = (
            (yi * c + yr * s).astype(BF16).reshape(rows, 512)
        )
    fetches[4].wait()
    stream_dot(inv, held, None, done, out_any, sems)


def middle(z, fwd, first, eight, inv, second, cos, sin):
    vmem, hbm = pl.BlockSpec(memory_space=pltpu.VMEM), pl.BlockSpec(memory_space=pltpu.HBM)
    return pl.pallas_call(
        middle_kernel,
        in_specs=[vmem] * 3 + [hbm] * 5,
        out_specs=hbm,
        out_shape=pltpu.HBM((1024, 512), BF16),
        scratch_shapes=[
            pltpu.VMEM((128, 512), F32),
            pltpu.VMEM((128, 512), F32),
            pltpu.VMEM((1024, 1024), BF16),
            pltpu.VMEM((1024, 1024), BF16),
            pltpu.VMEM((1024, 1024), BF16),
            pltpu.VMEM((1024, 512), BF16),
            pltpu.VMEM((1024, 512), BF16),
            pltpu.SemaphoreType.DMA((4,)),
            pltpu.SemaphoreType.DMA((5,)),
        ],
        cost_estimate=pl.CostEstimate(flops=5 * 2**30, bytes_accessed=2**21, transcendentals=2**19),
        compiler_params=pltpu.CompilerParams(vmem_limit_bytes=28 * MIB),
        name="filter_rows",
    )(
        resident(z), resident(fwd), second, remaining(cos), remaining(sin), remaining(first),
        remaining(eight), remaining(inv),
    )


def packed_row(lines, lane):
    return jnp.concatenate([lines[:512, lane : lane + 64], lines[512:, lane : lane + 64]], axis=1)


def local(patches, norm_gain, w_first, w_second, depth_kernel):
    packed = norm_and_pack(patches, norm_gain)
    lines = lax.all_to_all(packed, ("yl", "x"), 0, 0, tiled=True).reshape(1024, 512)

    fwd_w, inv_w, fwd_h, inv_h, eight, cos, sin = make_tables()
    block = lax.axis_index("x")
    wf = lax.dynamic_index_in_dim(w_first, block, 1, keepdims=False)
    ws = lax.dynamic_index_in_dim(w_second, block, 1, keepdims=False)
    taps = lax.dynamic_slice_in_dim(depth_kernel.reshape(9, 256), 64 * block, 64, 1)
    taps = jnp.concatenate([taps, taps], axis=1)
    first = first_layer(wf[0], wf[1])
    second = second_layer(ws[0], ws[1])

    freqs = columns(fwd_w, lines).reshape(128, 8, 512)
    whole = lax.all_to_all(freqs, ("row", "yl"), 0, 0, tiled=True).reshape(1024, 512)
    groups = 128
    down = [(i, (i + 1) % groups) for i in range(groups)]
    up = [(j, i) for i, j in down]
    above = lax.ppermute(packed_row(lines, 448), ("row", "yl"), down)
    below = lax.ppermute(packed_row(lines, 0), ("row", "yl"), up)
    conv = stencil(lines, above, below, taps)

    filtered = middle(whole, fwd_h, first, eight, inv_h, second, cos, sin)
    back = lax.all_to_all(filtered.reshape(128, 8, 512), ("row", "yl"), 0, 0, tiled=True)
    summed = columns(inv_w, back.reshape(1024, 512), conv).reshape(16, 64, 512)
    home = lax.all_to_all(summed, ("yl", "x"), 0, 0, tiled=True)
    return unpack_and_add(patches, home)


def solution(mesh):
    fine = Mesh(np.asarray(mesh.devices).reshape(32, 4, 4), ("row", "yl", "x"))
    return jax.shard_map(
        local,
        mesh=fine,
        in_specs=(P("row", ("yl", "x"), None), P(), P(), P(), P()),
        out_specs=P("row", ("yl", "x"), None),
        check_vma=False,
    )
```

```python
import functools
import math

import jax
import jax.numpy as jnp
import numpy as np
from jax import lax
from jax.experimental import pallas as pl
from jax.experimental.pallas import tpu as pltpu
from jax.sharding import Mesh
from jax.sharding import PartitionSpec as P

TURN = 1024
CHUNKS = 2
MIB = 1024 * 1024
F32 = jnp.float32
BF16 = jnp.bfloat16


def cos_of(idx):
    return jnp.cos((idx % TURN).astype(F32) * (2.0 * math.pi / TURN))


def sin_of(idx):
    return jnp.sin((idx % TURN).astype(F32) * (2.0 * math.pi / TURN))


def expand_kernel(steps, *refs):
    out_ref, half = refs[-1], (len(refs) - 1) // 2
    first = 0 if steps == 16 else steps * pl.program_id(0)

    def step(a, carry):
        v = None
        for e_ref, f_ref in zip(refs[:half], refs[half:-1]):
            term = e_ref[pl.ds(first + a, 1), :] * f_ref[...]
            v = term if v is None else v + term
        out_ref[pl.ds(pl.multiple_of(64 * a, 64), 64), :] = v.astype(BF16)
        return carry

    lax.fori_loop(0, steps, step, 0)


def outer_table(space, es, fs):
    whole = pl.BlockSpec(memory_space=pltpu.VMEM)
    stay = space == pltpu.VMEM
    return pl.pallas_call(
        functools.partial(expand_kernel, 16 if stay else 4),
        grid=(1,) if stay else (4,),
        in_specs=[whole] * (len(es) + len(fs)),
        out_specs=whole if stay else pl.BlockSpec((256, 1024), lambda g: (g, 0)),
        out_shape=space((1024, 1024), BF16),
        cost_estimate=pl.CostEstimate(flops=3 * 2**20, bytes_accessed=2**21, transcendentals=0),
        compiler_params=pltpu.CompilerParams(vmem_limit_bytes=4 * MIB),
        name="expand_table",
    )(*es, *fs)


def phase_table(space, ia, ib, scale):
    return outer_table(space, (cos_of(ia), sin_of(ia)), (cos_of(ib) * scale, -sin_of(ib) * scale))


def column(values):
    return jnp.asarray(values, jnp.int32)[:, None]


def split(idx, *sizes):
    out = []
    for s in reversed(sizes):
        out.append(idx % s)
        idx = idx // s
    return out[::-1]


def make_tables():
    lane = jnp.arange(1024, dtype=jnp.int32)[None, :]
    scale = 1.0 / 32.0
    a16 = jnp.arange(16, dtype=jnp.int32)[:, None]
    b64 = jnp.arange(64, dtype=jnp.int32)[:, None]
    pl_, ri, i = split(b64, 8, 2, 4)
    fwd_w = phase_table(pltpu.VMEM, 32 * a16 * lane, (4 * pl_ + i) * lane + 256 * ri, scale)
    p, lri, li = split(lane, 128, 2, 4)
    k = 4 * p + li
    weight = jnp.where(k == 0, 1.0, 2.0).astype(F32) * scale
    inv_w = phase_table(pltpu.VMEM, 64 * a16 * k, b64 * k + 256 * lri, weight)
    qhh, ro, qhl = split(a16, CHUNKS, 2, 8 // CHUNKS)
    qh = qhh * (8 // CHUNKS) + qhl
    bi, ql = split(b64, 4, 16)
    mask = jnp.where(bi == li, scale, 0.0).astype(F32)
    fwd_h = phase_table(pltpu.VMEM, 128 * qh * p + 256 * (ro - lri), 8 * ql * p, mask)
    lqhh, lro, lqhl, lli, lql = split(lane, CHUNKS, 2, 8 // CHUNKS, 4, 16)
    lq0 = 16 * (lqhh * (8 // CHUNKS) + lqhl) + lql
    mask_t = jnp.where(i == lli, scale, 0.0).astype(F32)
    inv_h = phase_table(pltpu.HBM, 64 * a16 * lq0, 8 * pl_ * lq0 + 256 * (lro - ri), mask_t)
    t, gri, e = split(a16, 4, 2, 2)
    gro, gh8, gc = split(lane, 2, 8, 64)
    e1 = cos_of(128 * (2 * t + e) * gh8 - 256 * (gro - gri))
    eye = jnp.where(b64 == gc, 1.0, 0.0).astype(F32)
    eight = outer_table(pltpu.HBM, (e1,), (eye,))
    q0 = jnp.arange(128, dtype=jnp.int32)[:, None]
    h8 = jnp.arange(512, dtype=jnp.int32)[None, :] // 64
    return fwd_w, inv_w, fwd_h, inv_h, eight, cos_of(q0 * h8), sin_of(q0 * h8)


def first_layer(w0, w1):
    lane = jnp.arange(1024, dtype=jnp.int32)[None, :]
    ri, h8 = split(jnp.arange(16, dtype=jnp.int32)[:, None], 2, 8)
    t, ro, e, _ = split(lane, 4, 2, 2, 64)
    angle = 128 * (2 * t + e) * h8 + 256 * (ro - ri)
    weights = (jnp.tile(w0.astype(F32), (1, 16)), jnp.tile(w1.astype(F32), (1, 16)))
    return outer_table(pltpu.HBM, (cos_of(angle), sin_of(angle)), weights)


def second_layer(w0, w1):
    z = jnp.zeros_like(w0)
    b0 = jnp.block([[w0, z], [z, w0]])
    b1 = jnp.block([[w1, z], [z, w1]])
    return jnp.block([[b0, b1], [-b1, b0]])


def low_half(rows):
    return lax.broadcasted_iota(jnp.int32, (rows, 128), 1) < 64


def swap(v):
    return pltpu.roll(v, 64, 1)


def norm_kernel(x_ref, gain_ref, packed_ref):
    low = low_half(64)
    ones = jnp.ones((256, 128), BF16)
    x = x_ref[...].reshape(512, 256)
    mean = dot(x, ones) * (1.0 / 256.0)
    d0, d1 = x[:, :128].astype(F32) - mean, x[:, 128:].astype(F32) - mean
    square = d0 * d0 + d1 * d1
    coarse = square.astype(BF16)
    fine = (square - coarse.astype(F32)).astype(BF16)
    var = dot(jnp.concatenate([coarse, fine], axis=1), ones) * (1.0 / 256.0)
    scale = lax.rsqrt(var + 1e-05)
    halves = (d0 * scale * gain_ref[:, :128], d1 * scale * gain_ref[:, 128:])
    for t in range(4):
        lanes = slice(128 * t, 128 * t + 128)
        for m in range(2):
            a = halves[m][128 * t : 128 * t + 64]
            b = halves[m][128 * t + 64 : 128 * t + 128]
            packed_ref[2 * m, :, lanes] = jnp.where(low, a, swap(b)).astype(BF16)
            packed_ref[2 * m + 1, :, lanes] = jnp.where(low, swap(a), b).astype(BF16)


def norm_and_pack(patches, gain):
    return pl.pallas_call(
        norm_kernel,
        grid=(4,),
        in_specs=[
            pl.BlockSpec((8, 64, 256), lambda g: (g, 0, 0)),
            pl.BlockSpec((1, 256), lambda g: (0, 0)),
        ],
        out_specs=pl.BlockSpec((4, 64, 512), lambda g: (g, 0, 0)),
        out_shape=pltpu.HBM((16, 64, 512), BF16),
        compiler_params=pltpu.CompilerParams(vmem_limit_bytes=12 * MIB),
        name="norm_pack",
    )(remaining(patches), gain.reshape(1, 256))


def final_kernel(x_ref, home_ref, out_ref):
    low = low_half(64)
    first = 4 * pl.program_id(0)
    for t in range(4):
        lanes = slice(128 * t, 128 * t + 128)
        for m in range(2):
            u = home_ref[first + 2 * m, :, lanes].astype(F32)
            v = home_ref[first + 2 * m + 1, :, lanes].astype(F32)
            chans = slice(128 * m, 128 * m + 128)
            even, odd = jnp.where(low, u, swap(v)), jnp.where(low, swap(u), v)
            out_ref[2 * t, :, chans] = (x_ref[2 * t, :, chans].astype(F32) + even).astype(BF16)
            out_ref[2 * t + 1, :, chans] = (x_ref[2 * t + 1, :, chans].astype(F32) + odd).astype(BF16)


def unpack_and_add(patches, home):
    return pl.pallas_call(
        final_kernel,
        grid=(4,),
        in_specs=[
            pl.BlockSpec((8, 64, 256), lambda g: (g, 0, 0)),
            pl.BlockSpec(memory_space=pltpu.VMEM),
        ],
        out_specs=pl.BlockSpec((8, 64, 256), lambda g: (g, 0, 0)),
        out_shape=jax.ShapeDtypeStruct((32, 64, 256), BF16),
        compiler_params=pltpu.CompilerParams(vmem_limit_bytes=8 * MIB),
        name="unpack_add",
    )(patches, resident(home))


def dot(a, b):
    return jnp.dot(a, b, preferred_element_type=F32)


def resident(v):
    return pltpu.with_memory_space_constraint(v, pltpu.VMEM)


def remaining(v):
    return pltpu.with_memory_space_constraint(v, pltpu.HBM)


def stream_dot(table, operand, extra, held, out, sems):
    copies = []
    for m in range(4):
        rows = slice(256 * m, 256 * m + 256)
        v = dot(table[rows, :], operand[...])
        if extra is not None:
            extra[m].wait()
            v = v + extra[4][rows, :]
        held[rows, :] = v.astype(BF16)
        copies.append(pltpu.make_async_copy(held.at[rows, :], out.at[rows, :], sems.at[m]))
        copies[-1].start()
    for copy in copies:
        copy.wait()


def columns_kernel(
    table_ref, x_ref, out_any, lines_any, last_ref, leading_ref, held, sems, line_sem
):
    keep = pltpu.make_async_copy(x_ref, lines_any, line_sem)
    keep.start()
    stream_dot(table_ref, x_ref, None, held, out_any, sems)
    low = low_half(512)
    top, bottom = x_ref[:512, 384:].astype(F32), x_ref[512:, 384:].astype(F32)
    last_ref[...] = jnp.where(low, swap(top), bottom).astype(BF16)
    top, bottom = x_ref[:512, :128].astype(F32), x_ref[512:, :128].astype(F32)
    leading_ref[...] = jnp.where(low, top, swap(bottom)).astype(BF16)
    keep.wait()


def forward_columns(table, x):
    vmem, hbm = pl.BlockSpec(memory_space=pltpu.VMEM), pl.BlockSpec(memory_space=pltpu.HBM)
    return pl.pallas_call(
        columns_kernel,
        in_specs=[vmem] * 2,
        out_specs=[hbm, hbm, vmem, vmem],
        out_shape=[
            pltpu.HBM((1024, 512), BF16),
            pltpu.HBM((1024, 512), BF16),
            jax.ShapeDtypeStruct((512, 128), BF16),
            jax.ShapeDtypeStruct((512, 128), BF16),
        ],
        scratch_shapes=[
            pltpu.VMEM((1024, 512), BF16),
            pltpu.SemaphoreType.DMA((4,)),
            pltpu.SemaphoreType.DMA,
        ],
        cost_estimate=pl.CostEstimate(flops=2**30, bytes_accessed=2**21, transcendentals=0),
        compiler_params=pltpu.CompilerParams(vmem_limit_bytes=12 * MIB),
        name="forward_columns",
    )(resident(table), resident(x))


def columns_add_kernel(table_ref, x_ref, extra_any, out_any, held, sems, extra, extra_sems):
    fetches = []
    for m in range(4):
        rows = slice(256 * m, 256 * m + 256)
        fetches.append(
            pltpu.make_async_copy(extra_any.at[rows, :], extra.at[rows, :], extra_sems.at[m])
        )
        fetches[-1].start()
    stream_dot(table_ref, x_ref, (*fetches, extra), held, out_any, sems)


def backward_columns(table, x, extra):
    vmem, hbm = pl.BlockSpec(memory_space=pltpu.VMEM), pl.BlockSpec(memory_space=pltpu.HBM)
    return pl.pallas_call(
        columns_add_kernel,
        in_specs=[vmem, vmem, hbm],
        out_specs=hbm,
        out_shape=pltpu.HBM((1024, 512), BF16),
        scratch_shapes=[
            pltpu.VMEM((1024, 512), BF16),
            pltpu.SemaphoreType.DMA((4,)),
            pltpu.VMEM((1024, 512), F32),
            pltpu.SemaphoreType.DMA((4,)),
        ],
        cost_estimate=pl.CostEstimate(flops=2**30, bytes_accessed=2**21, transcendentals=0),
        compiler_params=pltpu.CompilerParams(vmem_limit_bytes=12 * MIB),
        name="backward_columns",
    )(resident(table), resident(x), remaining(extra))


def stencil_kernel(x_ref, above_ref, below_ref, taps_ref, out_ref):
    low = low_half(512)

    def tile(t):
        return x_ref[:, 128 * t : 128 * t + 128].astype(F32)

    def between(t):
        if t < 0:
            other = above_ref[...].astype(F32)
            return jnp.concatenate(
                [
                    jnp.where(low, other, swap(tile(0)[:512])),
                    jnp.where(low, swap(other), swap(tile(0)[512:])),
                ],
                axis=0,
            )
        if t == 3:
            other = below_ref[...].astype(F32)
            return jnp.concatenate(
                [
                    jnp.where(low, swap(tile(3)[:512]), swap(other)),
                    jnp.where(low, swap(tile(3)[512:]), other),
                ],
                axis=0,
            )
        return jnp.where(low_half(1024), swap(tile(t)), swap(tile(t + 1)))

    for t in range(4):
        rows = (between(t - 1), tile(t), between(t))
        total = None
        for j in range(3):
            part = rows[0] * taps_ref[j : j + 1, :]
            part = part + rows[1] * taps_ref[3 + j : 4 + j, :]
            part = part + rows[2] * taps_ref[6 + j : 7 + j, :]
            if j != 1:
                part = pltpu.roll(part, 1 if j == 0 else 1023, 0)
            total = part if total is None else total + part
        out_ref[:, 128 * t : 128 * t + 128] = total


def stencil(x, above, below, taps):
    return pl.pallas_call(
        stencil_kernel,
        in_specs=[pl.BlockSpec(memory_space=pltpu.VMEM)] * 4,
        grid=(1,),
        out_specs=pl.BlockSpec((1024, 512), lambda g: (0, 0)),
        out_shape=pltpu.HBM((1024, 512), F32),
        cost_estimate=pl.CostEstimate(flops=2**24, bytes_accessed=2**22, transcendentals=0),
        compiler_params=pltpu.CompilerParams(vmem_limit_bytes=16 * MIB),
        name="stencil",
    )(x, above, below, taps)


def middle_kernel(
    z, fwd, second_ref, cos_any, sin_any, first_any, eight_any, inv_any, out_any,
    cos_ref, sin_ref, first, eight, inv, held, done, sems, fetch_sems,
):
    fetches = []
    for n, (src, dst) in enumerate(
        (
            (cos_any, cos_ref),
            (sin_any, sin_ref),
            (first_any, first),
            (eight_any, eight),
            (inv_any, inv),
        )
    ):
        fetches.append(pltpu.make_async_copy(src, dst, fetch_sems.at[n]))
        fetches[-1].start()
    rows = 512 // CHUNKS
    groups = 8 // CHUNKS
    for m in range(CHUNKS):
        u = dot(fwd[2 * rows * m : 2 * rows * (m + 1), :], z[...])
        shape = (groups, 4, 16, 512)
        ur, ui = u[:rows].reshape(shape), u[rows:].reshape(shape)
        if m == 0:
            fetches[0].wait()
            fetches[1].wait()
        c = cos_ref[16 * groups * m : 16 * groups * (m + 1), :].reshape(groups, 1, 16, 512)
        s = sin_ref[16 * groups * m : 16 * groups * (m + 1), :].reshape(groups, 1, 16, 512)
        vr = (ur * c + ui * s).astype(BF16).reshape(rows, 512)
        vi = (ui * c - ur * s).astype(BF16).reshape(rows, 512)
        if m == 0:
            fetches[2].wait()
        hidden = jnp.tanh(dot(vr, first[:512, :]) + dot(vi, first[512:, :])).astype(BF16)
        parts = []
        for t in range(4):
            v = dot(hidden[:, 256 * t : 256 * t + 256], second_ref[...])
            v = jnp.where(v > 0.25, v - 0.25, jnp.where(v < -0.25, v + 0.25, 0.0 * v))
            parts.append(v.astype(BF16))
        if m == 0:
            fetches[3].wait()
        y = dot(jnp.concatenate(parts, axis=1), eight[...])
        yr, yi = y[:, :512].reshape(shape), y[:, 512:].reshape(shape)
        held[2 * rows * m : 2 * rows * m + rows, :] = (yr * c - yi * s).astype(BF16).reshape(rows, 512)
        held[2 * rows * m + rows : 2 * rows * (m + 1), :] = (
            (yi * c + yr * s).astype(BF16).reshape(rows, 512)
        )
    fetches[4].wait()
    stream_dot(inv, held, None, done, out_any, sems)


def middle(z, fwd, first, eight, inv, second, cos, sin):
    vmem, hbm = pl.BlockSpec(memory_space=pltpu.VMEM), pl.BlockSpec(memory_space=pltpu.HBM)
    return pl.pallas_call(
        middle_kernel,
        in_specs=[vmem] * 3 + [hbm] * 5,
        out_specs=hbm,
        out_shape=pltpu.HBM((1024, 512), BF16),
        scratch_shapes=[
            pltpu.VMEM((128, 512), F32),
            pltpu.VMEM((128, 512), F32),
            pltpu.VMEM((1024, 1024), BF16),
            pltpu.VMEM((1024, 1024), BF16),
            pltpu.VMEM((1024, 1024), BF16),
            pltpu.VMEM((1024, 512), BF16),
            pltpu.VMEM((1024, 512), BF16),
            pltpu.SemaphoreType.DMA((4,)),
            pltpu.SemaphoreType.DMA((5,)),
        ],
        cost_estimate=pl.CostEstimate(flops=5 * 2**30, bytes_accessed=2**21, transcendentals=2**19),
        compiler_params=pltpu.CompilerParams(vmem_limit_bytes=28 * MIB),
        name="filter_rows",
    )(
        resident(z), resident(fwd), second, remaining(cos), remaining(sin), remaining(first),
        remaining(eight), remaining(inv),
    )


def local(patches, norm_gain, w_first, w_second, depth_kernel):
    packed = norm_and_pack(patches, norm_gain)
    lines = lax.all_to_all(packed, ("yl", "x"), 0, 0, tiled=True).reshape(1024, 512)

    fwd_w, inv_w, fwd_h, inv_h, eight, cos, sin = make_tables()
    block = lax.axis_index("x")
    wf = lax.dynamic_index_in_dim(w_first, block, 1, keepdims=False)
    ws = lax.dynamic_index_in_dim(w_second, block, 1, keepdims=False)
    taps = lax.dynamic_slice_in_dim(depth_kernel.reshape(9, 256), 64 * block, 64, 1)
    taps = jnp.concatenate([taps, taps], axis=1)
    first = first_layer(wf[0], wf[1])
    second = second_layer(ws[0], ws[1])

    freqs, kept, last, leading = forward_columns(fwd_w, lines)
    whole = lax.all_to_all(freqs.reshape(128, 8, 512), ("row", "yl"), 0, 0, tiled=True)
    groups = 128
    down = [(i, (i + 1) % groups) for i in range(groups)]
    up = [(j, i) for i, j in down]
    above = lax.ppermute(last, ("row", "yl"), down)
    below = lax.ppermute(leading, ("row", "yl"), up)
    whole, above, below = lax.optimization_barrier((whole, above, below))

    filtered = middle(whole.reshape(1024, 512), fwd_h, first, eight, inv_h, second, cos, sin)
    filtered, above, below = lax.optimization_barrier((filtered, above, below))
    back = lax.all_to_all(filtered.reshape(128, 8, 512), ("row", "yl"), 0, 0, tiled=True)
    conv = stencil(kept, above, below, taps)
    summed = backward_columns(inv_w, back.reshape(1024, 512), conv).reshape(16, 64, 512)
    home = lax.all_to_all(summed, ("yl", "x"), 0, 0, tiled=True)
    return unpack_and_add(patches, home)


def solution(mesh):
    fine = Mesh(np.asarray(mesh.devices).reshape(32, 4, 4), ("row", "yl", "x"))
    return jax.shard_map(
        local,
        mesh=fine,
        in_specs=(P("row", ("yl", "x"), None), P(), P(), P(), P()),
        out_specs=P("row", ("yl", "x"), None),
        check_vma=False,
    )
```

```python
import functools
import math

import jax
import jax.numpy as jnp
import numpy as np
from jax import lax
from jax.experimental import pallas as pl
from jax.experimental.pallas import tpu as pltpu
from jax.sharding import Mesh
from jax.sharding import PartitionSpec as P

TURN = 1024
CHUNKS = 2
MIB = 1024 * 1024
F32 = jnp.float32
BF16 = jnp.bfloat16


def iota(shape, dim):
    return lax.broadcasted_iota(jnp.int32, shape, dim)


def digit(idx, shift, bits):
    return (idx >> shift) & ((1 << bits) - 1)


def cos_sin(idx):
    idx = idx & (TURN - 1)
    quarter = (idx + TURN // 8) >> 8
    x = (idx - (quarter << 8)).astype(F32) * (2.0 * math.pi / TURN)
    y = x * x
    s = x * (1.0 + y * (-1.0 / 6 + y * (1.0 / 120 + y * (-1.0 / 5040 + y * (1.0 / 362880)))))
    c = 1.0 + y * (-1.0 / 2 + y * (1.0 / 24 + y * (-1.0 / 720 + y * (1.0 / 40320))))
    odd = (quarter & 1) == 1
    cos, sin = jnp.where(odd, s, c), jnp.where(odd, c, s)
    turned = (quarter + 1) & 3
    cos = jnp.where(turned >= 2, -cos, cos)
    sin = jnp.where((quarter & 3) >= 2, -sin, sin)
    return cos, sin


SCALE = 1.0 / 32.0


def forward_columns_phases():
    a, b = iota((16, 1024), 0), iota((64, 1024), 0)
    w = iota((64, 1024), 1)
    k = 4 * digit(b, 3, 3) + digit(b, 0, 2)
    return 32 * a * w[:16], k * w + 256 * digit(b, 2, 1), SCALE


def backward_columns_phases():
    a, b, lane = iota((16, 1024), 0), iota((64, 1024), 0), iota((64, 1024), 1)
    k = 4 * (lane >> 3) + digit(lane, 0, 2)
    weight = jnp.where(k == 0, SCALE, 2.0 * SCALE)
    return 64 * a * k[:16], b * k + 256 * digit(lane, 2, 1), weight


def forward_rows_phases():
    a, b, lane = iota((16, 1024), 0), iota((64, 1024), 0), iota((64, 1024), 1)
    qh = 4 * digit(a, 3, 1) + digit(a, 0, 2)
    p, ri = lane >> 3, digit(lane, 2, 1)
    ia = 128 * qh * p[:16] + 256 * (digit(a, 2, 1) - ri[:16])
    weight = jnp.where(digit(b, 4, 2) == digit(lane, 0, 2), SCALE, 0.0)
    return ia, 8 * digit(b, 0, 4) * p, weight


def backward_rows_phases():
    a, b, lane = iota((16, 1024), 0), iota((64, 1024), 0), iota((64, 1024), 1)
    q0 = 16 * (4 * digit(lane, 9, 1) + digit(lane, 6, 2)) + digit(lane, 0, 4)
    ro = digit(lane, 8, 1)
    weight = jnp.where(digit(b, 0, 2) == digit(lane, 4, 2), SCALE, 0.0)
    return 64 * a * q0[:16], 8 * digit(b, 3, 3) * q0 + 256 * (ro - digit(b, 2, 1)), weight


def table_kernel(phases, with_twiddles, stay, waited, *refs):
    refs = refs[waited:]
    out_ref, (ec, es, fc, fs) = refs[0], refs[-4:]
    steps = 16 if stay else 4

    @pl.when(pl.program_id(0) == 0)
    def _():
        ia, ib, weight = phases()
        ec[...], es[...] = cos_sin(ia)
        c, s = cos_sin(ib)
        fc[...], fs[...] = c * weight, s * weight
        if with_twiddles:
            angle = iota((128, 512), 0) * (iota((128, 512), 1) >> 6)
            refs[1][...], refs[2][...] = cos_sin(angle)

    first = 0 if stay else steps * pl.program_id(0)

    def step(a, carry):
        row = pl.ds(first + a, 1)
        out_ref[pl.ds(pl.multiple_of(64 * a, 64), 64), :] = (
            ec[row, :] * fc[...] - es[row, :] * fs[...]
        ).astype(BF16)
        return carry

    lax.fori_loop(0, steps, step, 0)


def table(space, phases, with_twiddles=False, after=()):
    stay = space == pltpu.VMEM
    whole = pl.BlockSpec(memory_space=pltpu.VMEM)
    twiddle_spec = pl.BlockSpec((128, 512), lambda g: (0, 0))
    out = pl.pallas_call(
        functools.partial(table_kernel, phases, with_twiddles, stay, len(after)),
        grid=(1,) if stay else (4,),
        in_specs=[pl.BlockSpec(memory_space=pltpu.HBM)] * len(after),
        out_specs=[whole if stay else pl.BlockSpec((256, 1024), lambda g: (g, 0))]
        + [twiddle_spec] * (2 * with_twiddles),
        out_shape=[space((1024, 1024), BF16)] + [pltpu.HBM((128, 512), F32)] * (2 * with_twiddles),
        scratch_shapes=[pltpu.VMEM((n, 1024), F32) for n in (16, 16, 64, 64)],
        cost_estimate=pl.CostEstimate(flops=2**23, bytes_accessed=2**21, transcendentals=0),
        compiler_params=pltpu.CompilerParams(vmem_limit_bytes=6 * MIB),
        name=phases.__name__,
    )(*[remaining(v) for v in after])
    return out if with_twiddles else out[0]


def blocks_kernel(first_w, second_w, first_ref, eight_ref, second_ref, acc, ass, bcc):
    block = lax.axis_index("x")
    low = low_half(64)

    def twice(ref, n):
        w = ref[n, block].astype(F32)
        return jnp.concatenate([w, w], axis=1)

    @pl.when(pl.program_id(0) == 0)
    def _():
        a, lane = iota((16, 1024), 0), iota((16, 1024), 1)
        q1 = 2 * digit(lane, 8, 2) + digit(lane, 6, 1)
        acc[...], ass[...] = cos_sin(
            128 * q1 * digit(a, 0, 3) + 256 * (digit(lane, 7, 1) - digit(a, 3, 1))
        )
        q1 = 2 * digit(a, 2, 2) + digit(a, 0, 1)
        bcc[...], _unused = cos_sin(
            128 * q1 * digit(lane, 6, 3) - 256 * (digit(lane, 9, 1) - digit(a, 1, 1))
        )
        w0, w1 = twice(second_w, 0), twice(second_w, 1)
        zero = jnp.zeros_like(w0)
        for half in range(2):
            def own(v):
                return (jnp.where(low, v, zero) if half == 0 else jnp.where(low, zero, v)).astype(BF16)

            re, im = slice(64 * half, 64 * half + 64), slice(128 + 64 * half, 192 + 64 * half)
            second_ref[re, :128], second_ref[re, 128:] = own(w0), own(w1)
            second_ref[im, :128], second_ref[im, 128:] = own(-w1), own(w0)

    w0, w1 = twice(first_w, 0), twice(first_w, 1)
    eye = jnp.where(iota((64, 128), 0) == (iota((64, 128), 1) & 63), 1.0, 0.0)
    first = 4 * pl.program_id(0)

    def step(a, carry):
        rows = pl.ds(pl.multiple_of(64 * a, 64), 64)
        row = pl.ds(first + a, 1)
        c, s, back = acc[row, :], ass[row, :], bcc[row, :]
        for t in range(8):
            lanes = slice(128 * t, 128 * t + 128)
            first_ref[rows, lanes] = (c[:, lanes] * w0 + s[:, lanes] * w1).astype(BF16)
            eight_ref[rows, lanes] = (back[:, lanes] * eye).astype(BF16)
        return carry

    lax.fori_loop(0, 4, step, 0)


def block_tables(w_first, w_second):
    vmem = pl.BlockSpec(memory_space=pltpu.VMEM)
    quarter = pl.BlockSpec((256, 1024), lambda g: (g, 0))
    return pl.pallas_call(
        blocks_kernel,
        grid=(4,),
        in_specs=[vmem, vmem],
        out_specs=[quarter, quarter, pl.BlockSpec((256, 256), lambda g: (0, 0))],
        out_shape=[
            pltpu.HBM((1024, 1024), BF16),
            pltpu.HBM((1024, 1024), BF16),
            pltpu.HBM((256, 256), BF16),
        ],
        scratch_shapes=[pltpu.VMEM((16, 1024), F32)] * 3,
        cost_estimate=pl.CostEstimate(flops=2**23, bytes_accessed=2**22, transcendentals=0),
        compiler_params=pltpu.CompilerParams(vmem_limit_bytes=8 * MIB),
        name="block_tables",
    )(w_first, w_second)


def low_half(rows):
    return lax.broadcasted_iota(jnp.int32, (rows, 128), 1) < 64


def swap(v):
    return pltpu.roll(v, 64, 1)


def norm_kernel(x_any, gain_ref, out_any, x_all, packed, in_sems, out_sems):
    low = low_half(64)
    ones = jnp.ones((256, 128), BF16)
    fetches, sends = [], []
    for g in range(4):
        rows = slice(8 * g, 8 * g + 8)
        fetches.append(pltpu.make_async_copy(x_any.at[rows], x_all.at[rows], in_sems.at[g]))
        fetches[-1].start()
    for g in range(4):
        fetches[g].wait()
        x = x_all[8 * g : 8 * g + 8].reshape(512, 256)
        mean = dot(x, ones) * (1.0 / 256.0)
        d0, d1 = x[:, :128].astype(F32) - mean, x[:, 128:].astype(F32) - mean
        square = d0 * d0 + d1 * d1
        coarse = square.astype(BF16)
        fine = (square - coarse.astype(F32)).astype(BF16)
        var = dot(jnp.concatenate([coarse, fine], axis=1), ones) * (1.0 / 256.0)
        scale = lax.rsqrt(var + 1e-05)
        halves = (d0 * scale * gain_ref[:, :128], d1 * scale * gain_ref[:, 128:])
        for t in range(4):
            lanes = slice(128 * t, 128 * t + 128)
            for m in range(2):
                a = halves[m][128 * t : 128 * t + 64]
                b = halves[m][128 * t + 64 : 128 * t + 128]
                packed[4 * g + 2 * m, :, lanes] = jnp.where(low, a, swap(b)).astype(BF16)
                packed[4 * g + 2 * m + 1, :, lanes] = jnp.where(low, swap(a), b).astype(BF16)
        parts = slice(4 * g, 4 * g + 4)
        sends.append(pltpu.make_async_copy(packed.at[parts], out_any.at[parts], out_sems.at[g]))
        sends[-1].start()
    for send in sends:
        send.wait()


def norm_and_pack(patches, gain):
    return pl.pallas_call(
        norm_kernel,
        in_specs=[pl.BlockSpec(memory_space=pltpu.HBM), pl.BlockSpec(memory_space=pltpu.VMEM)],
        out_specs=pl.BlockSpec(memory_space=pltpu.HBM),
        out_shape=pltpu.HBM((16, 64, 512), BF16),
        scratch_shapes=[
            pltpu.VMEM((32, 64, 256), BF16),
            pltpu.VMEM((16, 64, 512), BF16),
            pltpu.SemaphoreType.DMA((4,)),
            pltpu.SemaphoreType.DMA((4,)),
        ],
        compiler_params=pltpu.CompilerParams(vmem_limit_bytes=16 * MIB),
        name="norm_pack",
    )(remaining(patches), remaining(gain.reshape(1, 256)))


def final_kernel(x_ref, home_ref, out_ref):
    low = low_half(64)
    first = 4 * pl.program_id(0)
    for t in range(4):
        lanes = slice(128 * t, 128 * t + 128)
        for m in range(2):
            u = home_ref[first + 2 * m, :, lanes].astype(F32)
            v = home_ref[first + 2 * m + 1, :, lanes].astype(F32)
            chans = slice(128 * m, 128 * m + 128)
            even, odd = jnp.where(low, u, swap(v)), jnp.where(low, swap(u), v)
            out_ref[2 * t, :, chans] = (x_ref[2 * t, :, chans].astype(F32) + even).astype(BF16)
            out_ref[2 * t + 1, :, chans] = (x_ref[2 * t + 1, :, chans].astype(F32) + odd).astype(BF16)


def unpack_and_add(patches, home):
    return pl.pallas_call(
        final_kernel,
        grid=(4,),
        in_specs=[
            pl.BlockSpec((8, 64, 256), lambda g: (g, 0, 0)),
            pl.BlockSpec(memory_space=pltpu.VMEM),
        ],
        out_specs=pl.BlockSpec((8, 64, 256), lambda g: (g, 0, 0)),
        out_shape=jax.ShapeDtypeStruct((32, 64, 256), BF16),
        compiler_params=pltpu.CompilerParams(vmem_limit_bytes=8 * MIB),
        name="unpack_add",
    )(patches, resident(home))


def dot(a, b):
    return jnp.dot(a, b, preferred_element_type=F32)


def resident(v):
    return pltpu.with_memory_space_constraint(v, pltpu.VMEM)


def remaining(v):
    return pltpu.with_memory_space_constraint(v, pltpu.HBM)


def stream_dot(table, operand, extra, held, out, sems):
    copies = []
    for m in range(4):
        rows = slice(256 * m, 256 * m + 256)
        v = dot(table[rows, :], operand[...])
        if extra is not None:
            extra[m].wait()
            v = v + extra[4][rows, :].astype(F32)
        held[rows, :] = v.astype(BF16)
        copies.append(pltpu.make_async_copy(held.at[rows, :], out.at[rows, :], sems.at[m]))
        copies[-1].start()
    for copy in copies:
        copy.wait()


def columns_kernel(table_ref, x_ref, out_any, lines_any, held, sems, line_sem):
    keep = pltpu.make_async_copy(x_ref, lines_any, line_sem)
    keep.start()
    stream_dot(table_ref, x_ref, None, held, out_any, sems)
    keep.wait()


def forward_columns(table, x):
    vmem, hbm = pl.BlockSpec(memory_space=pltpu.VMEM), pl.BlockSpec(memory_space=pltpu.HBM)
    return pl.pallas_call(
        columns_kernel,
        in_specs=[vmem] * 2,
        out_specs=[hbm, hbm],
        out_shape=[pltpu.HBM((1024, 512), BF16), pltpu.HBM((1024, 512), BF16)],
        scratch_shapes=[
            pltpu.VMEM((1024, 512), BF16),
            pltpu.SemaphoreType.DMA((4,)),
            pltpu.SemaphoreType.DMA,
        ],
        cost_estimate=pl.CostEstimate(flops=2**30, bytes_accessed=2**21, transcendentals=0),
        compiler_params=pltpu.CompilerParams(vmem_limit_bytes=12 * MIB),
        name="forward_columns",
    )(resident(table), resident(x))


def rims_kernel(last_tile, leading_tile, last_ref, leading_ref):
    low = low_half(512)
    top, bottom = last_tile[:512].astype(F32), last_tile[512:].astype(F32)
    last_ref[...] = jnp.where(low, swap(top), bottom).astype(BF16)
    top, bottom = leading_tile[:512].astype(F32), leading_tile[512:].astype(F32)
    leading_ref[...] = jnp.where(low, top, swap(bottom)).astype(BF16)


def rims(lines):
    row = pl.BlockSpec((512, 128), lambda g: (0, 0))
    return pl.pallas_call(
        rims_kernel,
        grid=(1,),
        in_specs=[
            pl.BlockSpec((1024, 128), lambda g: (0, 3)),
            pl.BlockSpec((1024, 128), lambda g: (0, 0)),
        ],
        out_specs=[row, row],
        out_shape=[pltpu.HBM((512, 128), BF16)] * 2,
        cost_estimate=pl.CostEstimate(flops=2**17, bytes_accessed=2**20, transcendentals=0),
        compiler_params=pltpu.CompilerParams(vmem_limit_bytes=6 * MIB),
        name="rims",
    )(remaining(lines), remaining(lines))


def columns_add_kernel(table_ref, x_ref, extra_any, out_any, held, sems, extra, extra_sems):
    fetches = []
    for m in range(4):
        rows = slice(256 * m, 256 * m + 256)
        fetches.append(
            pltpu.make_async_copy(extra_any.at[rows, :], extra.at[rows, :], extra_sems.at[m])
        )
        fetches[-1].start()
    stream_dot(table_ref, x_ref, (*fetches, extra), held, out_any, sems)


def backward_columns(table, x, extra):
    vmem, hbm = pl.BlockSpec(memory_space=pltpu.VMEM), pl.BlockSpec(memory_space=pltpu.HBM)
    return pl.pallas_call(
        columns_add_kernel,
        in_specs=[vmem, vmem, hbm],
        out_specs=hbm,
        out_shape=pltpu.HBM((1024, 512), BF16),
        scratch_shapes=[
            pltpu.VMEM((1024, 512), BF16),
            pltpu.SemaphoreType.DMA((4,)),
            pltpu.VMEM((1024, 512), BF16),
            pltpu.SemaphoreType.DMA((4,)),
        ],
        cost_estimate=pl.CostEstimate(flops=2**30, bytes_accessed=2**21, transcendentals=0),
        compiler_params=pltpu.CompilerParams(vmem_limit_bytes=12 * MIB),
        name="backward_columns",
    )(resident(table), resident(x), remaining(extra))


def stencil_kernel(x_ref, above_ref, below_ref, taps_ref, out_ref):
    low = low_half(512)

    def tile(t):
        return x_ref[:, 128 * t : 128 * t + 128].astype(F32)

    def between(t):
        if t < 0:
            other = above_ref[...].astype(F32)
            return jnp.concatenate(
                [
                    jnp.where(low, other, swap(tile(0)[:512])),
                    jnp.where(low, swap(other), swap(tile(0)[512:])),
                ],
                axis=0,
            )
        if t == 3:
            other = below_ref[...].astype(F32)
            return jnp.concatenate(
                [
                    jnp.where(low, swap(tile(3)[:512]), swap(other)),
                    jnp.where(low, swap(tile(3)[512:]), other),
                ],
                axis=0,
            )
        return jnp.where(low_half(1024), swap(tile(t)), swap(tile(t + 1)))

    for t in range(4):
        rows = (between(t - 1), tile(t), between(t))
        total = None
        for j in range(3):
            part = rows[0] * taps_ref[j : j + 1, :]
            part = part + rows[1] * taps_ref[3 + j : 4 + j, :]
            part = part + rows[2] * taps_ref[6 + j : 7 + j, :]
            if j != 1:
                part = pltpu.roll(part, 1 if j == 0 else 1023, 0)
            total = part if total is None else total + part
        out_ref[:, 128 * t : 128 * t + 128] = total.astype(BF16)


def stencil(x, above, below, taps):
    return pl.pallas_call(
        stencil_kernel,
        in_specs=[pl.BlockSpec((1024, 512), lambda g: (0, 0))]
        + [pl.BlockSpec((512, 128), lambda g: (0, 0))] * 2
        + [pl.BlockSpec(memory_space=pltpu.VMEM)],
        grid=(1,),
        out_specs=pl.BlockSpec((1024, 512), lambda g: (0, 0)),
        out_shape=pltpu.HBM((1024, 512), BF16),
        cost_estimate=pl.CostEstimate(flops=2**24, bytes_accessed=2**22, transcendentals=0),
        compiler_params=pltpu.CompilerParams(vmem_limit_bytes=16 * MIB),
        name="stencil",
    )(remaining(x), remaining(above), remaining(below), taps)


def middle_kernel(
    z, fwd, cos_any, sin_any, first_any, eight_any, inv_any, second_any, out_any,
    cos_ref, sin_ref, first, eight, inv, second_ref, held, done, sems, fetch_sems,
):
    fetches = []
    for n, (src, dst) in enumerate(
        (
            (cos_any, cos_ref),
            (sin_any, sin_ref),
            (first_any, first),
            (eight_any, eight),
            (inv_any, inv),
            (second_any, second_ref),
        )
    ):
        fetches.append(pltpu.make_async_copy(src, dst, fetch_sems.at[n]))
    for n in (0, 1, 2, 5):
        fetches[n].start()
    rows = 512 // CHUNKS
    groups = 8 // CHUNKS
    for m in range(CHUNKS):
        u = dot(fwd[2 * rows * m : 2 * rows * (m + 1), :], z[...])
        shape = (groups, 4, 16, 512)
        ur, ui = u[:rows].reshape(shape), u[rows:].reshape(shape)
        if m == 0:
            fetches[0].wait()
            fetches[1].wait()
            fetches[3].start()
        c = cos_ref[16 * groups * m : 16 * groups * (m + 1), :].reshape(groups, 1, 16, 512)
        s = sin_ref[16 * groups * m : 16 * groups * (m + 1), :].reshape(groups, 1, 16, 512)
        vr = (ur * c + ui * s).astype(BF16).reshape(rows, 512)
        vi = (ui * c - ur * s).astype(BF16).reshape(rows, 512)
        if m == 0:
            fetches[2].wait()
            fetches[5].wait()
            fetches[4].start()
        hidden = jnp.tanh(dot(vr, first[:512, :]) + dot(vi, first[512:, :])).astype(BF16)
        parts = []
        for t in range(4):
            v = dot(hidden[:, 256 * t : 256 * t + 256], second_ref[...])
            v = jnp.where(v > 0.25, v - 0.25, jnp.where(v < -0.25, v + 0.25, 0.0 * v))
            parts.append(v.astype(BF16))
        if m == 0:
            fetches[3].wait()
        y = dot(jnp.concatenate(parts, axis=1), eight[...])
        yr, yi = y[:, :512].reshape(shape), y[:, 512:].reshape(shape)
        held[2 * rows * m : 2 * rows * m + rows, :] = (yr * c - yi * s).astype(BF16).reshape(rows, 512)
        held[2 * rows * m + rows : 2 * rows * (m + 1), :] = (
            (yi * c + yr * s).astype(BF16).reshape(rows, 512)
        )
    fetches[4].wait()
    stream_dot(inv, held, None, done, out_any, sems)


def middle(z, fwd, first, eight, inv, second, cos, sin):
    vmem, hbm = pl.BlockSpec(memory_space=pltpu.VMEM), pl.BlockSpec(memory_space=pltpu.HBM)
    return pl.pallas_call(
        middle_kernel,
        in_specs=[vmem] * 2 + [hbm] * 6,
        out_specs=hbm,
        out_shape=pltpu.HBM((1024, 512), BF16),
        scratch_shapes=[
            pltpu.VMEM((128, 512), F32),
            pltpu.VMEM((128, 512), F32),
            pltpu.VMEM((1024, 1024), BF16),
            pltpu.VMEM((1024, 1024), BF16),
            pltpu.VMEM((1024, 1024), BF16),
            pltpu.VMEM((256, 256), BF16),
            pltpu.VMEM((1024, 512), BF16),
            pltpu.VMEM((1024, 512), BF16),
            pltpu.SemaphoreType.DMA((4,)),
            pltpu.SemaphoreType.DMA((6,)),
        ],
        cost_estimate=pl.CostEstimate(flops=5 * 2**30, bytes_accessed=2**21, transcendentals=2**19),
        compiler_params=pltpu.CompilerParams(vmem_limit_bytes=28 * MIB),
        name="filter_rows",
    )(
        resident(z), resident(fwd), remaining(cos), remaining(sin), remaining(first),
        remaining(eight), remaining(inv), remaining(second),
    )


def local(patches, norm_gain, w_first, w_second, depth_kernel):
    packed = norm_and_pack(patches, norm_gain)
    lines = lax.all_to_all(packed, ("yl", "x"), 0, 0, tiled=True).reshape(1024, 512)

    fwd_w = table(pltpu.VMEM, forward_columns_phases)
    inv_w = table(pltpu.VMEM, backward_columns_phases)
    inv_h = table(pltpu.HBM, backward_rows_phases)
    first, eight, second = block_tables(w_first, w_second)
    fwd_h, cos, sin = table(pltpu.VMEM, forward_rows_phases, True, (second, inv_h))
    block = lax.axis_index("x")
    taps = lax.dynamic_slice_in_dim(depth_kernel.reshape(9, 256), 64 * block, 64, 1)
    taps = jnp.concatenate([taps, taps], axis=1)

    freqs, kept = forward_columns(fwd_w, lines)
    last, leading = rims(kept)
    whole = lax.all_to_all(freqs.reshape(128, 8, 512), ("row", "yl"), 0, 0, tiled=True)
    groups = 128
    down = [(i, (i + 1) % groups) for i in range(groups)]
    up = [(j, i) for i, j in down]
    above = lax.ppermute(last, ("row", "yl"), down)
    below = lax.ppermute(leading, ("row", "yl"), up)
    whole, above, below = lax.optimization_barrier((whole, above, below))

    filtered = middle(whole.reshape(1024, 512), fwd_h, first, eight, inv_h, second, cos, sin)
    filtered, above, below = lax.optimization_barrier((filtered, above, below))
    back = lax.all_to_all(filtered.reshape(128, 8, 512), ("row", "yl"), 0, 0, tiled=True)
    conv = stencil(kept, above, below, taps)
    summed = backward_columns(inv_w, back.reshape(1024, 512), conv).reshape(16, 64, 512)
    home = lax.all_to_all(summed, ("yl", "x"), 0, 0, tiled=True)
    return unpack_and_add(patches, home)


def solution(mesh):
    fine = Mesh(np.asarray(mesh.devices).reshape(32, 4, 4), ("row", "yl", "x"))
    return jax.shard_map(
        local,
        mesh=fine,
        in_specs=(P("row", ("yl", "x"), None), P(), P(), P(), P()),
        out_specs=P("row", ("yl", "x"), None),
        check_vma=False,
    )
```

```python
import functools
import math

import jax
import jax.numpy as jnp
import numpy as np
from jax import lax
from jax.experimental import pallas as pl
from jax.experimental.pallas import tpu as pltpu
from jax.sharding import Mesh
from jax.sharding import PartitionSpec as P

TURN = 1024
CHUNKS = 2
MIB = 1024 * 1024
F32 = jnp.float32
BF16 = jnp.bfloat16


def iota(shape, dim):
    return lax.broadcasted_iota(jnp.int32, shape, dim)


def digit(idx, shift, bits):
    return (idx >> shift) & ((1 << bits) - 1)


def cos_sin(idx):
    idx = idx & (TURN - 1)
    quarter = (idx + TURN // 8) >> 8
    x = (idx - (quarter << 8)).astype(F32) * (2.0 * math.pi / TURN)
    y = x * x
    s = x * (1.0 + y * (-1.0 / 6 + y * (1.0 / 120 + y * (-1.0 / 5040 + y * (1.0 / 362880)))))
    c = 1.0 + y * (-1.0 / 2 + y * (1.0 / 24 + y * (-1.0 / 720 + y * (1.0 / 40320))))
    odd = (quarter & 1) == 1
    cos, sin = jnp.where(odd, s, c), jnp.where(odd, c, s)
    turned = (quarter + 1) & 3
    cos = jnp.where(turned >= 2, -cos, cos)
    sin = jnp.where((quarter & 3) >= 2, -sin, sin)
    return cos, sin


SCALE = 1.0 / 32.0


def forward_columns_phases():
    a, b = iota((16, 1024), 0), iota((64, 1024), 0)
    w = iota((64, 1024), 1)
    k = 4 * digit(b, 3, 3) + digit(b, 0, 2)
    return 32 * a * w[:16], k * w + 256 * digit(b, 2, 1), SCALE


def backward_columns_phases():
    a, b, lane = iota((16, 1024), 0), iota((64, 1024), 0), iota((64, 1024), 1)
    k = 4 * (lane >> 3) + digit(lane, 0, 2)
    weight = jnp.where(k == 0, SCALE, 2.0 * SCALE)
    return 64 * a * k[:16], b * k + 256 * digit(lane, 2, 1), weight


def forward_rows_phases():
    a, b, lane = iota((16, 1024), 0), iota((64, 1024), 0), iota((64, 1024), 1)
    qh = 4 * digit(a, 3, 1) + digit(a, 0, 2)
    p, ri = lane >> 3, digit(lane, 2, 1)
    ia = 128 * qh * p[:16] + 256 * (digit(a, 2, 1) - ri[:16])
    weight = jnp.where(digit(b, 4, 2) == digit(lane, 0, 2), SCALE, 0.0)
    return ia, 8 * digit(b, 0, 4) * p, weight


def backward_rows_phases():
    a, b, lane = iota((16, 1024), 0), iota((64, 1024), 0), iota((64, 1024), 1)
    q0 = 16 * (4 * digit(lane, 9, 1) + digit(lane, 6, 2)) + digit(lane, 0, 4)
    ro = digit(lane, 8, 1)
    weight = jnp.where(digit(b, 0, 2) == digit(lane, 4, 2), SCALE, 0.0)
    return 64 * a * q0[:16], 8 * digit(b, 3, 3) * q0 + 256 * (ro - digit(b, 2, 1)), weight


def table_kernel(phases, with_twiddles, stay, waited, *refs):
    refs = refs[waited:]
    out_ref, (ec, es, fc, fs) = refs[0], refs[-4:]
    steps = 16 if stay else 4

    @pl.when(pl.program_id(0) == 0)
    def _():
        ia, ib, weight = phases()
        ec[...], es[...] = cos_sin(ia)
        c, s = cos_sin(ib)
        fc[...], fs[...] = c * weight, s * weight
        if with_twiddles:
            angle = iota((128, 512), 0) * (iota((128, 512), 1) >> 6)
            refs[1][...], refs[2][...] = cos_sin(angle)

    first = 0 if stay else steps * pl.program_id(0)

    def step(a, carry):
        row = pl.ds(first + a, 1)
        out_ref[pl.ds(pl.multiple_of(64 * a, 64), 64), :] = (
            ec[row, :] * fc[...] - es[row, :] * fs[...]
        ).astype(BF16)
        return carry

    lax.fori_loop(0, steps, step, 0)


def table(space, phases, with_twiddles=False, after=()):
    stay = space == pltpu.VMEM
    whole = pl.BlockSpec(memory_space=pltpu.VMEM)
    twiddle_spec = pl.BlockSpec((128, 512), lambda g: (0, 0))
    out = pl.pallas_call(
        functools.partial(table_kernel, phases, with_twiddles, stay, len(after)),
        grid=(1,) if stay else (4,),
        in_specs=[pl.BlockSpec(memory_space=pltpu.HBM)] * len(after),
        out_specs=[whole if stay else pl.BlockSpec((256, 1024), lambda g: (g, 0))]
        + [twiddle_spec] * (2 * with_twiddles),
        out_shape=[space((1024, 1024), BF16)] + [pltpu.HBM((128, 512), F32)] * (2 * with_twiddles),
        scratch_shapes=[pltpu.VMEM((n, 1024), F32) for n in (16, 16, 64, 64)],
        cost_estimate=pl.CostEstimate(flops=2**23, bytes_accessed=2**21, transcendentals=0),
        compiler_params=pltpu.CompilerParams(vmem_limit_bytes=6 * MIB),
        name=phases.__name__,
    )(*[remaining(v) for v in after])
    return out if with_twiddles else out[0]


def blocks_kernel(first_w, second_w, first_ref, eight_ref, second_ref, acc, ass, bcc):
    block = lax.axis_index("x")
    low = low_half(64)

    def twice(ref, n):
        w = ref[n, block].astype(F32)
        return jnp.concatenate([w, w], axis=1)

    @pl.when(pl.program_id(0) == 0)
    def _():
        a, lane = iota((16, 1024), 0), iota((16, 1024), 1)
        q1 = 2 * digit(lane, 8, 2) + digit(lane, 6, 1)
        acc[...], ass[...] = cos_sin(
            128 * q1 * digit(a, 0, 3) + 256 * (digit(lane, 7, 1) - digit(a, 3, 1))
        )
        q1 = 2 * digit(a, 2, 2) + digit(a, 0, 1)
        bcc[...], _unused = cos_sin(
            128 * q1 * digit(lane, 6, 3) - 256 * (digit(lane, 9, 1) - digit(a, 1, 1))
        )
        w0, w1 = twice(second_w, 0), twice(second_w, 1)
        zero = jnp.zeros_like(w0)
        for half in range(2):
            def own(v):
                return (jnp.where(low, v, zero) if half == 0 else jnp.where(low, zero, v)).astype(BF16)

            re, im = slice(64 * half, 64 * half + 64), slice(128 + 64 * half, 192 + 64 * half)
            second_ref[re, :128], second_ref[re, 128:] = own(w0), own(w1)
            second_ref[im, :128], second_ref[im, 128:] = own(-w1), own(w0)

    w0, w1 = twice(first_w, 0), twice(first_w, 1)
    eye = jnp.where(iota((64, 128), 0) == (iota((64, 128), 1) & 63), 1.0, 0.0)
    first = 4 * pl.program_id(0)

    def step(a, carry):
        rows = pl.ds(pl.multiple_of(64 * a, 64), 64)
        row = pl.ds(first + a, 1)
        c, s, back = acc[row, :], ass[row, :], bcc[row, :]
        for t in range(8):
            lanes = slice(128 * t, 128 * t + 128)
            first_ref[rows, lanes] = (c[:, lanes] * w0 + s[:, lanes] * w1).astype(BF16)
            eight_ref[rows, lanes] = (back[:, lanes] * eye).astype(BF16)
        return carry

    lax.fori_loop(0, 4, step, 0)


def block_tables(w_first, w_second):
    vmem = pl.BlockSpec(memory_space=pltpu.VMEM)
    quarter = pl.BlockSpec((256, 1024), lambda g: (g, 0))
    return pl.pallas_call(
        blocks_kernel,
        grid=(4,),
        in_specs=[vmem, vmem],
        out_specs=[quarter, quarter, pl.BlockSpec((256, 256), lambda g: (0, 0))],
        out_shape=[
            pltpu.HBM((1024, 1024), BF16),
            pltpu.HBM((1024, 1024), BF16),
            pltpu.HBM((256, 256), BF16),
        ],
        scratch_shapes=[pltpu.VMEM((16, 1024), F32)] * 3,
        cost_estimate=pl.CostEstimate(flops=2**23, bytes_accessed=2**22, transcendentals=0),
        compiler_params=pltpu.CompilerParams(vmem_limit_bytes=8 * MIB),
        name="block_tables",
    )(w_first, w_second)


def low_half(rows):
    return lax.broadcasted_iota(jnp.int32, (rows, 128), 1) < 64


def swap(v):
    return pltpu.roll(v, 64, 1)


def normed_halves(x_ref, gain_ref):
    ones = jnp.ones((256, 128), BF16)
    x = x_ref[...].reshape(512, 256)
    mean = dot(x, ones) * (1.0 / 256.0)
    d0, d1 = x[:, :128].astype(F32) - mean, x[:, 128:].astype(F32) - mean
    square = d0 * d0 + d1 * d1
    coarse = square.astype(BF16)
    fine = (square - coarse.astype(F32)).astype(BF16)
    var = dot(jnp.concatenate([coarse, fine], axis=1), ones) * (1.0 / 256.0)
    scale = lax.rsqrt(var + 1e-05)
    return d0 * scale * gain_ref[:, :128], d1 * scale * gain_ref[:, 128:]


def norm_kernel(x_any, gain_ref, out_any, x_all, packed, in_sems, out_sems):
    low = low_half(64)
    fetches, sends = [], []
    for g in range(4):
        rows = slice(8 * g, 8 * g + 8)
        fetches.append(pltpu.make_async_copy(x_any.at[rows], x_all.at[rows], in_sems.at[g]))
        fetches[-1].start()
    for g in range(4):
        fetches[g].wait()
        halves = normed_halves(x_all.at[8 * g : 8 * g + 8], gain_ref)
        for t in range(4):
            lanes = slice(128 * t, 128 * t + 128)
            for m in range(2):
                a = halves[m][128 * t : 128 * t + 64]
                b = halves[m][128 * t + 64 : 128 * t + 128]
                packed[4 * g + 2 * m, :, lanes] = jnp.where(low, a, swap(b)).astype(BF16)
                packed[4 * g + 2 * m + 1, :, lanes] = jnp.where(low, swap(a), b).astype(BF16)
        parts = slice(4 * g, 4 * g + 4)
        sends.append(pltpu.make_async_copy(packed.at[parts], out_any.at[parts], out_sems.at[g]))
        sends[-1].start()
    for send in sends:
        send.wait()


def home_norm_kernel(x_ref, gain_ref, out_ref):
    for m, half in enumerate(normed_halves(x_ref, gain_ref)):
        out_ref[:, :, 128 * m : 128 * m + 128] = half.astype(BF16).reshape(8, 64, 128)


def home_norm(patches, gain):
    block = pl.BlockSpec((8, 64, 256), lambda g: (g, 0, 0))
    return pl.pallas_call(
        home_norm_kernel,
        grid=(4,),
        in_specs=[block, pl.BlockSpec((1, 256), lambda g: (0, 0))],
        out_specs=block,
        out_shape=pltpu.HBM((32, 64, 256), BF16),
        cost_estimate=pl.CostEstimate(flops=2**24, bytes_accessed=2**21, transcendentals=0),
        compiler_params=pltpu.CompilerParams(vmem_limit_bytes=12 * MIB),
        name="home_norm",
    )(remaining(patches), remaining(gain.reshape(1, 256)))


def norm_and_pack(patches, gain):
    return pl.pallas_call(
        norm_kernel,
        in_specs=[pl.BlockSpec(memory_space=pltpu.HBM), pl.BlockSpec(memory_space=pltpu.VMEM)],
        out_specs=pl.BlockSpec(memory_space=pltpu.HBM),
        out_shape=pltpu.HBM((16, 64, 512), BF16),
        scratch_shapes=[
            pltpu.VMEM((32, 64, 256), BF16),
            pltpu.VMEM((16, 64, 512), BF16),
            pltpu.SemaphoreType.DMA((4,)),
            pltpu.SemaphoreType.DMA((4,)),
        ],
        compiler_params=pltpu.CompilerParams(vmem_limit_bytes=16 * MIB),
        name="norm_pack",
    )(remaining(patches), remaining(gain.reshape(1, 256)))


def final_kernel(base_ref, home_ref, out_ref):
    low = low_half(64)
    first = 4 * pl.program_id(0)
    for t in range(4):
        lanes = slice(128 * t, 128 * t + 128)
        for m in range(2):
            u = home_ref[first + 2 * m, :, lanes].astype(F32)
            v = home_ref[first + 2 * m + 1, :, lanes].astype(F32)
            chans = slice(128 * m, 128 * m + 128)
            even, odd = jnp.where(low, u, swap(v)), jnp.where(low, swap(u), v)
            out_ref[2 * t, :, chans] = (base_ref[2 * t, :, chans] + even).astype(BF16)
            out_ref[2 * t + 1, :, chans] = (base_ref[2 * t + 1, :, chans] + odd).astype(BF16)


def unpack_and_add(base, home):
    return pl.pallas_call(
        final_kernel,
        grid=(4,),
        in_specs=[
            pl.BlockSpec((8, 64, 256), lambda g: (g, 0, 0)),
            pl.BlockSpec(memory_space=pltpu.VMEM),
        ],
        out_specs=pl.BlockSpec((8, 64, 256), lambda g: (g, 0, 0)),
        out_shape=jax.ShapeDtypeStruct((32, 64, 256), BF16),
        compiler_params=pltpu.CompilerParams(vmem_limit_bytes=8 * MIB),
        name="unpack_add",
    )(base, resident(home))


def dot(a, b):
    return jnp.dot(a, b, preferred_element_type=F32)


def resident(v):
    return pltpu.with_memory_space_constraint(v, pltpu.VMEM)


def remaining(v):
    return pltpu.with_memory_space_constraint(v, pltpu.HBM)


def stream_dot(table, operand, held, out, sems):
    copies = []
    for m in range(4):
        rows = slice(256 * m, 256 * m + 256)
        held[rows, :] = dot(table[rows, :], operand[...]).astype(BF16)
        copies.append(pltpu.make_async_copy(held.at[rows, :], out.at[rows, :], sems.at[m]))
        copies[-1].start()
    for copy in copies:
        copy.wait()


def columns_kernel(table_ref, x_ref, out_any, held, sems):
    stream_dot(table_ref, x_ref, held, out_any, sems)


def columns(table, x):
    return pl.pallas_call(
        columns_kernel,
        in_specs=[pl.BlockSpec(memory_space=pltpu.VMEM)] * 2,
        out_specs=pl.BlockSpec(memory_space=pltpu.HBM),
        out_shape=pltpu.HBM((1024, 512), BF16),
        scratch_shapes=[pltpu.VMEM((1024, 512), BF16), pltpu.SemaphoreType.DMA((4,))],
        cost_estimate=pl.CostEstimate(flops=2**30, bytes_accessed=2**21, transcendentals=0),
        compiler_params=pltpu.CompilerParams(vmem_limit_bytes=12 * MIB),
        name="along_columns",
    )(resident(table), resident(x))


def stencil_kernel(
    x_ref, normed_ref, top_ref, bottom_ref, left_ref, right_ref, taps_ref, out_ref,
    rows, side, left_sum, right_sum,
):
    def tap(i, j):
        return taps_ref[3 * i + j : 3 * i + j + 1, :]

    @pl.when(pl.program_id(0) == 0)
    def _():
        rows[0], rows[33] = top_ref[...], bottom_ref[...]
        rows[1:33] = normed_ref[...]
        for rim_ref, sum_ref, j in ((left_ref, left_sum, 0), (right_ref, right_sum, 2)):
            side[...] = rim_ref[...].astype(F32)
            sum_ref[...] = side[0:32] * tap(0, j) + side[1:33] * tap(1, j) + side[2:34] * tap(2, j)

    column = iota((64, 256), 0)

    def step(r, carry):
        h = 8 * pl.program_id(0) + r
        around = [rows[h + i].astype(F32) for i in range(3)]

        def part(j):
            return around[0] * tap(0, j) + around[1] * tap(1, j) + around[2] * tap(2, j)

        left = jnp.where(column == 0, left_sum[pl.ds(h, 1), :], pltpu.roll(part(0), 1, 0))
        right = jnp.where(column == 63, right_sum[pl.ds(h, 1), :], pltpu.roll(part(2), 63, 0))
        out_ref[r] = x_ref[r].astype(F32) + (left + part(1) + right)
        return carry

    lax.fori_loop(0, 8, step, 0)


def stencil(x, normed, top, bottom, left, right, taps):
    block = pl.BlockSpec((8, 64, 256), lambda g: (g, 0, 0))
    row = pl.BlockSpec((64, 256), lambda g: (0, 0))
    side = pl.BlockSpec((34, 256), lambda g: (0, 0))
    return pl.pallas_call(
        stencil_kernel,
        grid=(4,),
        in_specs=[
            block,
            pl.BlockSpec((32, 64, 256), lambda g: (0, 0, 0)),
            row, row, side, side,
            pl.BlockSpec((9, 256), lambda g: (0, 0)),
        ],
        out_specs=block,
        out_shape=pltpu.HBM((32, 64, 256), F32),
        scratch_shapes=[
            pltpu.VMEM((34, 64, 256), BF16),
            pltpu.VMEM((34, 256), F32),
            pltpu.VMEM((32, 256), F32),
            pltpu.VMEM((32, 256), F32),
        ],
        cost_estimate=pl.CostEstimate(flops=2**24, bytes_accessed=2**22, transcendentals=0),
        compiler_params=pltpu.CompilerParams(vmem_limit_bytes=12 * MIB),
        name="stencil",
    )(*[remaining(v) for v in (x, normed, top, bottom, left, right, taps)])


def middle_kernel(
    z, fwd, cos_any, sin_any, first_any, eight_any, inv_any, second_any, out_any,
    cos_ref, sin_ref, first, eight, inv, second_ref, held, done, sems, fetch_sems,
):
    fetches = []
    for n, (src, dst) in enumerate(
        (
            (cos_any, cos_ref),
            (sin_any, sin_ref),
            (first_any, first),
            (eight_any, eight),
            (inv_any, inv),
            (second_any, second_ref),
        )
    ):
        fetches.append(pltpu.make_async_copy(src, dst, fetch_sems.at[n]))
    for n in (0, 1, 2, 5):
        fetches[n].start()
    rows = 512 // CHUNKS
    groups = 8 // CHUNKS
    for m in range(CHUNKS):
        u = dot(fwd[2 * rows * m : 2 * rows * (m + 1), :], z[...])
        shape = (groups, 4, 16, 512)
        ur, ui = u[:rows].reshape(shape), u[rows:].reshape(shape)
        if m == 0:
            fetches[0].wait()
            fetches[1].wait()
            fetches[3].start()
        c = cos_ref[16 * groups * m : 16 * groups * (m + 1), :].reshape(groups, 1, 16, 512)
        s = sin_ref[16 * groups * m : 16 * groups * (m + 1), :].reshape(groups, 1, 16, 512)
        vr = (ur * c + ui * s).astype(BF16).reshape(rows, 512)
        vi = (ui * c - ur * s).astype(BF16).reshape(rows, 512)
        if m == 0:
            fetches[2].wait()
            fetches[5].wait()
            fetches[4].start()
        hidden = jnp.tanh(dot(vr, first[:512, :]) + dot(vi, first[512:, :])).astype(BF16)
        parts = []
        for t in range(4):
            v = dot(hidden[:, 256 * t : 256 * t + 256], second_ref[...])
            v = jnp.where(v > 0.25, v - 0.25, jnp.where(v < -0.25, v + 0.25, 0.0 * v))
            parts.append(v.astype(BF16))
        if m == 0:
            fetches[3].wait()
        y = dot(jnp.concatenate(parts, axis=1), eight[...])
        yr, yi = y[:, :512].reshape(shape), y[:, 512:].reshape(shape)
        held[2 * rows * m : 2 * rows * m + rows, :] = (yr * c - yi * s).astype(BF16).reshape(rows, 512)
        held[2 * rows * m + rows : 2 * rows * (m + 1), :] = (
            (yi * c + yr * s).astype(BF16).reshape(rows, 512)
        )
    fetches[4].wait()
    stream_dot(inv, held, done, out_any, sems)


def middle(z, fwd, first, eight, inv, second, cos, sin):
    vmem, hbm = pl.BlockSpec(memory_space=pltpu.VMEM), pl.BlockSpec(memory_space=pltpu.HBM)
    return pl.pallas_call(
        middle_kernel,
        in_specs=[vmem] * 2 + [hbm] * 6,
        out_specs=hbm,
        out_shape=pltpu.HBM((1024, 512), BF16),
        scratch_shapes=[
            pltpu.VMEM((128, 512), F32),
            pltpu.VMEM((128, 512), F32),
            pltpu.VMEM((1024, 1024), BF16),
            pltpu.VMEM((1024, 1024), BF16),
            pltpu.VMEM((1024, 1024), BF16),
            pltpu.VMEM((256, 256), BF16),
            pltpu.VMEM((1024, 512), BF16),
            pltpu.VMEM((1024, 512), BF16),
            pltpu.SemaphoreType.DMA((4,)),
            pltpu.SemaphoreType.DMA((6,)),
        ],
        cost_estimate=pl.CostEstimate(flops=5 * 2**30, bytes_accessed=2**21, transcendentals=2**19),
        compiler_params=pltpu.CompilerParams(vmem_limit_bytes=28 * MIB),
        name="filter_rows",
    )(
        resident(z), resident(fwd), remaining(cos), remaining(sin), remaining(first),
        remaining(eight), remaining(inv), remaining(second),
    )


def local(patches, norm_gain, w_first, w_second, depth_kernel):
    packed = norm_and_pack(patches, norm_gain)
    lines = lax.all_to_all(packed, ("yl", "x"), 0, 0, tiled=True).reshape(1024, 512)

    fwd_w = table(pltpu.VMEM, forward_columns_phases)
    inv_w = table(pltpu.VMEM, backward_columns_phases)
    inv_h = table(pltpu.HBM, backward_rows_phases)
    first, eight, second = block_tables(w_first, w_second)
    fwd_h, cos, sin = table(pltpu.VMEM, forward_rows_phases, True, (second, inv_h))

    def neighbours(first, last, axis):
        n = lax.axis_size(axis)
        before = lax.ppermute(last, axis, [(i, (i + 1) % n) for i in range(n)])
        after = lax.ppermute(first, axis, [((i + 1) % n, i) for i in range(n)])
        return before, after

    normed = home_norm(patches, norm_gain)
    top, bottom = neighbours(normed[0], normed[31], "row")
    lines, top, bottom = lax.optimization_barrier((lines, top, bottom))

    freqs = columns(fwd_w, lines)
    whole = lax.all_to_all(freqs.reshape(128, 8, 512), ("row", "yl"), 0, 0, tiled=True)
    sides = [
        jnp.concatenate([top[w : w + 1], normed[:, w], bottom[w : w + 1]], axis=0) for w in (0, 63)
    ]
    left, right = neighbours(sides[0], sides[1], ("yl", "x"))
    whole, left, right = lax.optimization_barrier((whole, left, right))

    filtered = middle(whole.reshape(1024, 512), fwd_h, first, eight, inv_h, second, cos, sin)
    filtered, left, right = lax.optimization_barrier((filtered, left, right))
    back = lax.all_to_all(filtered.reshape(128, 8, 512), ("row", "yl"), 0, 0, tiled=True)
    base = stencil(patches, normed, top, bottom, left, right, depth_kernel.reshape(9, 256))
    spectral = columns(inv_w, back.reshape(1024, 512))
    spectral, base = lax.optimization_barrier((spectral, base))
    home = lax.all_to_all(spectral.reshape(16, 64, 512), ("yl", "x"), 0, 0, tiled=True)
    return unpack_and_add(base, home)


def solution(mesh):
    fine = Mesh(np.asarray(mesh.devices).reshape(32, 4, 4), ("row", "yl", "x"))
    return jax.shard_map(
        local,
        mesh=fine,
        in_specs=(P("row", ("yl", "x"), None), P(), P(), P(), P()),
        out_specs=P("row", ("yl", "x"), None),
        check_vma=False,
    )
```

```python
import functools
import math

import jax
import jax.numpy as jnp
import numpy as np
from jax import lax
from jax.experimental import pallas as pl
from jax.experimental.pallas import tpu as pltpu
from jax.sharding import Mesh
from jax.sharding import PartitionSpec as P

TURN = 1024
CHUNKS = 2
MIB = 1024 * 1024
F32 = jnp.float32
BF16 = jnp.bfloat16


def iota(shape, dim):
    return lax.broadcasted_iota(jnp.int32, shape, dim)


def digit(idx, shift, bits):
    return (idx >> shift) & ((1 << bits) - 1)


def cos_sin(idx):
    idx = idx & (TURN - 1)
    quarter = (idx + TURN // 8) >> 8
    x = (idx - (quarter << 8)).astype(F32) * (2.0 * math.pi / TURN)
    y = x * x
    s = x * (1.0 + y * (-1.0 / 6 + y * (1.0 / 120 + y * (-1.0 / 5040 + y * (1.0 / 362880)))))
    c = 1.0 + y * (-1.0 / 2 + y * (1.0 / 24 + y * (-1.0 / 720 + y * (1.0 / 40320))))
    odd = (quarter & 1) == 1
    cos, sin = jnp.where(odd, s, c), jnp.where(odd, c, s)
    turned = (quarter + 1) & 3
    cos = jnp.where(turned >= 2, -cos, cos)
    sin = jnp.where((quarter & 3) >= 2, -sin, sin)
    return cos, sin


SCALE = 1.0 / 32.0


def forward_columns_phases():
    a, b = iota((16, 1024), 0), iota((64, 1024), 0)
    w = iota((64, 1024), 1)
    k = 4 * digit(b, 3, 3) + digit(b, 0, 2)
    return 32 * a * w[:16], k * w + 256 * digit(b, 2, 1), SCALE


def backward_columns_phases():
    a, b, lane = iota((16, 1024), 0), iota((64, 1024), 0), iota((64, 1024), 1)
    k = 4 * (lane >> 3) + digit(lane, 0, 2)
    weight = jnp.where(k == 0, SCALE, 2.0 * SCALE)
    return 64 * a * k[:16], b * k + 256 * digit(lane, 2, 1), weight


def forward_rows_phases():
    a, b, lane = iota((16, 1024), 0), iota((64, 1024), 0), iota((64, 1024), 1)
    qh = 4 * digit(a, 3, 1) + digit(a, 0, 2)
    p, ri = lane >> 3, digit(lane, 2, 1)
    ia = 128 * qh * p[:16] + 256 * (digit(a, 2, 1) - ri[:16])
    weight = jnp.where(digit(b, 4, 2) == digit(lane, 0, 2), SCALE, 0.0)
    return ia, 8 * digit(b, 0, 4) * p, weight


def backward_rows_phases():
    a, b, lane = iota((16, 1024), 0), iota((64, 1024), 0), iota((64, 1024), 1)
    q0 = 16 * (4 * digit(lane, 9, 1) + digit(lane, 6, 2)) + digit(lane, 0, 4)
    ro = digit(lane, 8, 1)
    weight = jnp.where(digit(b, 0, 2) == digit(lane, 4, 2), SCALE, 0.0)
    return 64 * a * q0[:16], 8 * digit(b, 3, 3) * q0 + 256 * (ro - digit(b, 2, 1)), weight


def table_kernel(phases, with_twiddles, stay, waited, *refs):
    refs = refs[waited:]
    out_ref, (ec, es, fc, fs) = refs[0], refs[-4:]
    steps = 16 if stay else 4

    @pl.when(pl.program_id(0) == 0)
    def _():
        ia, ib, weight = phases()
        ec[...], es[...] = cos_sin(ia)
        c, s = cos_sin(ib)
        fc[...], fs[...] = c * weight, s * weight
        if with_twiddles:
            lane = iota((128, 512), 1)
            angle = iota((128, 512), 0) * ((lane >> 7) + 4 * digit(lane, 6, 1))
            refs[1][...], refs[2][...] = cos_sin(angle)

    first = 0 if stay else steps * pl.program_id(0)

    def step(a, carry):
        row = pl.ds(first + a, 1)
        out_ref[pl.ds(pl.multiple_of(64 * a, 64), 64), :] = (
            ec[row, :] * fc[...] - es[row, :] * fs[...]
        ).astype(BF16)
        return carry

    lax.fori_loop(0, steps, step, 0)


def table(space, phases, with_twiddles=False, after=()):
    stay = space == pltpu.VMEM
    whole = pl.BlockSpec(memory_space=pltpu.VMEM)
    twiddle_spec = pl.BlockSpec((128, 512), lambda g: (0, 0))
    out = pl.pallas_call(
        functools.partial(table_kernel, phases, with_twiddles, stay, len(after)),
        grid=(1,) if stay else (4,),
        in_specs=[pl.BlockSpec(memory_space=pltpu.HBM)] * len(after),
        out_specs=[whole if stay else pl.BlockSpec((256, 1024), lambda g: (g, 0))]
        + [twiddle_spec] * (2 * with_twiddles),
        out_shape=[space((1024, 1024), BF16)] + [pltpu.HBM((128, 512), F32)] * (2 * with_twiddles),
        scratch_shapes=[pltpu.VMEM((n, 1024), F32) for n in (16, 16, 64, 64)],
        cost_estimate=pl.CostEstimate(flops=2**23, bytes_accessed=2**21, transcendentals=0),
        compiler_params=pltpu.CompilerParams(vmem_limit_bytes=6 * MIB),
        name=phases.__name__,
    )(*[remaining(v) for v in after])
    return out if with_twiddles else out[0]


def blocks_kernel(first_w, second_w, first_ref, last_ref, second_ref, fc, fs, bc):
    block = lax.axis_index("x")
    low = low_half(64)
    a, lane = iota((16, 256), 0), iota((16, 256), 1)
    t, ri, row_e = a >> 2, digit(a, 1, 1), a & 1
    ro, lane_e = lane >> 7, digit(lane, 6, 1)
    fc[...], fs[...] = cos_sin(128 * lane_e * (t + 4 * row_e) + 256 * (ro - ri))
    bc[...], _unused = cos_sin(128 * row_e * (t + 4 * lane_e) - 256 * (ro - ri))

    def twice(ref, n):
        w = ref[n, block].astype(F32)
        return jnp.concatenate([w, w], axis=1)

    w0, w1 = twice(second_w, 0), twice(second_w, 1)
    zero = jnp.zeros_like(w0)
    for half in range(2):
        def own(v):
            return (jnp.where(low, v, zero) if half == 0 else jnp.where(low, zero, v)).astype(BF16)

        re, im = slice(64 * half, 64 * half + 64), slice(128 + 64 * half, 192 + 64 * half)
        second_ref[re, :128], second_ref[re, 128:] = own(w0), own(w1)
        second_ref[im, :128], second_ref[im, 128:] = own(-w1), own(w0)

    w0, w1 = twice(first_w, 0), twice(first_w, 1)
    eye = jnp.where(iota((64, 128), 0) == (iota((64, 128), 1) & 63), 1.0, 0.0)
    for n in range(16):
        rows = slice(64 * n, 64 * n + 64)
        for lanes in (slice(0, 128), slice(128, 256)):
            first_ref[rows, lanes] = (
                fc[n : n + 1, lanes] * w0 + fs[n : n + 1, lanes] * w1
            ).astype(BF16)
            last_ref[rows, lanes] = (bc[n : n + 1, lanes] * eye).astype(BF16)


def block_tables(w_first, w_second):
    vmem = pl.BlockSpec(memory_space=pltpu.VMEM)
    return pl.pallas_call(
        blocks_kernel,
        grid=(1,),
        in_specs=[vmem, vmem],
        out_specs=[
            pl.BlockSpec((1024, 256), lambda g: (0, 0)),
            pl.BlockSpec((1024, 256), lambda g: (0, 0)),
            pl.BlockSpec((256, 256), lambda g: (0, 0)),
        ],
        out_shape=[pltpu.HBM((n, 256), BF16) for n in (1024, 1024, 256)],
        scratch_shapes=[pltpu.VMEM((16, 256), F32)] * 3,
        cost_estimate=pl.CostEstimate(flops=2**21, bytes_accessed=2**20, transcendentals=0),
        compiler_params=pltpu.CompilerParams(vmem_limit_bytes=6 * MIB),
        name="block_tables",
    )(w_first, w_second)


def low_half(rows):
    return lax.broadcasted_iota(jnp.int32, (rows, 128), 1) < 64


def swap(v):
    return pltpu.roll(v, 64, 1)


def normed_halves(x, gain_ref):
    ones = jnp.ones((256, 128), BF16)
    mean = dot(x, ones) * (1.0 / 256.0)
    d0, d1 = x[:, :128].astype(F32) - mean, x[:, 128:].astype(F32) - mean
    square = d0 * d0 + d1 * d1
    coarse = square.astype(BF16)
    fine = (square - coarse.astype(F32)).astype(BF16)
    var = dot(jnp.concatenate([coarse, fine], axis=1), ones) * (1.0 / 256.0)
    scale = lax.rsqrt(var + 1e-05)
    return d0 * scale * gain_ref[:, :128], d1 * scale * gain_ref[:, 128:]


def norm_kernel(x_any, gain_ref, out_any, x_all, packed, in_sems, out_sems):
    low = low_half(64)
    fetches, sends = [], []
    for n in range(2):
        rows = slice(16 * n, 16 * n + 16)
        fetches.append(pltpu.make_async_copy(x_any.at[rows], x_all.at[rows], in_sems.at[n]))
        fetches[-1].start()
    for n in range(2):
        fetches[n].wait()
        halves = normed_halves(x_all[16 * n : 16 * n + 16].reshape(1024, 256), gain_ref)
        for g in range(2):
            first = 4 * (2 * n + g)
            for t in range(4):
                lanes = slice(128 * t, 128 * t + 128)
                for m in range(2):
                    a = halves[m][512 * g + 64 * t : 512 * g + 64 * t + 64]
                    b = halves[m][512 * g + 64 * t + 256 : 512 * g + 64 * t + 320]
                    packed[first + 2 * m, :, lanes] = jnp.where(low, a, swap(b)).astype(BF16)
                    packed[first + 2 * m + 1, :, lanes] = jnp.where(low, swap(a), b).astype(BF16)
        parts = slice(8 * n, 8 * n + 8)
        sends.append(pltpu.make_async_copy(packed.at[parts], out_any.at[parts], out_sems.at[n]))
        sends[-1].start()
    for send in sends:
        send.wait()


def home_norm_kernel(x_ref, gain_ref, out_ref):
    for m, half in enumerate(normed_halves(x_ref[...].reshape(512, 256), gain_ref)):
        out_ref[:, :, 128 * m : 128 * m + 128] = half.astype(BF16).reshape(8, 64, 128)


def home_norm(patches, gain):
    block = pl.BlockSpec((8, 64, 256), lambda g: (g, 0, 0))
    return pl.pallas_call(
        home_norm_kernel,
        grid=(4,),
        in_specs=[block, pl.BlockSpec((1, 256), lambda g: (0, 0))],
        out_specs=block,
        out_shape=pltpu.HBM((32, 64, 256), BF16),
        cost_estimate=pl.CostEstimate(flops=2**24, bytes_accessed=2**21, transcendentals=0),
        compiler_params=pltpu.CompilerParams(vmem_limit_bytes=12 * MIB),
        name="home_norm",
    )(remaining(patches), remaining(gain.reshape(1, 256)))


def norm_and_pack(patches, gain):
    return pl.pallas_call(
        norm_kernel,
        in_specs=[pl.BlockSpec(memory_space=pltpu.HBM), pl.BlockSpec(memory_space=pltpu.VMEM)],
        out_specs=pl.BlockSpec(memory_space=pltpu.HBM),
        out_shape=pltpu.HBM((16, 64, 512), BF16),
        scratch_shapes=[
            pltpu.VMEM((32, 64, 256), BF16),
            pltpu.VMEM((16, 64, 512), BF16),
            pltpu.SemaphoreType.DMA((2,)),
            pltpu.SemaphoreType.DMA((2,)),
        ],
        compiler_params=pltpu.CompilerParams(vmem_limit_bytes=16 * MIB),
        name="norm_pack",
    )(remaining(patches), remaining(gain.reshape(1, 256)))


def final_kernel(base_ref, home_ref, out_ref):
    low = low_half(64)
    first, row = 4 * pl.program_id(0), 8 * pl.program_id(0)
    for t in range(4):
        lanes = slice(128 * t, 128 * t + 128)
        for m in range(2):
            u = home_ref[first + 2 * m, :, lanes].astype(F32)
            v = home_ref[first + 2 * m + 1, :, lanes].astype(F32)
            chans = slice(128 * m, 128 * m + 128)
            even, odd = jnp.where(low, u, swap(v)), jnp.where(low, swap(u), v)
            out_ref[t, :, chans] = (base_ref[row + t, :, chans] + even).astype(BF16)
            out_ref[t + 4, :, chans] = (base_ref[row + t + 4, :, chans] + odd).astype(BF16)


def unpack_and_add(base, home):
    return pl.pallas_call(
        final_kernel,
        grid=(4,),
        in_specs=[pl.BlockSpec(memory_space=pltpu.VMEM)] * 2,
        out_specs=pl.BlockSpec((8, 64, 256), lambda g: (g, 0, 0)),
        out_shape=jax.ShapeDtypeStruct((32, 64, 256), BF16),
        compiler_params=pltpu.CompilerParams(vmem_limit_bytes=8 * MIB),
        name="unpack_add",
    )(resident(base), resident(home))


def dot(a, b):
    return jnp.dot(a, b, preferred_element_type=F32)


def resident(v):
    return pltpu.with_memory_space_constraint(v, pltpu.VMEM)


def remaining(v):
    return pltpu.with_memory_space_constraint(v, pltpu.HBM)


def stream_dot(table, operand, held, out, sems):
    copies = []
    for m in range(4):
        rows = slice(256 * m, 256 * m + 256)
        held[rows, :] = dot(table[rows, :], operand[...]).astype(BF16)
        copies.append(pltpu.make_async_copy(held.at[rows, :], out.at[rows, :], sems.at[m]))
        copies[-1].start()
    for copy in copies:
        copy.wait()


def columns_kernel(table_ref, x_ref, out_any, held, sems):
    stream_dot(table_ref, x_ref, held, out_any, sems)


def columns(table, x):
    return pl.pallas_call(
        columns_kernel,
        in_specs=[pl.BlockSpec(memory_space=pltpu.VMEM)] * 2,
        out_specs=pl.BlockSpec(memory_space=pltpu.HBM),
        out_shape=pltpu.HBM((1024, 512), BF16),
        scratch_shapes=[pltpu.VMEM((1024, 512), BF16), pltpu.SemaphoreType.DMA((4,))],
        cost_estimate=pl.CostEstimate(flops=2**30, bytes_accessed=2**21, transcendentals=0),
        compiler_params=pltpu.CompilerParams(vmem_limit_bytes=12 * MIB),
        name="along_columns",
    )(resident(table), resident(x))


def stencil_kernel(
    x_ref, normed_ref, top_ref, bottom_ref, left_ref, right_ref, taps_ref, out_ref,
    rows, side, left_sum, right_sum,
):
    def tap(i, j):
        return taps_ref[3 * i + j : 3 * i + j + 1, :]

    @pl.when(pl.program_id(0) == 0)
    def _():
        rows[0], rows[33] = top_ref[...], bottom_ref[...]
        rows[1:33] = normed_ref[...]
        for rim_ref, sum_ref, j in ((left_ref, left_sum, 0), (right_ref, right_sum, 2)):
            side[...] = rim_ref[...].astype(F32)
            sum_ref[...] = side[0:32] * tap(0, j) + side[1:33] * tap(1, j) + side[2:34] * tap(2, j)

    column = iota((64, 256), 0)

    def step(r, carry):
        h = 8 * pl.program_id(0) + r
        around = [rows[h + i].astype(F32) for i in range(3)]

        def part(j):
            return around[0] * tap(0, j) + around[1] * tap(1, j) + around[2] * tap(2, j)

        left = jnp.where(column == 0, left_sum[pl.ds(h, 1), :], pltpu.roll(part(0), 1, 0))
        right = jnp.where(column == 63, right_sum[pl.ds(h, 1), :], pltpu.roll(part(2), 63, 0))
        out_ref[h] = x_ref[r].astype(F32) + (left + part(1) + right)
        return carry

    lax.fori_loop(0, 8, step, 0)


def stencil(x, normed, top, bottom, left, right, taps):
    block = pl.BlockSpec((8, 64, 256), lambda g: (g, 0, 0))
    row = pl.BlockSpec((64, 256), lambda g: (0, 0))
    side = pl.BlockSpec((34, 256), lambda g: (0, 0))
    return pl.pallas_call(
        stencil_kernel,
        grid=(4,),
        in_specs=[
            block,
            pl.BlockSpec((32, 64, 256), lambda g: (0, 0, 0)),
            row, row, side, side,
            pl.BlockSpec((9, 256), lambda g: (0, 0)),
        ],
        out_specs=pl.BlockSpec(memory_space=pltpu.VMEM),
        out_shape=pltpu.VMEM((32, 64, 256), F32),
        scratch_shapes=[
            pltpu.VMEM((34, 64, 256), BF16),
            pltpu.VMEM((34, 256), F32),
            pltpu.VMEM((32, 256), F32),
            pltpu.VMEM((32, 256), F32),
        ],
        cost_estimate=pl.CostEstimate(flops=2**24, bytes_accessed=2**22, transcendentals=0),
        compiler_params=pltpu.CompilerParams(vmem_limit_bytes=12 * MIB),
        name="stencil",
    )(*[remaining(v) for v in (x, normed, top, bottom, left, right, taps)])


def butterfly(x, sign):
    re, im = [v[:, :128] for v in x], [v[:, 128:] for v in x]

    def pair(v):
        return v[0] + v[2], v[0] - v[2], v[1] + v[3], v[1] - v[3]

    (er, dr, fr, gr), (ei, di, fi, gi) = pair(re), pair(im)
    plus, minus = (dr - gi, di + gr), (dr + gi, di - gr)
    if sign < 0:
        plus, minus = minus, plus
    return (er + fr, ei + fi), plus, (er - fr, ei - fi), minus


def beside(pair):
    return jnp.concatenate(pair, axis=1)


def middle_kernel(
    z, fwd, cos_any, sin_any, first_any, second_any, last_any, inv_any, out_any,
    cos_ref, sin_ref, first, second, last, inv, held, done, sems, fetch_sems,
):
    fetches = []
    for n, (src, dst) in enumerate(
        (
            (cos_any, cos_ref),
            (sin_any, sin_ref),
            (first_any, first),
            (second_any, second),
            (last_any, last),
            (inv_any, inv),
        )
    ):
        fetches.append(pltpu.make_async_copy(src, dst, fetch_sems.at[n]))
        fetches[-1].start()
    rows = 512 // CHUNKS
    groups = 8 // CHUNKS
    shape = (groups, 4, 16, 128)
    for m in range(CHUNKS):
        u = dot(fwd[2 * rows * m : 2 * rows * (m + 1), :], z[...])
        if m == 0:
            for fetch in fetches[:4]:
                fetch.wait()

        def twiddles(t):
            part = (slice(16 * groups * m, 16 * groups * (m + 1)), slice(128 * t, 128 * t + 128))
            return [ref[part].reshape(groups, 1, 16, 128) for ref in (cos_ref, sin_ref)]

        parts = []
        for t in range(4):
            ur = u[:rows, 128 * t : 128 * t + 128].reshape(shape)
            ui = u[rows:, 128 * t : 128 * t + 128].reshape(shape)
            c, s = twiddles(t)
            vr, vi = (ur * c + ui * s).reshape(rows, 128), (ui * c - ur * s).reshape(rows, 128)
            parts.append(dot(beside((vr.astype(BF16), vi.astype(BF16))), first[256 * t : 256 * t + 256, :]))
        kept = []
        for part in butterfly(parts, -1):
            v = dot(jnp.tanh(beside(part)).astype(BF16), second[...])
            kept.append(jnp.where(v > 0.25, v - 0.25, jnp.where(v < -0.25, v + 0.25, 0.0 * v)))
        if m == 0:
            fetches[4].wait()
        for t, part in enumerate(butterfly(kept, 1)):
            y = dot(beside(part).astype(BF16), last[256 * t : 256 * t + 256, :])
            yr, yi = y[:, :128].reshape(shape), y[:, 128:].reshape(shape)
            c, s = twiddles(t)
            lanes = slice(128 * t, 128 * t + 128)
            held[2 * rows * m : 2 * rows * m + rows, lanes] = (
                (yr * c - yi * s).astype(BF16).reshape(rows, 128)
            )
            held[2 * rows * m + rows : 2 * rows * (m + 1), lanes] = (
                (yi * c + yr * s).astype(BF16).reshape(rows, 128)
            )
    fetches[5].wait()
    stream_dot(inv, held, done, out_any, sems)


def middle(z, fwd, cos, sin, first, second, last, inv):
    vmem, hbm = pl.BlockSpec(memory_space=pltpu.VMEM), pl.BlockSpec(memory_space=pltpu.HBM)
    return pl.pallas_call(
        middle_kernel,
        in_specs=[vmem] * 2 + [hbm] * 6,
        out_specs=hbm,
        out_shape=pltpu.HBM((1024, 512), BF16),
        scratch_shapes=[
            pltpu.VMEM((128, 512), F32),
            pltpu.VMEM((128, 512), F32),
            pltpu.VMEM((1024, 256), BF16),
            pltpu.VMEM((256, 256), BF16),
            pltpu.VMEM((1024, 256), BF16),
            pltpu.VMEM((1024, 1024), BF16),
            pltpu.VMEM((1024, 512), BF16),
            pltpu.VMEM((1024, 512), BF16),
            pltpu.SemaphoreType.DMA((4,)),
            pltpu.SemaphoreType.DMA((6,)),
        ],
        cost_estimate=pl.CostEstimate(flops=3 * 2**30, bytes_accessed=2**21, transcendentals=2**19),
        compiler_params=pltpu.CompilerParams(vmem_limit_bytes=24 * MIB),
        name="filter_rows",
    )(
        resident(z), resident(fwd), *[remaining(v) for v in (cos, sin, first, second, last, inv)]
    )


def local(patches, norm_gain, w_first, w_second, depth_kernel):
    packed = norm_and_pack(patches, norm_gain)
    lines = lax.all_to_all(packed, ("yl", "x"), 0, 0, tiled=True).reshape(1024, 512)

    fwd_w = table(pltpu.VMEM, forward_columns_phases)
    inv_w = table(pltpu.VMEM, backward_columns_phases)
    inv_h = table(pltpu.HBM, backward_rows_phases)
    first, last, second = block_tables(w_first, w_second)
    fwd_h, cos, sin = table(pltpu.VMEM, forward_rows_phases, True, (second, inv_h))

    def neighbours(first, last, axis):
        n = lax.axis_size(axis)
        before = lax.ppermute(last, axis, [(i, (i + 1) % n) for i in range(n)])
        after = lax.ppermute(first, axis, [((i + 1) % n, i) for i in range(n)])
        return before, after

    normed = home_norm(patches, norm_gain)
    lines, normed = lax.optimization_barrier((lines, normed))

    freqs = columns(fwd_w, lines)
    whole = lax.all_to_all(freqs.reshape(128, 8, 512), ("row", "yl"), 0, 0, tiled=True)
    top, bottom = neighbours(normed[0], normed[31], "row")
    whole, top, bottom = lax.optimization_barrier((whole, top, bottom))

    filtered = middle(whole.reshape(1024, 512), fwd_h, cos, sin, first, second, last, inv_h)
    filtered, top, bottom, normed = lax.optimization_barrier((filtered, top, bottom, normed))
    back = lax.all_to_all(filtered.reshape(128, 8, 512), ("row", "yl"), 0, 0, tiled=True)
    sides = [
        jnp.concatenate([top[w : w + 1], normed[:, w], bottom[w : w + 1]], axis=0) for w in (0, 63)
    ]
    left, right = neighbours(sides[0], sides[1], ("yl", "x"))
    back, left, right = lax.optimization_barrier((back, left, right))

    spectral = columns(inv_w, back.reshape(1024, 512))
    spectral, left, right = lax.optimization_barrier((spectral, left, right))
    home = lax.all_to_all(spectral.reshape(16, 64, 512), ("yl", "x"), 0, 0, tiled=True)
    base = stencil(patches, normed, top, bottom, left, right, depth_kernel.reshape(9, 256))
    return unpack_and_add(base, home)


def solution(mesh):
    fine = Mesh(np.asarray(mesh.devices).reshape(32, 4, 4), ("row", "yl", "x"))
    return jax.shard_map(
        local,
        mesh=fine,
        in_specs=(P("row", ("yl", "x"), None), P(), P(), P(), P()),
        out_specs=P("row", ("yl", "x"), None),
        check_vma=False,
    )
```

```python
import functools
import math

import jax
import jax.numpy as jnp
import numpy as np
from jax import lax
from jax.experimental import pallas as pl
from jax.experimental.pallas import tpu as pltpu
from jax.sharding import Mesh
from jax.sharding import PartitionSpec as P

TURN = 1024
CHUNKS = 2
MIB = 1024 * 1024
F32 = jnp.float32
BF16 = jnp.bfloat16


def iota(shape, dim):
    return lax.broadcasted_iota(jnp.int32, shape, dim)


def digit(idx, shift, bits):
    return (idx >> shift) & ((1 << bits) - 1)


def cos_sin(idx):
    idx = idx & (TURN - 1)
    quarter = (idx + TURN // 8) >> 8
    x = (idx - (quarter << 8)).astype(F32) * (2.0 * math.pi / TURN)
    y = x * x
    s = x * (1.0 + y * (-1.0 / 6 + y * (1.0 / 120 + y * (-1.0 / 5040 + y * (1.0 / 362880)))))
    c = 1.0 + y * (-1.0 / 2 + y * (1.0 / 24 + y * (-1.0 / 720 + y * (1.0 / 40320))))
    odd = (quarter & 1) == 1
    cos, sin = jnp.where(odd, s, c), jnp.where(odd, c, s)
    turned = (quarter + 1) & 3
    cos = jnp.where(turned >= 2, -cos, cos)
    sin = jnp.where((quarter & 3) >= 2, -sin, sin)
    return cos, sin


SCALE = 1.0 / 32.0


def forward_columns_phases():
    a, b = iota((16, 1024), 0), iota((64, 1024), 0)
    w = iota((64, 1024), 1)
    k = 4 * digit(b, 3, 3) + digit(b, 0, 2)
    return 32 * a * w[:16], k * w + 256 * digit(b, 2, 1), SCALE


def backward_columns_phases():
    a, b, lane = iota((16, 1024), 0), iota((64, 1024), 0), iota((64, 1024), 1)
    k = 4 * (lane >> 3) + digit(lane, 0, 2)
    weight = jnp.where(k == 0, SCALE, 2.0 * SCALE)
    return 64 * a * k[:16], b * k + 256 * digit(lane, 2, 1), weight


def forward_rows_phases():
    a, b, lane = iota((16, 1024), 0), iota((64, 1024), 0), iota((64, 1024), 1)
    qh = 4 * digit(a, 3, 1) + digit(a, 0, 2)
    p, ri = lane >> 3, digit(lane, 2, 1)
    ia = 128 * qh * p[:16] + 256 * (digit(a, 2, 1) - ri[:16])
    weight = jnp.where(digit(b, 4, 2) == digit(lane, 0, 2), SCALE, 0.0)
    return ia, 8 * digit(b, 0, 4) * p, weight


def backward_rows_phases():
    a, b, lane = iota((16, 1024), 0), iota((64, 1024), 0), iota((64, 1024), 1)
    q0 = 16 * (4 * digit(lane, 9, 1) + digit(lane, 6, 2)) + digit(lane, 0, 4)
    ro = digit(lane, 8, 1)
    weight = jnp.where(digit(b, 0, 2) == digit(lane, 4, 2), SCALE, 0.0)
    return 64 * a * q0[:16], 8 * digit(b, 3, 3) * q0 + 256 * (ro - digit(b, 2, 1)), weight


def table_kernel(phases, with_twiddles, stay, waited, *refs):
    refs = refs[waited:]
    out_ref, (ec, es, fc, fs) = refs[0], refs[-4:]
    steps = 16 if stay else 4

    @pl.when(pl.program_id(0) == 0)
    def _():
        ia, ib, weight = phases()
        ec[...], es[...] = cos_sin(ia)
        c, s = cos_sin(ib)
        fc[...], fs[...] = c * weight, s * weight
        if with_twiddles:
            lane = iota((128, 512), 1)
            angle = iota((128, 512), 0) * ((lane >> 7) + 4 * digit(lane, 6, 1))
            refs[1][...], refs[2][...] = cos_sin(angle)

    first = 0 if stay else steps * pl.program_id(0)

    def step(a, carry):
        row = pl.ds(first + a, 1)
        out_ref[pl.ds(pl.multiple_of(64 * a, 64), 64), :] = (
            ec[row, :] * fc[...] - es[row, :] * fs[...]
        ).astype(BF16)
        return carry

    lax.fori_loop(0, steps, step, 0)


def table(space, phases, with_twiddles=False, after=()):
    stay = space == pltpu.VMEM
    whole = pl.BlockSpec(memory_space=pltpu.VMEM)
    twiddle_spec = pl.BlockSpec((128, 512), lambda g: (0, 0))
    out = pl.pallas_call(
        functools.partial(table_kernel, phases, with_twiddles, stay, len(after)),
        grid=(1,) if stay else (4,),
        in_specs=[pl.BlockSpec(memory_space=pltpu.HBM)] * len(after),
        out_specs=[whole if stay else pl.BlockSpec((256, 1024), lambda g: (g, 0))]
        + [twiddle_spec] * (2 * with_twiddles),
        out_shape=[space((1024, 1024), BF16)] + [pltpu.HBM((128, 512), F32)] * (2 * with_twiddles),
        scratch_shapes=[pltpu.VMEM((n, 1024), F32) for n in (16, 16, 64, 64)],
        cost_estimate=pl.CostEstimate(flops=2**23, bytes_accessed=2**21, transcendentals=0),
        compiler_params=pltpu.CompilerParams(vmem_limit_bytes=6 * MIB),
        name=phases.__name__,
    )(*[remaining(v) for v in after])
    return out if with_twiddles else out[0]


def blocks_kernel(first_w, second_w, first_ref, last_ref, second_ref, fc, fs, bc):
    block = lax.axis_index("x")
    low = low_half(64)
    a, lane = iota((16, 256), 0), iota((16, 256), 1)
    t, ri, row_e = a >> 2, digit(a, 1, 1), a & 1
    ro, lane_e = lane >> 7, digit(lane, 6, 1)
    fc[...], fs[...] = cos_sin(128 * lane_e * (t + 4 * row_e) + 256 * (ro - ri))
    bc[...], _unused = cos_sin(128 * row_e * (t + 4 * lane_e) - 256 * (ro - ri))

    def twice(ref, n):
        w = ref[n, block].astype(F32)
        return jnp.concatenate([w, w], axis=1)

    w0, w1 = twice(second_w, 0), twice(second_w, 1)
    zero = jnp.zeros_like(w0)
    for half in range(2):
        def own(v):
            return (jnp.where(low, v, zero) if half == 0 else jnp.where(low, zero, v)).astype(BF16)

        re, im = slice(64 * half, 64 * half + 64), slice(128 + 64 * half, 192 + 64 * half)
        second_ref[re, :128], second_ref[re, 128:] = own(w0), own(w1)
        second_ref[im, :128], second_ref[im, 128:] = own(-w1), own(w0)

    w0, w1 = twice(first_w, 0), twice(first_w, 1)
    eye = jnp.where(iota((64, 128), 0) == (iota((64, 128), 1) & 63), 1.0, 0.0)
    for n in range(16):
        rows = slice(64 * n, 64 * n + 64)
        for lanes in (slice(0, 128), slice(128, 256)):
            first_ref[rows, lanes] = (
                fc[n : n + 1, lanes] * w0 + fs[n : n + 1, lanes] * w1
            ).astype(BF16)
            last_ref[rows, lanes] = (bc[n : n + 1, lanes] * eye).astype(BF16)


def block_tables(w_first, w_second):
    vmem = pl.BlockSpec(memory_space=pltpu.VMEM)
    return pl.pallas_call(
        blocks_kernel,
        grid=(1,),
        in_specs=[vmem, vmem],
        out_specs=[
            pl.BlockSpec((1024, 256), lambda g: (0, 0)),
            pl.BlockSpec((1024, 256), lambda g: (0, 0)),
            pl.BlockSpec((256, 256), lambda g: (0, 0)),
        ],
        out_shape=[pltpu.HBM((n, 256), BF16) for n in (1024, 1024, 256)],
        scratch_shapes=[pltpu.VMEM((16, 256), F32)] * 3,
        cost_estimate=pl.CostEstimate(flops=2**21, bytes_accessed=2**20, transcendentals=0),
        compiler_params=pltpu.CompilerParams(vmem_limit_bytes=6 * MIB),
        name="block_tables",
    )(w_first, w_second)


def low_half(rows):
    return lax.broadcasted_iota(jnp.int32, (rows, 128), 1) < 64


def swap(v):
    return pltpu.roll(v, 64, 1)


def normed_halves(x, gain_ref):
    ones = jnp.ones((256, 128), BF16)
    mean = dot(x, ones) * (1.0 / 256.0)
    d0, d1 = x[:, :128].astype(F32) - mean, x[:, 128:].astype(F32) - mean
    square = d0 * d0 + d1 * d1
    coarse = square.astype(BF16)
    fine = (square - coarse.astype(F32)).astype(BF16)
    var = dot(jnp.concatenate([coarse, fine], axis=1), ones) * (1.0 / 256.0)
    scale = lax.rsqrt(var + 1e-05)
    return d0 * scale * gain_ref[:, :128], d1 * scale * gain_ref[:, 128:]


def norm_kernel(x_any, gain_ref, out_any, x_all, packed, in_sems, out_sems):
    low = low_half(64)
    fetches, sends = [], []
    for n in range(2):
        rows = slice(16 * n, 16 * n + 16)
        fetches.append(pltpu.make_async_copy(x_any.at[rows], x_all.at[rows], in_sems.at[n]))
        fetches[-1].start()
    for n in range(2):
        fetches[n].wait()
        halves = normed_halves(x_all[16 * n : 16 * n + 16].reshape(1024, 256), gain_ref)
        for g in range(2):
            first = 4 * (2 * n + g)
            for t in range(4):
                lanes = slice(128 * t, 128 * t + 128)
                for m in range(2):
                    a = halves[m][512 * g + 64 * t : 512 * g + 64 * t + 64]
                    b = halves[m][512 * g + 64 * t + 256 : 512 * g + 64 * t + 320]
                    packed[first + 2 * m, :, lanes] = jnp.where(low, a, swap(b)).astype(BF16)
                    packed[first + 2 * m + 1, :, lanes] = jnp.where(low, swap(a), b).astype(BF16)
        parts = slice(8 * n, 8 * n + 8)
        sends.append(pltpu.make_async_copy(packed.at[parts], out_any.at[parts], out_sems.at[n]))
        sends[-1].start()
    for send in sends:
        send.wait()


def home_norm_kernel(x_ref, gain_ref, out_ref):
    for m, half in enumerate(normed_halves(x_ref[...].reshape(512, 256), gain_ref)):
        out_ref[:, :, 128 * m : 128 * m + 128] = half.astype(BF16).reshape(8, 64, 128)


def home_norm(patches, gain):
    block = pl.BlockSpec((8, 64, 256), lambda g: (g, 0, 0))
    return pl.pallas_call(
        home_norm_kernel,
        grid=(4,),
        in_specs=[block, pl.BlockSpec((1, 256), lambda g: (0, 0))],
        out_specs=block,
        out_shape=pltpu.HBM((32, 64, 256), BF16),
        cost_estimate=pl.CostEstimate(flops=2**24, bytes_accessed=2**21, transcendentals=0),
        compiler_params=pltpu.CompilerParams(vmem_limit_bytes=12 * MIB),
        name="home_norm",
    )(remaining(patches), remaining(gain.reshape(1, 256)))


def norm_and_pack(patches, gain):
    return pl.pallas_call(
        norm_kernel,
        in_specs=[pl.BlockSpec(memory_space=pltpu.HBM), pl.BlockSpec(memory_space=pltpu.VMEM)],
        out_specs=pl.BlockSpec(memory_space=pltpu.HBM),
        out_shape=pltpu.HBM((16, 64, 512), BF16),
        scratch_shapes=[
            pltpu.VMEM((32, 64, 256), BF16),
            pltpu.VMEM((16, 64, 512), BF16),
            pltpu.SemaphoreType.DMA((2,)),
            pltpu.SemaphoreType.DMA((2,)),
        ],
        compiler_params=pltpu.CompilerParams(vmem_limit_bytes=16 * MIB),
        name="norm_pack",
    )(remaining(patches), remaining(gain.reshape(1, 256)))


def final_kernel(base_ref, home_ref, out_ref):
    low = low_half(64)
    first, row = 4 * pl.program_id(0), 8 * pl.program_id(0)
    for t in range(4):
        lanes = slice(128 * t, 128 * t + 128)
        for m in range(2):
            u = home_ref[first + 2 * m, :, lanes].astype(F32)
            v = home_ref[first + 2 * m + 1, :, lanes].astype(F32)
            chans = slice(128 * m, 128 * m + 128)
            even, odd = jnp.where(low, u, swap(v)), jnp.where(low, swap(u), v)
            out_ref[t, :, chans] = (base_ref[row + t, :, chans] + even).astype(BF16)
            out_ref[t + 4, :, chans] = (base_ref[row + t + 4, :, chans] + odd).astype(BF16)


def unpack_and_add(base, home):
    return pl.pallas_call(
        final_kernel,
        grid=(4,),
        in_specs=[pl.BlockSpec(memory_space=pltpu.VMEM)] * 2,
        out_specs=pl.BlockSpec((8, 64, 256), lambda g: (g, 0, 0)),
        out_shape=jax.ShapeDtypeStruct((32, 64, 256), BF16),
        compiler_params=pltpu.CompilerParams(vmem_limit_bytes=8 * MIB),
        name="unpack_add",
    )(resident(base), resident(home))


def dot(a, b):
    return jnp.dot(a, b, preferred_element_type=F32)


def resident(v):
    return pltpu.with_memory_space_constraint(v, pltpu.VMEM)


def remaining(v):
    return pltpu.with_memory_space_constraint(v, pltpu.HBM)


def stream_dot(table, operand, held, out, sems):
    copies = []
    for m in range(4):
        rows = slice(256 * m, 256 * m + 256)
        held[rows, :] = dot(table[rows, :], operand[...]).astype(BF16)
        copies.append(pltpu.make_async_copy(held.at[rows, :], out.at[rows, :], sems.at[m]))
        copies[-1].start()
    for copy in copies:
        copy.wait()


def columns_kernel(table_ref, x_ref, out_any, held, sems):
    stream_dot(table_ref, x_ref, held, out_any, sems)


def columns(table, x):
    return pl.pallas_call(
        columns_kernel,
        in_specs=[pl.BlockSpec(memory_space=pltpu.VMEM)] * 2,
        out_specs=pl.BlockSpec(memory_space=pltpu.HBM),
        out_shape=pltpu.HBM((1024, 512), BF16),
        scratch_shapes=[pltpu.VMEM((1024, 512), BF16), pltpu.SemaphoreType.DMA((4,))],
        cost_estimate=pl.CostEstimate(flops=2**30, bytes_accessed=2**21, transcendentals=0),
        compiler_params=pltpu.CompilerParams(vmem_limit_bytes=12 * MIB),
        name="along_columns",
    )(resident(table), resident(x))


def stencil_kernel(
    x_ref, normed_ref, top_ref, bottom_ref, left_ref, right_ref, taps_ref, out_ref,
    rows, side, left_sum, right_sum,
):
    def tap(i, j):
        return taps_ref[3 * i + j : 3 * i + j + 1, :]

    @pl.when(pl.program_id(0) == 0)
    def _():
        rows[0], rows[33] = top_ref[:64, :], bottom_ref[:64, :]
        rows[1:33] = normed_ref[...]
        above, below = top_ref[64:66, :].astype(F32), bottom_ref[64:66, :].astype(F32)
        for rim_ref, sum_ref, j in ((left_ref, left_sum, 0), (right_ref, right_sum, 2)):
            corner = slice(j // 2, j // 2 + 1)
            side[0:1, :], side[33:34, :] = above[corner], below[corner]
            side[1:33, :] = rim_ref[...].astype(F32)
            sum_ref[...] = side[0:32] * tap(0, j) + side[1:33] * tap(1, j) + side[2:34] * tap(2, j)

    column = iota((64, 256), 0)

    def step(r, carry):
        h = 8 * pl.program_id(0) + r
        around = [rows[h + i].astype(F32) for i in range(3)]

        def part(j):
            return around[0] * tap(0, j) + around[1] * tap(1, j) + around[2] * tap(2, j)

        left = jnp.where(column == 0, left_sum[pl.ds(h, 1), :], pltpu.roll(part(0), 1, 0))
        right = jnp.where(column == 63, right_sum[pl.ds(h, 1), :], pltpu.roll(part(2), 63, 0))
        out_ref[h] = x_ref[r].astype(F32) + (left + part(1) + right)
        return carry

    lax.fori_loop(0, 8, step, 0)


def stencil(x, normed, top, bottom, left, right, taps):
    block = pl.BlockSpec((8, 64, 256), lambda g: (g, 0, 0))
    row = pl.BlockSpec((66, 256), lambda g: (0, 0))
    side = pl.BlockSpec((32, 256), lambda g: (0, 0))
    return pl.pallas_call(
        stencil_kernel,
        grid=(4,),
        in_specs=[
            block,
            pl.BlockSpec((32, 64, 256), lambda g: (0, 0, 0)),
            row, row, side, side,
            pl.BlockSpec((9, 256), lambda g: (0, 0)),
        ],
        out_specs=pl.BlockSpec(memory_space=pltpu.VMEM),
        out_shape=pltpu.VMEM((32, 64, 256), F32),
        scratch_shapes=[
            pltpu.VMEM((34, 64, 256), BF16),
            pltpu.VMEM((34, 256), F32),
            pltpu.VMEM((32, 256), F32),
            pltpu.VMEM((32, 256), F32),
        ],
        cost_estimate=pl.CostEstimate(flops=2**24, bytes_accessed=2**22, transcendentals=0),
        compiler_params=pltpu.CompilerParams(vmem_limit_bytes=12 * MIB),
        name="stencil",
    )(*[remaining(v) for v in (x, normed, top, bottom, left, right, taps)])


def butterfly(x, sign):
    re, im = [v[:, :128] for v in x], [v[:, 128:] for v in x]

    def pair(v):
        return v[0] + v[2], v[0] - v[2], v[1] + v[3], v[1] - v[3]

    (er, dr, fr, gr), (ei, di, fi, gi) = pair(re), pair(im)
    plus, minus = (dr - gi, di + gr), (dr + gi, di - gr)
    if sign < 0:
        plus, minus = minus, plus
    return (er + fr, ei + fi), plus, (er - fr, ei - fi), minus


def beside(pair):
    return jnp.concatenate(pair, axis=1)


def middle_kernel(
    z, fwd, cos_any, sin_any, first_any, second_any, last_any, inv_any, out_any,
    cos_ref, sin_ref, first, second, last, inv, held, done, sems, fetch_sems,
):
    fetches = []
    for n, (src, dst) in enumerate(
        (
            (cos_any, cos_ref),
            (sin_any, sin_ref),
            (first_any, first),
            (second_any, second),
            (last_any, last),
            (inv_any, inv),
        )
    ):
        fetches.append(pltpu.make_async_copy(src, dst, fetch_sems.at[n]))
        fetches[-1].start()
    rows = 512 // CHUNKS
    groups = 8 // CHUNKS
    shape = (groups, 4, 16, 128)
    for m in range(CHUNKS):
        u = dot(fwd[2 * rows * m : 2 * rows * (m + 1), :], z[...])
        if m == 0:
            for fetch in fetches[:4]:
                fetch.wait()

        def twiddles(t):
            part = (slice(16 * groups * m, 16 * groups * (m + 1)), slice(128 * t, 128 * t + 128))
            return [ref[part].reshape(groups, 1, 16, 128) for ref in (cos_ref, sin_ref)]

        parts = []
        for t in range(4):
            ur = u[:rows, 128 * t : 128 * t + 128].reshape(shape)
            ui = u[rows:, 128 * t : 128 * t + 128].reshape(shape)
            c, s = twiddles(t)
            vr, vi = (ur * c + ui * s).reshape(rows, 128), (ui * c - ur * s).reshape(rows, 128)
            parts.append(dot(beside((vr.astype(BF16), vi.astype(BF16))), first[256 * t : 256 * t + 256, :]))
        kept = []
        for part in butterfly(parts, -1):
            v = dot(jnp.tanh(beside(part)).astype(BF16), second[...])
            kept.append(jnp.where(v > 0.25, v - 0.25, jnp.where(v < -0.25, v + 0.25, 0.0 * v)))
        if m == 0:
            fetches[4].wait()
        for t, part in enumerate(butterfly(kept, 1)):
            y = dot(beside(part).astype(BF16), last[256 * t : 256 * t + 256, :])
            yr, yi = y[:, :128].reshape(shape), y[:, 128:].reshape(shape)
            c, s = twiddles(t)
            lanes = slice(128 * t, 128 * t + 128)
            held[2 * rows * m : 2 * rows * m + rows, lanes] = (
                (yr * c - yi * s).astype(BF16).reshape(rows, 128)
            )
            held[2 * rows * m + rows : 2 * rows * (m + 1), lanes] = (
                (yi * c + yr * s).astype(BF16).reshape(rows, 128)
            )
    fetches[5].wait()
    stream_dot(inv, held, done, out_any, sems)


def middle(z, fwd, cos, sin, first, second, last, inv):
    vmem, hbm = pl.BlockSpec(memory_space=pltpu.VMEM), pl.BlockSpec(memory_space=pltpu.HBM)
    return pl.pallas_call(
        middle_kernel,
        in_specs=[vmem] * 2 + [hbm] * 6,
        out_specs=hbm,
        out_shape=pltpu.HBM((1024, 512), BF16),
        scratch_shapes=[
            pltpu.VMEM((128, 512), F32),
            pltpu.VMEM((128, 512), F32),
            pltpu.VMEM((1024, 256), BF16),
            pltpu.VMEM((256, 256), BF16),
            pltpu.VMEM((1024, 256), BF16),
            pltpu.VMEM((1024, 1024), BF16),
            pltpu.VMEM((1024, 512), BF16),
            pltpu.VMEM((1024, 512), BF16),
            pltpu.SemaphoreType.DMA((4,)),
            pltpu.SemaphoreType.DMA((6,)),
        ],
        cost_estimate=pl.CostEstimate(flops=3 * 2**30, bytes_accessed=2**21, transcendentals=2**19),
        compiler_params=pltpu.CompilerParams(vmem_limit_bytes=24 * MIB),
        name="filter_rows",
    )(
        resident(z), resident(fwd), *[remaining(v) for v in (cos, sin, first, second, last, inv)]
    )


def local(patches, norm_gain, w_first, w_second, depth_kernel):
    packed = norm_and_pack(patches, norm_gain)
    lines = lax.all_to_all(packed, ("yl", "x"), 0, 0, tiled=True).reshape(1024, 512)

    fwd_w = table(pltpu.VMEM, forward_columns_phases)
    inv_w = table(pltpu.VMEM, backward_columns_phases)
    inv_h = table(pltpu.HBM, backward_rows_phases)
    first, last, second = block_tables(w_first, w_second)
    fwd_h, cos, sin = table(pltpu.VMEM, forward_rows_phases, True, (second, inv_h))

    def neighbours(first, last, axis):
        n = lax.axis_size(axis)
        before = lax.ppermute(last, axis, [(i, (i + 1) % n) for i in range(n)])
        after = lax.ppermute(first, axis, [((i + 1) % n, i) for i in range(n)])
        return before, after

    normed = home_norm(patches, norm_gain)
    lines, normed = lax.optimization_barrier((lines, normed))

    freqs = columns(fwd_w, lines)
    whole = lax.all_to_all(freqs.reshape(128, 8, 512), ("row", "yl"), 0, 0, tiled=True)
    left, right = neighbours(normed[:, 0], normed[:, 63], ("yl", "x"))
    whole, left, right = lax.optimization_barrier((whole, left, right))

    filtered = middle(whole.reshape(1024, 512), fwd_h, cos, sin, first, second, last, inv_h)
    filtered, left, right, normed = lax.optimization_barrier((filtered, left, right, normed))
    back = lax.all_to_all(filtered.reshape(128, 8, 512), ("row", "yl"), 0, 0, tiled=True)
    wide = [jnp.concatenate([normed[h], left[h : h + 1], right[h : h + 1]], axis=0) for h in (0, 31)]
    top, bottom = neighbours(wide[0], wide[1], "row")

    spectral = columns(inv_w, back.reshape(1024, 512))
    spectral, top, bottom = lax.optimization_barrier((spectral, top, bottom))
    home = lax.all_to_all(spectral.reshape(16, 64, 512), ("yl", "x"), 0, 0, tiled=True)
    base = stencil(patches, normed, top, bottom, left, right, depth_kernel.reshape(9, 256))
    return unpack_and_add(base, home)


def solution(mesh):
    fine = Mesh(np.asarray(mesh.devices).reshape(32, 4, 4), ("row", "yl", "x"))
    return jax.shard_map(
        local,
        mesh=fine,
        in_specs=(P("row", ("yl", "x"), None), P(), P(), P(), P()),
        out_specs=P("row", ("yl", "x"), None),
        check_vma=False,
    )
```

```python
import functools
import math

import jax
import jax.numpy as jnp
import numpy as np
from jax import lax
from jax.experimental import pallas as pl
from jax.experimental.pallas import tpu as pltpu
from jax.sharding import Mesh
from jax.sharding import PartitionSpec as P

TURN = 1024
CHUNKS = 2
MIB = 1024 * 1024
F32 = jnp.float32
BF16 = jnp.bfloat16


def iota(shape, dim):
    return lax.broadcasted_iota(jnp.int32, shape, dim)


def digit(idx, shift, bits):
    return (idx >> shift) & ((1 << bits) - 1)


def cos_sin(idx):
    idx = idx & (TURN - 1)
    quarter = (idx + TURN // 8) >> 8
    x = (idx - (quarter << 8)).astype(F32) * (2.0 * math.pi / TURN)
    y = x * x
    s = x * (1.0 + y * (-1.0 / 6 + y * (1.0 / 120 + y * (-1.0 / 5040 + y * (1.0 / 362880)))))
    c = 1.0 + y * (-1.0 / 2 + y * (1.0 / 24 + y * (-1.0 / 720 + y * (1.0 / 40320))))
    odd = (quarter & 1) == 1
    cos, sin = jnp.where(odd, s, c), jnp.where(odd, c, s)
    turned = (quarter + 1) & 3
    cos = jnp.where(turned >= 2, -cos, cos)
    sin = jnp.where((quarter & 3) >= 2, -sin, sin)
    return cos, sin


SCALE = 1.0 / 32.0


def forward_columns_phases():
    a, b = iota((16, 1024), 0), iota((64, 1024), 0)
    w = iota((64, 1024), 1)
    k = 4 * digit(b, 3, 3) + digit(b, 0, 2)
    return 32 * a * w[:16], k * w + 256 * digit(b, 2, 1), SCALE


def backward_columns_phases():
    a, b, lane = iota((16, 1024), 0), iota((64, 1024), 0), iota((64, 1024), 1)
    k = 4 * (lane >> 3) + digit(lane, 0, 2)
    weight = jnp.where(k == 0, SCALE, 2.0 * SCALE)
    return 64 * a * k[:16], b * k + 256 * digit(lane, 2, 1), weight


def forward_rows_phases():
    a, b, lane = iota((16, 1024), 0), iota((64, 1024), 0), iota((64, 1024), 1)
    qh = 4 * digit(a, 3, 1) + digit(a, 0, 2)
    p, ri = lane >> 3, digit(lane, 2, 1)
    ia = 128 * qh * p[:16] + 256 * (digit(a, 2, 1) - ri[:16])
    weight = jnp.where(digit(b, 4, 2) == digit(lane, 0, 2), SCALE, 0.0)
    return ia, 8 * digit(b, 0, 4) * p, weight


def backward_rows_phases():
    a, b, lane = iota((16, 1024), 0), iota((64, 1024), 0), iota((64, 1024), 1)
    q0 = 16 * (4 * digit(lane, 9, 1) + digit(lane, 6, 2)) + digit(lane, 0, 4)
    ro = digit(lane, 8, 1)
    weight = jnp.where(digit(b, 0, 2) == digit(lane, 4, 2), SCALE, 0.0)
    return 64 * a * q0[:16], 8 * digit(b, 3, 3) * q0 + 256 * (ro - digit(b, 2, 1)), weight


def table_kernel(phases, with_twiddles, stay, waited, *refs):
    refs = refs[waited:]
    out_ref, (ec, es, fc, fs) = refs[0], refs[-4:]
    steps = 16 if stay else 4

    @pl.when(pl.program_id(0) == 0)
    def _():
        ia, ib, weight = phases()
        ec[...], es[...] = cos_sin(ia)
        c, s = cos_sin(ib)
        fc[...], fs[...] = c * weight, s * weight
        if with_twiddles:
            lane = iota((128, 512), 1)
            angle = iota((128, 512), 0) * ((lane >> 7) + 4 * digit(lane, 6, 1))
            refs[1][...], refs[2][...] = cos_sin(angle)

    first = 0 if stay else steps * pl.program_id(0)

    def step(a, carry):
        row = pl.ds(first + a, 1)
        out_ref[pl.ds(pl.multiple_of(64 * a, 64), 64), :] = (
            ec[row, :] * fc[...] - es[row, :] * fs[...]
        ).astype(BF16)
        return carry

    lax.fori_loop(0, steps, step, 0)


def table(space, phases, with_twiddles=False, after=()):
    stay = space == pltpu.VMEM
    whole = pl.BlockSpec(memory_space=pltpu.VMEM)
    twiddle_spec = pl.BlockSpec((128, 512), lambda g: (0, 0))
    out = pl.pallas_call(
        functools.partial(table_kernel, phases, with_twiddles, stay, len(after)),
        grid=(1,) if stay else (4,),
        in_specs=[pl.BlockSpec(memory_space=pltpu.HBM)] * len(after),
        out_specs=[whole if stay else pl.BlockSpec((256, 1024), lambda g: (g, 0))]
        + [twiddle_spec] * (2 * with_twiddles),
        out_shape=[space((1024, 1024), BF16)] + [pltpu.HBM((128, 512), F32)] * (2 * with_twiddles),
        scratch_shapes=[pltpu.VMEM((n, 1024), F32) for n in (16, 16, 64, 64)],
        cost_estimate=pl.CostEstimate(flops=2**23, bytes_accessed=2**21, transcendentals=0),
        compiler_params=pltpu.CompilerParams(vmem_limit_bytes=6 * MIB),
        name=phases.__name__,
    )(*[remaining(v) for v in after])
    return out if with_twiddles else out[0]


def blocks_kernel(first_w, second_w, first_ref, last_ref, second_ref, fc, fs, bc):
    block = lax.axis_index("x")
    low = low_half(64)
    a, lane = iota((16, 256), 0), iota((16, 256), 1)
    t, ri, row_e = a >> 2, digit(a, 1, 1), a & 1
    ro, lane_e = lane >> 7, digit(lane, 6, 1)
    fc[...], fs[...] = cos_sin(128 * lane_e * (t + 4 * row_e) + 256 * (ro - ri))
    bc[...], _unused = cos_sin(128 * row_e * (t + 4 * lane_e) - 256 * (ro - ri))

    def twice(ref, n):
        w = ref[n, block].astype(F32)
        return jnp.concatenate([w, w], axis=1)

    w0, w1 = twice(second_w, 0), twice(second_w, 1)
    zero = jnp.zeros_like(w0)
    for half in range(2):
        def own(v):
            return (jnp.where(low, v, zero) if half == 0 else jnp.where(low, zero, v)).astype(BF16)

        re, im = slice(64 * half, 64 * half + 64), slice(128 + 64 * half, 192 + 64 * half)
        second_ref[re, :128], second_ref[re, 128:] = own(w0), own(w1)
        second_ref[im, :128], second_ref[im, 128:] = own(-w1), own(w0)

    w0, w1 = twice(first_w, 0), twice(first_w, 1)
    eye = jnp.where(iota((64, 128), 0) == (iota((64, 128), 1) & 63), 1.0, 0.0)
    for n in range(16):
        rows = slice(64 * n, 64 * n + 64)
        for lanes in (slice(0, 128), slice(128, 256)):
            first_ref[rows, lanes] = (
                fc[n : n + 1, lanes] * w0 + fs[n : n + 1, lanes] * w1
            ).astype(BF16)
            last_ref[rows, lanes] = (bc[n : n + 1, lanes] * eye).astype(BF16)


def block_tables(w_first, w_second):
    vmem = pl.BlockSpec(memory_space=pltpu.VMEM)
    return pl.pallas_call(
        blocks_kernel,
        grid=(1,),
        in_specs=[vmem, vmem],
        out_specs=[
            pl.BlockSpec((1024, 256), lambda g: (0, 0)),
            pl.BlockSpec((1024, 256), lambda g: (0, 0)),
            pl.BlockSpec((256, 256), lambda g: (0, 0)),
        ],
        out_shape=[pltpu.HBM((n, 256), BF16) for n in (1024, 1024, 256)],
        scratch_shapes=[pltpu.VMEM((16, 256), F32)] * 3,
        cost_estimate=pl.CostEstimate(flops=2**21, bytes_accessed=2**20, transcendentals=0),
        compiler_params=pltpu.CompilerParams(vmem_limit_bytes=6 * MIB),
        name="block_tables",
    )(w_first, w_second)


def low_half(rows):
    return lax.broadcasted_iota(jnp.int32, (rows, 128), 1) < 64


def swap(v):
    return pltpu.roll(v, 64, 1)


def normed_halves(x, gain_ref):
    ones = jnp.ones((256, 128), BF16)
    mean = dot(x, ones) * (1.0 / 256.0)
    d0, d1 = x[:, :128].astype(F32) - mean, x[:, 128:].astype(F32) - mean
    square = d0 * d0 + d1 * d1
    coarse = square.astype(BF16)
    fine = (square - coarse.astype(F32)).astype(BF16)
    var = dot(jnp.concatenate([coarse, fine], axis=1), ones) * (1.0 / 256.0)
    scale = lax.rsqrt(var + 1e-05)
    return d0 * scale * gain_ref[:, :128], d1 * scale * gain_ref[:, 128:]


def norm_kernel(x_any, gain_ref, out_any, x_all, packed, in_sems, out_sems):
    low = low_half(64)
    fetches, sends = [], []
    for n in range(2):
        rows = slice(16 * n, 16 * n + 16)
        fetches.append(pltpu.make_async_copy(x_any.at[rows], x_all.at[rows], in_sems.at[n]))
        fetches[-1].start()
    for n in range(2):
        fetches[n].wait()
        halves = normed_halves(x_all[16 * n : 16 * n + 16].reshape(1024, 256), gain_ref)
        for g in range(2):
            first = 4 * (2 * n + g)
            for t in range(4):
                lanes = slice(128 * t, 128 * t + 128)
                for m in range(2):
                    a = halves[m][512 * g + 64 * t : 512 * g + 64 * t + 64]
                    b = halves[m][512 * g + 64 * t + 256 : 512 * g + 64 * t + 320]
                    packed[first + 2 * m, :, lanes] = jnp.where(low, a, swap(b)).astype(BF16)
                    packed[first + 2 * m + 1, :, lanes] = jnp.where(low, swap(a), b).astype(BF16)
        parts = slice(8 * n, 8 * n + 8)
        sends.append(pltpu.make_async_copy(packed.at[parts], out_any.at[parts], out_sems.at[n]))
        sends[-1].start()
    for send in sends:
        send.wait()


def home_norm_kernel(x_ref, gain_ref, out_ref):
    for m, half in enumerate(normed_halves(x_ref[...].reshape(512, 256), gain_ref)):
        out_ref[:, :, 128 * m : 128 * m + 128] = half.astype(BF16).reshape(8, 64, 128)


def home_norm(patches, gain):
    block = pl.BlockSpec((8, 64, 256), lambda g: (g, 0, 0))
    return pl.pallas_call(
        home_norm_kernel,
        grid=(4,),
        in_specs=[block, pl.BlockSpec((1, 256), lambda g: (0, 0))],
        out_specs=block,
        out_shape=pltpu.HBM((32, 64, 256), BF16),
        cost_estimate=pl.CostEstimate(flops=2**24, bytes_accessed=2**21, transcendentals=0),
        compiler_params=pltpu.CompilerParams(vmem_limit_bytes=12 * MIB),
        name="home_norm",
    )(remaining(patches), remaining(gain.reshape(1, 256)))


def norm_and_pack(patches, gain):
    return pl.pallas_call(
        norm_kernel,
        in_specs=[pl.BlockSpec(memory_space=pltpu.HBM), pl.BlockSpec(memory_space=pltpu.VMEM)],
        out_specs=pl.BlockSpec(memory_space=pltpu.HBM),
        out_shape=pltpu.HBM((16, 64, 512), BF16),
        scratch_shapes=[
            pltpu.VMEM((32, 64, 256), BF16),
            pltpu.VMEM((16, 64, 512), BF16),
            pltpu.SemaphoreType.DMA((2,)),
            pltpu.SemaphoreType.DMA((2,)),
        ],
        compiler_params=pltpu.CompilerParams(vmem_limit_bytes=16 * MIB),
        name="norm_pack",
    )(remaining(patches), remaining(gain.reshape(1, 256)))


def final_kernel(base_ref, home_ref, out_any, held, sems):
    low = low_half(64)
    sends = []
    for g in range(4):
        for t in range(4):
            lanes = slice(128 * t, 128 * t + 128)
            for m in range(2):
                u = home_ref[4 * g + 2 * m, :, lanes].astype(F32)
                v = home_ref[4 * g + 2 * m + 1, :, lanes].astype(F32)
                chans, row = slice(128 * m, 128 * m + 128), 8 * g + t
                even, odd = jnp.where(low, u, swap(v)), jnp.where(low, swap(u), v)
                held[row, :, chans] = (base_ref[row, :, chans] + even).astype(BF16)
                held[row + 4, :, chans] = (base_ref[row + 4, :, chans] + odd).astype(BF16)
        rows = slice(8 * g, 8 * g + 8)
        sends.append(pltpu.make_async_copy(held.at[rows], out_any.at[rows], sems.at[g]))
        sends[-1].start()
    for send in sends:
        send.wait()


def unpack_and_add(base, home):
    return pl.pallas_call(
        final_kernel,
        in_specs=[pl.BlockSpec(memory_space=pltpu.VMEM)] * 2,
        out_specs=pl.BlockSpec(memory_space=pltpu.HBM),
        out_shape=pltpu.HBM((32, 64, 256), BF16),
        scratch_shapes=[pltpu.VMEM((32, 64, 256), BF16), pltpu.SemaphoreType.DMA((4,))],
        compiler_params=pltpu.CompilerParams(vmem_limit_bytes=8 * MIB),
        name="unpack_add",
    )(resident(base), resident(home))


def dot(a, b):
    return jnp.dot(a, b, preferred_element_type=F32)


def resident(v):
    return pltpu.with_memory_space_constraint(v, pltpu.VMEM)


def remaining(v):
    return pltpu.with_memory_space_constraint(v, pltpu.HBM)


def stream_dot(table, operand, held, out, sems):
    copies = []
    for m in range(4):
        rows = slice(256 * m, 256 * m + 256)
        held[rows, :] = dot(table[rows, :], operand[...]).astype(BF16)
        copies.append(pltpu.make_async_copy(held.at[rows, :], out.at[rows, :], sems.at[m]))
        copies[-1].start()
    for copy in copies:
        copy.wait()


def columns_kernel(table_ref, x_ref, out_any, held, sems):
    stream_dot(table_ref, x_ref, held, out_any, sems)


def columns(table, x):
    return pl.pallas_call(
        columns_kernel,
        in_specs=[pl.BlockSpec(memory_space=pltpu.VMEM)] * 2,
        out_specs=pl.BlockSpec(memory_space=pltpu.HBM),
        out_shape=pltpu.HBM((1024, 512), BF16),
        scratch_shapes=[pltpu.VMEM((1024, 512), BF16), pltpu.SemaphoreType.DMA((4,))],
        cost_estimate=pl.CostEstimate(flops=2**30, bytes_accessed=2**21, transcendentals=0),
        compiler_params=pltpu.CompilerParams(vmem_limit_bytes=12 * MIB),
        name="along_columns",
    )(resident(table), resident(x))


def stencil_kernel(
    x_ref, normed_ref, top_ref, bottom_ref, left_ref, right_ref, taps_ref, out_ref,
    rows, side, left_sum, right_sum,
):
    def tap(i, j):
        return taps_ref[3 * i + j : 3 * i + j + 1, :]

    @pl.when(pl.program_id(0) == 0)
    def _():
        rows[0], rows[33] = top_ref[...], bottom_ref[...]
        rows[1:33] = normed_ref[...]
        for rim_ref, sum_ref, j in ((left_ref, left_sum, 0), (right_ref, right_sum, 2)):
            side[...] = rim_ref[...].astype(F32)
            sum_ref[...] = side[0:32] * tap(0, j) + side[1:33] * tap(1, j) + side[2:34] * tap(2, j)

    column = iota((64, 256), 0)

    def step(r, carry):
        h = 8 * pl.program_id(0) + r
        around = [rows[h + i].astype(F32) for i in range(3)]

        def part(j):
            return around[0] * tap(0, j) + around[1] * tap(1, j) + around[2] * tap(2, j)

        left = jnp.where(column == 0, left_sum[pl.ds(h, 1), :], pltpu.roll(part(0), 1, 0))
        right = jnp.where(column == 63, right_sum[pl.ds(h, 1), :], pltpu.roll(part(2), 63, 0))
        out_ref[h] = x_ref[r].astype(F32) + (left + part(1) + right)
        return carry

    lax.fori_loop(0, 8, step, 0)


def stencil(x, normed, top, bottom, left, right, taps):
    block = pl.BlockSpec((8, 64, 256), lambda g: (g, 0, 0))
    row = pl.BlockSpec((64, 256), lambda g: (0, 0))
    side = pl.BlockSpec((34, 256), lambda g: (0, 0))
    return pl.pallas_call(
        stencil_kernel,
        grid=(4,),
        in_specs=[
            block,
            pl.BlockSpec((32, 64, 256), lambda g: (0, 0, 0)),
            row, row, side, side,
            pl.BlockSpec((9, 256), lambda g: (0, 0)),
        ],
        out_specs=pl.BlockSpec(memory_space=pltpu.VMEM),
        out_shape=pltpu.VMEM((32, 64, 256), F32),
        scratch_shapes=[
            pltpu.VMEM((34, 64, 256), BF16),
            pltpu.VMEM((34, 256), F32),
            pltpu.VMEM((32, 256), F32),
            pltpu.VMEM((32, 256), F32),
        ],
        cost_estimate=pl.CostEstimate(flops=2**24, bytes_accessed=2**22, transcendentals=0),
        compiler_params=pltpu.CompilerParams(vmem_limit_bytes=12 * MIB),
        name="stencil",
    )(*[remaining(v) for v in (x, normed, top, bottom, left, right, taps)])


def butterfly(x, sign):
    re, im = [v[:, :128] for v in x], [v[:, 128:] for v in x]

    def pair(v):
        return v[0] + v[2], v[0] - v[2], v[1] + v[3], v[1] - v[3]

    (er, dr, fr, gr), (ei, di, fi, gi) = pair(re), pair(im)
    plus, minus = (dr - gi, di + gr), (dr + gi, di - gr)
    if sign < 0:
        plus, minus = minus, plus
    return (er + fr, ei + fi), plus, (er - fr, ei - fi), minus


def beside(pair):
    return jnp.concatenate(pair, axis=1)


def middle_kernel(
    z, fwd, cos_any, sin_any, first_any, second_any, last_any, inv_any, out_any,
    cos_ref, sin_ref, first, second, last, inv, held, done, sems, fetch_sems,
):
    fetches = []
    for n, (src, dst) in enumerate(
        (
            (cos_any, cos_ref),
            (sin_any, sin_ref),
            (first_any, first),
            (second_any, second),
            (last_any, last),
            (inv_any, inv),
        )
    ):
        fetches.append(pltpu.make_async_copy(src, dst, fetch_sems.at[n]))
        fetches[-1].start()
    rows = 512 // CHUNKS
    groups = 8 // CHUNKS
    shape = (groups, 4, 16, 128)
    for m in range(CHUNKS):
        u = dot(fwd[2 * rows * m : 2 * rows * (m + 1), :], z[...])
        if m == 0:
            for fetch in fetches[:4]:
                fetch.wait()

        def twiddles(t):
            part = (slice(16 * groups * m, 16 * groups * (m + 1)), slice(128 * t, 128 * t + 128))
            return [ref[part].reshape(groups, 1, 16, 128) for ref in (cos_ref, sin_ref)]

        parts = []
        for t in range(4):
            ur = u[:rows, 128 * t : 128 * t + 128].reshape(shape)
            ui = u[rows:, 128 * t : 128 * t + 128].reshape(shape)
            c, s = twiddles(t)
            vr, vi = (ur * c + ui * s).reshape(rows, 128), (ui * c - ur * s).reshape(rows, 128)
            parts.append(dot(beside((vr.astype(BF16), vi.astype(BF16))), first[256 * t : 256 * t + 256, :]))
        kept = []
        for part in butterfly(parts, -1):
            v = dot(jnp.tanh(beside(part)).astype(BF16), second[...])
            kept.append(jnp.where(v > 0.25, v - 0.25, jnp.where(v < -0.25, v + 0.25, 0.0 * v)))
        if m == 0:
            fetches[4].wait()
        for t, part in enumerate(butterfly(kept, 1)):
            y = dot(beside(part).astype(BF16), last[256 * t : 256 * t + 256, :])
            yr, yi = y[:, :128].reshape(shape), y[:, 128:].reshape(shape)
            c, s = twiddles(t)
            lanes = slice(128 * t, 128 * t + 128)
            held[2 * rows * m : 2 * rows * m + rows, lanes] = (
                (yr * c - yi * s).astype(BF16).reshape(rows, 128)
            )
            held[2 * rows * m + rows : 2 * rows * (m + 1), lanes] = (
                (yi * c + yr * s).astype(BF16).reshape(rows, 128)
            )
    fetches[5].wait()
    stream_dot(inv, held, done, out_any, sems)


def middle(z, fwd, cos, sin, first, second, last, inv):
    vmem, hbm = pl.BlockSpec(memory_space=pltpu.VMEM), pl.BlockSpec(memory_space=pltpu.HBM)
    return pl.pallas_call(
        middle_kernel,
        in_specs=[vmem] * 2 + [hbm] * 6,
        out_specs=hbm,
        out_shape=pltpu.HBM((1024, 512), BF16),
        scratch_shapes=[
            pltpu.VMEM((128, 512), F32),
            pltpu.VMEM((128, 512), F32),
            pltpu.VMEM((1024, 256), BF16),
            pltpu.VMEM((256, 256), BF16),
            pltpu.VMEM((1024, 256), BF16),
            pltpu.VMEM((1024, 1024), BF16),
            pltpu.VMEM((1024, 512), BF16),
            pltpu.VMEM((1024, 512), BF16),
            pltpu.SemaphoreType.DMA((4,)),
            pltpu.SemaphoreType.DMA((6,)),
        ],
        cost_estimate=pl.CostEstimate(flops=3 * 2**30, bytes_accessed=2**21, transcendentals=2**19),
        compiler_params=pltpu.CompilerParams(vmem_limit_bytes=24 * MIB),
        name="filter_rows",
    )(
        resident(z), resident(fwd), *[remaining(v) for v in (cos, sin, first, second, last, inv)]
    )


def local(patches, norm_gain, w_first, w_second, depth_kernel):
    packed = norm_and_pack(patches, norm_gain)
    lines = lax.all_to_all(packed, ("yl", "x"), 0, 0, tiled=True).reshape(1024, 512)

    fwd_w = table(pltpu.VMEM, forward_columns_phases)
    inv_w = table(pltpu.VMEM, backward_columns_phases)
    inv_h = table(pltpu.HBM, backward_rows_phases)
    first, last, second = block_tables(w_first, w_second)
    fwd_h, cos, sin = table(pltpu.VMEM, forward_rows_phases, True, (second, inv_h))

    def neighbours(first, last, axis):
        n = lax.axis_size(axis)
        before = lax.ppermute(last, axis, [(i, (i + 1) % n) for i in range(n)])
        after = lax.ppermute(first, axis, [((i + 1) % n, i) for i in range(n)])
        return before, after

    normed = home_norm(patches, norm_gain)
    top, bottom = neighbours(normed[0], normed[31], "row")

    freqs = columns(fwd_w, lines)
    freqs, top, bottom, normed = lax.optimization_barrier((freqs, top, bottom, normed))
    whole = lax.all_to_all(freqs.reshape(128, 8, 512), ("row", "yl"), 0, 0, tiled=True)
    sides = [
        jnp.concatenate([top[w : w + 1], normed[:, w], bottom[w : w + 1]], axis=0) for w in (0, 63)
    ]
    left, right = neighbours(sides[0], sides[1], ("yl", "x"))
    whole, left, right = lax.optimization_barrier((whole, left, right))

    filtered = middle(whole.reshape(1024, 512), fwd_h, cos, sin, first, second, last, inv_h)
    back = lax.all_to_all(filtered.reshape(128, 8, 512), ("row", "yl"), 0, 0, tiled=True)
    spectral = columns(inv_w, back.reshape(1024, 512))
    spectral, left, right = lax.optimization_barrier((spectral, left, right))
    home = lax.all_to_all(spectral.reshape(16, 64, 512), ("yl", "x"), 0, 0, tiled=True)
    base = stencil(patches, normed, top, bottom, left, right, depth_kernel.reshape(9, 256))
    return unpack_and_add(base, home)


def solution(mesh):
    fine = Mesh(np.asarray(mesh.devices).reshape(32, 4, 4), ("row", "yl", "x"))
    return jax.shard_map(
        local,
        mesh=fine,
        in_specs=(P("row", ("yl", "x"), None), P(), P(), P(), P()),
        out_specs=P("row", ("yl", "x"), None),
        check_vma=False,
    )
```

```python
import functools
import math

import jax
import jax.numpy as jnp
import numpy as np
from jax import lax
from jax.experimental import pallas as pl
from jax.experimental.pallas import tpu as pltpu
from jax.sharding import Mesh
from jax.sharding import PartitionSpec as P

TURN = 1024
CHUNKS = 2
MIB = 1024 * 1024
F32 = jnp.float32
BF16 = jnp.bfloat16


def iota(shape, dim):
    return lax.broadcasted_iota(jnp.int32, shape, dim)


def digit(idx, shift, bits):
    return (idx >> shift) & ((1 << bits) - 1)


def cos_sin(idx):
    idx = idx & (TURN - 1)
    quarter = (idx + TURN // 8) >> 8
    x = (idx - (quarter << 8)).astype(F32) * (2.0 * math.pi / TURN)
    y = x * x
    s = x * (1.0 + y * (-1.0 / 6 + y * (1.0 / 120 + y * (-1.0 / 5040 + y * (1.0 / 362880)))))
    c = 1.0 + y * (-1.0 / 2 + y * (1.0 / 24 + y * (-1.0 / 720 + y * (1.0 / 40320))))
    odd = (quarter & 1) == 1
    cos, sin = jnp.where(odd, s, c), jnp.where(odd, c, s)
    turned = (quarter + 1) & 3
    cos = jnp.where(turned >= 2, -cos, cos)
    sin = jnp.where((quarter & 3) >= 2, -sin, sin)
    return cos, sin


SCALE = 1.0 / 32.0


def forward_columns_phases():
    a, b = iota((16, 1024), 0), iota((64, 1024), 0)
    w = iota((64, 1024), 1)
    k = 4 * digit(b, 3, 3) + digit(b, 0, 2)
    return 32 * a * w[:16], k * w + 256 * digit(b, 2, 1), SCALE


def backward_columns_phases():
    a, b, lane = iota((16, 1024), 0), iota((64, 1024), 0), iota((64, 1024), 1)
    k = 4 * (lane >> 3) + digit(lane, 0, 2)
    weight = jnp.where(k == 0, SCALE, 2.0 * SCALE)
    return 64 * a * k[:16], b * k + 256 * digit(lane, 2, 1), weight


def forward_rows_phases():
    a, b, lane = iota((16, 1024), 0), iota((64, 1024), 0), iota((64, 1024), 1)
    qh = 4 * digit(a, 3, 1) + digit(a, 0, 2)
    p, ri = lane >> 3, digit(lane, 2, 1)
    ia = 128 * qh * p[:16] + 256 * (digit(a, 2, 1) - ri[:16])
    weight = jnp.where(digit(b, 4, 2) == digit(lane, 0, 2), SCALE, 0.0)
    return ia, 8 * digit(b, 0, 4) * p, weight


def backward_rows_phases():
    a, b, lane = iota((16, 1024), 0), iota((64, 1024), 0), iota((64, 1024), 1)
    q0 = 16 * (4 * digit(lane, 9, 1) + digit(lane, 6, 2)) + digit(lane, 0, 4)
    ro = digit(lane, 8, 1)
    weight = jnp.where(digit(b, 0, 2) == digit(lane, 4, 2), SCALE, 0.0)
    return 64 * a * q0[:16], 8 * digit(b, 3, 3) * q0 + 256 * (ro - digit(b, 2, 1)), weight


def table_kernel(phases, with_twiddles, stay, waited, *refs):
    refs = refs[waited:]
    out_ref, (ec, es, fc, fs) = refs[0], refs[-4:]
    steps = 16 if stay else 4

    @pl.when(pl.program_id(0) == 0)
    def _():
        ia, ib, weight = phases()
        ec[...], es[...] = cos_sin(ia)
        c, s = cos_sin(ib)
        fc[...], fs[...] = c * weight, s * weight
        if with_twiddles:
            lane = iota((128, 512), 1)
            angle = iota((128, 512), 0) * ((lane >> 7) + 4 * digit(lane, 6, 1))
            refs[1][...], refs[2][...] = cos_sin(angle)

    first = 0 if stay else steps * pl.program_id(0)

    def step(a, carry):
        row = pl.ds(first + a, 1)
        out_ref[pl.ds(pl.multiple_of(64 * a, 64), 64), :] = (
            ec[row, :] * fc[...] - es[row, :] * fs[...]
        ).astype(BF16)
        return carry

    lax.fori_loop(0, steps, step, 0)


def table(space, phases, with_twiddles=False, after=()):
    stay = space == pltpu.VMEM
    whole = pl.BlockSpec(memory_space=pltpu.VMEM)
    twiddle_spec = pl.BlockSpec((128, 512), lambda g: (0, 0))
    out = pl.pallas_call(
        functools.partial(table_kernel, phases, with_twiddles, stay, len(after)),
        grid=(1,) if stay else (4,),
        in_specs=[pl.BlockSpec(memory_space=pltpu.HBM)] * len(after),
        out_specs=[whole if stay else pl.BlockSpec((256, 1024), lambda g: (g, 0))]
        + [twiddle_spec] * (2 * with_twiddles),
        out_shape=[space((1024, 1024), BF16)] + [pltpu.HBM((128, 512), F32)] * (2 * with_twiddles),
        scratch_shapes=[pltpu.VMEM((n, 1024), F32) for n in (16, 16, 64, 64)],
        cost_estimate=pl.CostEstimate(flops=2**23, bytes_accessed=2**21, transcendentals=0),
        compiler_params=pltpu.CompilerParams(vmem_limit_bytes=6 * MIB),
        name=phases.__name__,
    )(*[remaining(v) for v in after])
    return out if with_twiddles else out[0]


def blocks_kernel(first_w, second_w, first_ref, last_ref, second_ref, fc, fs, bc):
    block = lax.axis_index("x")
    low = low_half(64)
    a, lane = iota((16, 256), 0), iota((16, 256), 1)
    t, ri, row_e = a >> 2, digit(a, 1, 1), a & 1
    ro, lane_e = lane >> 7, digit(lane, 6, 1)
    fc[...], fs[...] = cos_sin(128 * lane_e * (t + 4 * row_e) + 256 * (ro - ri))
    bc[...], _unused = cos_sin(128 * row_e * (t + 4 * lane_e) - 256 * (ro - ri))

    def twice(ref, n):
        w = ref[n, block].astype(F32)
        return jnp.concatenate([w, w], axis=1)

    w0, w1 = twice(second_w, 0), twice(second_w, 1)
    zero = jnp.zeros_like(w0)
    for half in range(2):
        def own(v):
            return (jnp.where(low, v, zero) if half == 0 else jnp.where(low, zero, v)).astype(BF16)

        re, im = slice(64 * half, 64 * half + 64), slice(128 + 64 * half, 192 + 64 * half)
        second_ref[re, :128], second_ref[re, 128:] = own(w0), own(w1)
        second_ref[im, :128], second_ref[im, 128:] = own(-w1), own(w0)

    w0, w1 = twice(first_w, 0), twice(first_w, 1)
    eye = jnp.where(iota((64, 128), 0) == (iota((64, 128), 1) & 63), 1.0, 0.0)
    for n in range(16):
        rows = slice(64 * n, 64 * n + 64)
        for lanes in (slice(0, 128), slice(128, 256)):
            first_ref[rows, lanes] = (
                fc[n : n + 1, lanes] * w0 + fs[n : n + 1, lanes] * w1
            ).astype(BF16)
            last_ref[rows, lanes] = (bc[n : n + 1, lanes] * eye).astype(BF16)


def block_tables(w_first, w_second):
    vmem = pl.BlockSpec(memory_space=pltpu.VMEM)
    return pl.pallas_call(
        blocks_kernel,
        grid=(1,),
        in_specs=[vmem, vmem],
        out_specs=[
            pl.BlockSpec((1024, 256), lambda g: (0, 0)),
            pl.BlockSpec((1024, 256), lambda g: (0, 0)),
            pl.BlockSpec((256, 256), lambda g: (0, 0)),
        ],
        out_shape=[pltpu.HBM((n, 256), BF16) for n in (1024, 1024, 256)],
        scratch_shapes=[pltpu.VMEM((16, 256), F32)] * 3,
        cost_estimate=pl.CostEstimate(flops=2**21, bytes_accessed=2**20, transcendentals=0),
        compiler_params=pltpu.CompilerParams(vmem_limit_bytes=6 * MIB),
        name="block_tables",
    )(w_first, w_second)


def low_half(rows):
    return lax.broadcasted_iota(jnp.int32, (rows, 128), 1) < 64


def swap(v):
    return pltpu.roll(v, 64, 1)


def normed_halves(x, gain_ref):
    ones = jnp.ones((256, 128), BF16)
    mean = dot(x, ones) * (1.0 / 256.0)
    d0, d1 = x[:, :128].astype(F32) - mean, x[:, 128:].astype(F32) - mean
    square = d0 * d0 + d1 * d1
    coarse = square.astype(BF16)
    fine = (square - coarse.astype(F32)).astype(BF16)
    var = dot(jnp.concatenate([coarse, fine], axis=1), ones) * (1.0 / 256.0)
    scale = lax.rsqrt(var + 1e-05)
    return d0 * scale * gain_ref[:, :128], d1 * scale * gain_ref[:, 128:]


def norm_kernel(x_any, gain_ref, out_any, x_all, packed, in_sems, out_sems):
    low = low_half(64)
    fetches, sends = [], []
    for n in range(2):
        rows = slice(16 * n, 16 * n + 16)
        fetches.append(pltpu.make_async_copy(x_any.at[rows], x_all.at[rows], in_sems.at[n]))
        fetches[-1].start()
    for n in range(2):
        fetches[n].wait()
        halves = normed_halves(x_all[16 * n : 16 * n + 16].reshape(1024, 256), gain_ref)
        for g in range(2):
            first = 4 * (2 * n + g)
            for t in range(4):
                lanes = slice(128 * t, 128 * t + 128)
                for m in range(2):
                    a = halves[m][512 * g + 64 * t : 512 * g + 64 * t + 64]
                    b = halves[m][512 * g + 64 * t + 256 : 512 * g + 64 * t + 320]
                    packed[first + 2 * m, :, lanes] = jnp.where(low, a, swap(b)).astype(BF16)
                    packed[first + 2 * m + 1, :, lanes] = jnp.where(low, swap(a), b).astype(BF16)
        parts = slice(8 * n, 8 * n + 8)
        sends.append(pltpu.make_async_copy(packed.at[parts], out_any.at[parts], out_sems.at[n]))
        sends[-1].start()
    for send in sends:
        send.wait()


def home_norm_kernel(x_ref, gain_ref, out_ref):
    for m, half in enumerate(normed_halves(x_ref[...].reshape(512, 256), gain_ref)):
        out_ref[:, :, 128 * m : 128 * m + 128] = half.astype(BF16).reshape(8, 64, 128)


def home_norm(patches, gain):
    block = pl.BlockSpec((8, 64, 256), lambda g: (g, 0, 0))
    return pl.pallas_call(
        home_norm_kernel,
        grid=(4,),
        in_specs=[block, pl.BlockSpec((1, 256), lambda g: (0, 0))],
        out_specs=block,
        out_shape=pltpu.HBM((32, 64, 256), BF16),
        cost_estimate=pl.CostEstimate(flops=2**24, bytes_accessed=2**21, transcendentals=0),
        compiler_params=pltpu.CompilerParams(vmem_limit_bytes=12 * MIB),
        name="home_norm",
    )(remaining(patches), remaining(gain.reshape(1, 256)))


def norm_and_pack(patches, gain):
    return pl.pallas_call(
        norm_kernel,
        in_specs=[pl.BlockSpec(memory_space=pltpu.HBM), pl.BlockSpec(memory_space=pltpu.VMEM)],
        out_specs=pl.BlockSpec(memory_space=pltpu.HBM),
        out_shape=pltpu.HBM((16, 64, 512), BF16),
        scratch_shapes=[
            pltpu.VMEM((32, 64, 256), BF16),
            pltpu.VMEM((16, 64, 512), BF16),
            pltpu.SemaphoreType.DMA((2,)),
            pltpu.SemaphoreType.DMA((2,)),
        ],
        compiler_params=pltpu.CompilerParams(vmem_limit_bytes=16 * MIB),
        name="norm_pack",
    )(remaining(patches), remaining(gain.reshape(1, 256)))


def final_kernel(base_ref, home_ref, out_any, held, sems):
    low = low_half(64)
    sends = []
    for g in range(4):
        for t in range(4):
            lanes = slice(128 * t, 128 * t + 128)
            for m in range(2):
                u = home_ref[4 * g + 2 * m, :, lanes].astype(F32)
                v = home_ref[4 * g + 2 * m + 1, :, lanes].astype(F32)
                chans, row = slice(128 * m, 128 * m + 128), 8 * g + t
                even, odd = jnp.where(low, u, swap(v)), jnp.where(low, swap(u), v)
                held[row, :, chans] = (base_ref[row, :, chans] + even).astype(BF16)
                held[row + 4, :, chans] = (base_ref[row + 4, :, chans] + odd).astype(BF16)
        rows = slice(8 * g, 8 * g + 8)
        sends.append(pltpu.make_async_copy(held.at[rows], out_any.at[rows], sems.at[g]))
        sends[-1].start()
    for send in sends:
        send.wait()


def unpack_and_add(base, home):
    return pl.pallas_call(
        final_kernel,
        in_specs=[pl.BlockSpec(memory_space=pltpu.VMEM)] * 2,
        out_specs=pl.BlockSpec(memory_space=pltpu.HBM),
        out_shape=pltpu.HBM((32, 64, 256), BF16),
        scratch_shapes=[pltpu.VMEM((32, 64, 256), BF16), pltpu.SemaphoreType.DMA((4,))],
        compiler_params=pltpu.CompilerParams(vmem_limit_bytes=8 * MIB),
        name="unpack_add",
    )(resident(base), resident(home))


def dot(a, b):
    return jnp.dot(a, b, preferred_element_type=F32)


def resident(v):
    return pltpu.with_memory_space_constraint(v, pltpu.VMEM)


def remaining(v):
    return pltpu.with_memory_space_constraint(v, pltpu.HBM)


def stream_dot(table, operand, held, out, sems):
    copies = []
    for m in range(4):
        rows = slice(256 * m, 256 * m + 256)
        held[rows, :] = dot(table[rows, :], operand[...]).astype(BF16)
        copies.append(pltpu.make_async_copy(held.at[rows, :], out.at[rows, :], sems.at[m]))
        copies[-1].start()
    for copy in copies:
        copy.wait()


def columns_kernel(table_ref, x_ref, out_any, held, sems):
    stream_dot(table_ref, x_ref, held, out_any, sems)


def columns(table, x):
    return pl.pallas_call(
        columns_kernel,
        in_specs=[pl.BlockSpec(memory_space=pltpu.VMEM)] * 2,
        out_specs=pl.BlockSpec(memory_space=pltpu.HBM),
        out_shape=pltpu.HBM((1024, 512), BF16),
        scratch_shapes=[pltpu.VMEM((1024, 512), BF16), pltpu.SemaphoreType.DMA((4,))],
        cost_estimate=pl.CostEstimate(flops=2**30, bytes_accessed=2**21, transcendentals=0),
        compiler_params=pltpu.CompilerParams(vmem_limit_bytes=12 * MIB),
        name="along_columns",
    )(resident(table), resident(x))


def stencil_kernel(
    x_ref, normed_ref, top_ref, bottom_ref, left_ref, right_ref, taps_ref, out_ref,
    rows, side, left_sum, right_sum,
):
    def tap(i, j):
        return taps_ref[3 * i + j : 3 * i + j + 1, :]

    @pl.when(pl.program_id(0) == 0)
    def _():
        rows[0], rows[33] = top_ref[...], bottom_ref[...]
        rows[1:33] = normed_ref[...]
        for rim_ref, sum_ref, j in ((left_ref, left_sum, 0), (right_ref, right_sum, 2)):
            side[...] = rim_ref[...].astype(F32)
            sum_ref[...] = side[0:32] * tap(0, j) + side[1:33] * tap(1, j) + side[2:34] * tap(2, j)

    column = iota((64, 256), 0)

    def step(r, carry):
        h = 8 * pl.program_id(0) + r
        around = [rows[h + i].astype(F32) for i in range(3)]

        def part(j):
            return around[0] * tap(0, j) + around[1] * tap(1, j) + around[2] * tap(2, j)

        left = jnp.where(column == 0, left_sum[pl.ds(h, 1), :], pltpu.roll(part(0), 1, 0))
        right = jnp.where(column == 63, right_sum[pl.ds(h, 1), :], pltpu.roll(part(2), 63, 0))
        out_ref[h] = x_ref[r].astype(F32) + (left + part(1) + right)
        return carry

    lax.fori_loop(0, 8, step, 0)


def stencil(x, normed, top, bottom, left, right, taps):
    block = pl.BlockSpec((8, 64, 256), lambda g: (g, 0, 0))
    row = pl.BlockSpec((64, 256), lambda g: (0, 0))
    side = pl.BlockSpec((34, 256), lambda g: (0, 0))
    return pl.pallas_call(
        stencil_kernel,
        grid=(4,),
        in_specs=[
            block,
            pl.BlockSpec((32, 64, 256), lambda g: (0, 0, 0)),
            row, row, side, side,
            pl.BlockSpec((9, 256), lambda g: (0, 0)),
        ],
        out_specs=pl.BlockSpec(memory_space=pltpu.VMEM),
        out_shape=pltpu.VMEM((32, 64, 256), F32),
        scratch_shapes=[
            pltpu.VMEM((34, 64, 256), BF16),
            pltpu.VMEM((34, 256), F32),
            pltpu.VMEM((32, 256), F32),
            pltpu.VMEM((32, 256), F32),
        ],
        cost_estimate=pl.CostEstimate(flops=2**24, bytes_accessed=2**22, transcendentals=0),
        compiler_params=pltpu.CompilerParams(vmem_limit_bytes=12 * MIB),
        name="stencil",
    )(*[remaining(v) for v in (x, normed, top, bottom, left, right, taps)])


def butterfly(x, sign):
    re, im = [v[:, :128] for v in x], [v[:, 128:] for v in x]

    def pair(v):
        return v[0] + v[2], v[0] - v[2], v[1] + v[3], v[1] - v[3]

    (er, dr, fr, gr), (ei, di, fi, gi) = pair(re), pair(im)
    plus, minus = (dr - gi, di + gr), (dr + gi, di - gr)
    if sign < 0:
        plus, minus = minus, plus
    return (er + fr, ei + fi), plus, (er - fr, ei - fi), minus


def beside(pair):
    return jnp.concatenate(pair, axis=1)


def middle_kernel(
    z, fwd, cos_any, sin_any, first_any, second_any, last_any, inv_any, out_any,
    cos_ref, sin_ref, first, second, last, inv, held, done, sems, fetch_sems,
):
    fetches = []
    for n, (src, dst) in enumerate(
        (
            (cos_any, cos_ref),
            (sin_any, sin_ref),
            (first_any, first),
            (second_any, second),
            (last_any, last),
            (inv_any, inv),
        )
    ):
        fetches.append(pltpu.make_async_copy(src, dst, fetch_sems.at[n]))
        fetches[-1].start()
    rows = 512 // CHUNKS
    groups = 8 // CHUNKS
    shape = (groups, 4, 16, 128)
    for m in range(CHUNKS):
        u = dot(fwd[2 * rows * m : 2 * rows * (m + 1), :], z[...])
        if m == 0:
            for fetch in fetches[:4]:
                fetch.wait()

        def twiddles(t):
            part = (slice(16 * groups * m, 16 * groups * (m + 1)), slice(128 * t, 128 * t + 128))
            return [ref[part].reshape(groups, 1, 16, 128) for ref in (cos_ref, sin_ref)]

        parts = []
        for t in range(4):
            ur = u[:rows, 128 * t : 128 * t + 128].reshape(shape)
            ui = u[rows:, 128 * t : 128 * t + 128].reshape(shape)
            c, s = twiddles(t)
            vr, vi = (ur * c + ui * s).reshape(rows, 128), (ui * c - ur * s).reshape(rows, 128)
            parts.append(dot(beside((vr.astype(BF16), vi.astype(BF16))), first[256 * t : 256 * t + 256, :]))
        kept = []
        for part in butterfly(parts, -1):
            v = dot(jnp.tanh(beside(part)).astype(BF16), second[...])
            kept.append(jnp.where(v > 0.25, v - 0.25, jnp.where(v < -0.25, v + 0.25, 0.0 * v)))
        if m == 0:
            fetches[4].wait()
        for t, part in enumerate(butterfly(kept, 1)):
            y = dot(beside(part).astype(BF16), last[256 * t : 256 * t + 256, :])
            yr, yi = y[:, :128].reshape(shape), y[:, 128:].reshape(shape)
            c, s = twiddles(t)
            lanes = slice(128 * t, 128 * t + 128)
            held[2 * rows * m : 2 * rows * m + rows, lanes] = (
                (yr * c - yi * s).astype(BF16).reshape(rows, 128)
            )
            held[2 * rows * m + rows : 2 * rows * (m + 1), lanes] = (
                (yi * c + yr * s).astype(BF16).reshape(rows, 128)
            )
    fetches[5].wait()
    stream_dot(inv, held, done, out_any, sems)


def middle(z, fwd, cos, sin, first, second, last, inv):
    vmem, hbm = pl.BlockSpec(memory_space=pltpu.VMEM), pl.BlockSpec(memory_space=pltpu.HBM)
    return pl.pallas_call(
        middle_kernel,
        in_specs=[vmem] * 2 + [hbm] * 6,
        out_specs=hbm,
        out_shape=pltpu.HBM((1024, 512), BF16),
        scratch_shapes=[
            pltpu.VMEM((128, 512), F32),
            pltpu.VMEM((128, 512), F32),
            pltpu.VMEM((1024, 256), BF16),
            pltpu.VMEM((256, 256), BF16),
            pltpu.VMEM((1024, 256), BF16),
            pltpu.VMEM((1024, 1024), BF16),
            pltpu.VMEM((1024, 512), BF16),
            pltpu.VMEM((1024, 512), BF16),
            pltpu.SemaphoreType.DMA((4,)),
            pltpu.SemaphoreType.DMA((6,)),
        ],
        cost_estimate=pl.CostEstimate(flops=3 * 2**30, bytes_accessed=2**21, transcendentals=2**19),
        compiler_params=pltpu.CompilerParams(vmem_limit_bytes=24 * MIB),
        name="filter_rows",
    )(
        resident(z), resident(fwd), *[remaining(v) for v in (cos, sin, first, second, last, inv)]
    )


def local(patches, norm_gain, w_first, w_second, depth_kernel):
    packed = norm_and_pack(patches, norm_gain)
    lines = lax.all_to_all(packed, ("yl", "x"), 0, 0, tiled=True).reshape(1024, 512)

    fwd_w = table(pltpu.VMEM, forward_columns_phases)
    inv_w = table(pltpu.VMEM, backward_columns_phases)
    inv_h = table(pltpu.HBM, backward_rows_phases)
    first, last, second = block_tables(w_first, w_second)
    fwd_h, cos, sin = table(pltpu.VMEM, forward_rows_phases, True, (second, inv_h))

    def neighbours(first, last, axis):
        n = lax.axis_size(axis)
        before = lax.ppermute(last, axis, [(i, (i + 1) % n) for i in range(n)])
        after = lax.ppermute(first, axis, [((i + 1) % n, i) for i in range(n)])
        return before, after

    normed = home_norm(patches, norm_gain)
    lines, normed = lax.optimization_barrier((lines, normed))

    freqs = columns(fwd_w, lines)
    whole = lax.all_to_all(freqs.reshape(128, 8, 512), ("row", "yl"), 0, 0, tiled=True)
    top, bottom = neighbours(normed[0], normed[31], "row")

    filtered = middle(whole.reshape(1024, 512), fwd_h, cos, sin, first, second, last, inv_h)
    filtered, top, bottom, normed = lax.optimization_barrier((filtered, top, bottom, normed))
    back = lax.all_to_all(filtered.reshape(128, 8, 512), ("row", "yl"), 0, 0, tiled=True)
    sides = [
        jnp.concatenate([top[w : w + 1], normed[:, w], bottom[w : w + 1]], axis=0) for w in (0, 63)
    ]
    left, right = neighbours(sides[0], sides[1], ("yl", "x"))
    back, left, right = lax.optimization_barrier((back, left, right))

    spectral = columns(inv_w, back.reshape(1024, 512))
    spectral, left, right = lax.optimization_barrier((spectral, left, right))
    home = lax.all_to_all(spectral.reshape(16, 64, 512), ("yl", "x"), 0, 0, tiled=True)
    base = stencil(patches, normed, top, bottom, left, right, depth_kernel.reshape(9, 256))
    return unpack_and_add(base, home)


def solution(mesh):
    fine = Mesh(np.asarray(mesh.devices).reshape(32, 4, 4), ("row", "yl", "x"))
    return jax.shard_map(
        local,
        mesh=fine,
        in_specs=(P("row", ("yl", "x"), None), P(), P(), P(), P()),
        out_specs=P("row", ("yl", "x"), None),
        check_vma=False,
    )
```

```python
import functools
import math

import jax
import jax.numpy as jnp
import numpy as np
from jax import lax
from jax.experimental import pallas as pl
from jax.experimental.pallas import tpu as pltpu
from jax.sharding import Mesh
from jax.sharding import PartitionSpec as P

TURN = 1024
CHUNKS = 2
MIB = 1024 * 1024
F32 = jnp.float32
BF16 = jnp.bfloat16


def iota(shape, dim):
    return lax.broadcasted_iota(jnp.int32, shape, dim)


def digit(idx, shift, bits):
    return (idx >> shift) & ((1 << bits) - 1)


def cos_sin(idx):
    idx = idx & (TURN - 1)
    quarter = (idx + TURN // 8) >> 8
    x = (idx - (quarter << 8)).astype(F32) * (2.0 * math.pi / TURN)
    y = x * x
    s = x * (1.0 + y * (-1.0 / 6 + y * (1.0 / 120 + y * (-1.0 / 5040 + y * (1.0 / 362880)))))
    c = 1.0 + y * (-1.0 / 2 + y * (1.0 / 24 + y * (-1.0 / 720 + y * (1.0 / 40320))))
    odd = (quarter & 1) == 1
    cos, sin = jnp.where(odd, s, c), jnp.where(odd, c, s)
    turned = (quarter + 1) & 3
    cos = jnp.where(turned >= 2, -cos, cos)
    sin = jnp.where((quarter & 3) >= 2, -sin, sin)
    return cos, sin


SCALE = 1.0 / 32.0


def forward_columns_phases():
    a, b = iota((16, 1024), 0), iota((64, 1024), 0)
    w = iota((64, 1024), 1)
    k = 4 * digit(b, 3, 3) + digit(b, 0, 2)
    return 32 * a * w[:16], k * w + 256 * digit(b, 2, 1), SCALE


def backward_columns_phases():
    a, b, lane = iota((16, 1024), 0), iota((64, 1024), 0), iota((64, 1024), 1)
    k = 4 * (lane >> 3) + digit(lane, 0, 2)
    weight = jnp.where(k == 0, SCALE, 2.0 * SCALE)
    return 64 * a * k[:16], b * k + 256 * digit(lane, 2, 1), weight


def forward_rows_phases():
    a, b, lane = iota((16, 1024), 0), iota((64, 1024), 0), iota((64, 1024), 1)
    qh = 4 * digit(a, 3, 1) + digit(a, 0, 2)
    p, ri = lane >> 3, digit(lane, 2, 1)
    ia = 128 * qh * p[:16] + 256 * (digit(a, 2, 1) - ri[:16])
    weight = jnp.where(digit(b, 4, 2) == digit(lane, 0, 2), SCALE, 0.0)
    return ia, 8 * digit(b, 0, 4) * p, weight


def backward_rows_phases():
    a, b, lane = iota((16, 1024), 0), iota((64, 1024), 0), iota((64, 1024), 1)
    q0 = 16 * (4 * digit(lane, 9, 1) + digit(lane, 6, 2)) + digit(lane, 0, 4)
    ro = digit(lane, 8, 1)
    weight = jnp.where(digit(b, 0, 2) == digit(lane, 4, 2), SCALE, 0.0)
    return 64 * a * q0[:16], 8 * digit(b, 3, 3) * q0 + 256 * (ro - digit(b, 2, 1)), weight


def table_kernel(phases, with_twiddles, stay, waited, *refs):
    refs = refs[waited:]
    out_ref, (ec, es, fc, fs) = refs[0], refs[-4:]
    steps = 16 if stay else 4

    @pl.when(pl.program_id(0) == 0)
    def _():
        ia, ib, weight = phases()
        ec[...], es[...] = cos_sin(ia)
        c, s = cos_sin(ib)
        fc[...], fs[...] = c * weight, s * weight
        if with_twiddles:
            lane = iota((128, 512), 1)
            angle = iota((128, 512), 0) * ((lane >> 7) + 4 * digit(lane, 6, 1))
            refs[1][...], refs[2][...] = cos_sin(angle)

    first = 0 if stay else steps * pl.program_id(0)

    def step(a, carry):
        row = pl.ds(first + a, 1)
        out_ref[pl.ds(pl.multiple_of(64 * a, 64), 64), :] = (
            ec[row, :] * fc[...] - es[row, :] * fs[...]
        ).astype(BF16)
        return carry

    lax.fori_loop(0, steps, step, 0)


def table(space, phases, with_twiddles=False, after=()):
    stay = space == pltpu.VMEM
    whole = pl.BlockSpec(memory_space=pltpu.VMEM)
    twiddle_spec = pl.BlockSpec((128, 512), lambda g: (0, 0))
    out = pl.pallas_call(
        functools.partial(table_kernel, phases, with_twiddles, stay, len(after)),
        grid=(1,) if stay else (4,),
        in_specs=[pl.BlockSpec(memory_space=pltpu.HBM)] * len(after),
        out_specs=[whole if stay else pl.BlockSpec((256, 1024), lambda g: (g, 0))]
        + [twiddle_spec] * (2 * with_twiddles),
        out_shape=[space((1024, 1024), BF16)] + [pltpu.HBM((128, 512), F32)] * (2 * with_twiddles),
        scratch_shapes=[pltpu.VMEM((n, 1024), F32) for n in (16, 16, 64, 64)],
        cost_estimate=pl.CostEstimate(flops=2**23, bytes_accessed=2**21, transcendentals=0),
        compiler_params=pltpu.CompilerParams(vmem_limit_bytes=6 * MIB),
        name=phases.__name__,
    )(*[remaining(v) for v in after])
    return out if with_twiddles else out[0]


def blocks_kernel(first_w, second_w, first_ref, last_ref, second_ref, fc, fs, bc):
    block = lax.axis_index("x")
    low = low_half(64)
    a, lane = iota((16, 256), 0), iota((16, 256), 1)
    t, ri, row_e = a >> 2, digit(a, 1, 1), a & 1
    ro, lane_e = lane >> 7, digit(lane, 6, 1)
    fc[...], fs[...] = cos_sin(128 * lane_e * (t + 4 * row_e) + 256 * (ro - ri))
    bc[...], _unused = cos_sin(128 * row_e * (t + 4 * lane_e) - 256 * (ro - ri))

    def twice(ref, n):
        w = ref[n, block].astype(F32)
        return jnp.concatenate([w, w], axis=1)

    w0, w1 = twice(second_w, 0), twice(second_w, 1)
    zero = jnp.zeros_like(w0)
    for half in range(2):
        def own(v):
            return (jnp.where(low, v, zero) if half == 0 else jnp.where(low, zero, v)).astype(BF16)

        re, im = slice(64 * half, 64 * half + 64), slice(128 + 64 * half, 192 + 64 * half)
        second_ref[re, :128], second_ref[re, 128:] = own(w0), own(w1)
        second_ref[im, :128], second_ref[im, 128:] = own(-w1), own(w0)

    w0, w1 = twice(first_w, 0), twice(first_w, 1)
    eye = jnp.where(iota((64, 128), 0) == (iota((64, 128), 1) & 63), 1.0, 0.0)
    for n in range(16):
        rows = slice(64 * n, 64 * n + 64)
        for lanes in (slice(0, 128), slice(128, 256)):
            first_ref[rows, lanes] = (
                fc[n : n + 1, lanes] * w0 + fs[n : n + 1, lanes] * w1
            ).astype(BF16)
            last_ref[rows, lanes] = (bc[n : n + 1, lanes] * eye).astype(BF16)


def block_tables(w_first, w_second):
    vmem = pl.BlockSpec(memory_space=pltpu.VMEM)
    return pl.pallas_call(
        blocks_kernel,
        grid=(1,),
        in_specs=[vmem, vmem],
        out_specs=[
            pl.BlockSpec((1024, 256), lambda g: (0, 0)),
            pl.BlockSpec((1024, 256), lambda g: (0, 0)),
            pl.BlockSpec((256, 256), lambda g: (0, 0)),
        ],
        out_shape=[pltpu.HBM((n, 256), BF16) for n in (1024, 1024, 256)],
        scratch_shapes=[pltpu.VMEM((16, 256), F32)] * 3,
        cost_estimate=pl.CostEstimate(flops=2**21, bytes_accessed=2**20, transcendentals=0),
        compiler_params=pltpu.CompilerParams(vmem_limit_bytes=6 * MIB),
        name="block_tables",
    )(w_first, w_second)


def low_half(rows):
    return lax.broadcasted_iota(jnp.int32, (rows, 128), 1) < 64


def swap(v):
    return pltpu.roll(v, 64, 1)


def normed_halves(x, gain_ref):
    ones = jnp.ones((256, 128), BF16)
    mean = dot(x, ones) * (1.0 / 256.0)
    d0, d1 = x[:, :128].astype(F32) - mean, x[:, 128:].astype(F32) - mean
    square = d0 * d0 + d1 * d1
    coarse = square.astype(BF16)
    fine = (square - coarse.astype(F32)).astype(BF16)
    var = dot(jnp.concatenate([coarse, fine], axis=1), ones) * (1.0 / 256.0)
    scale = lax.rsqrt(var + 1e-05)
    return d0 * scale * gain_ref[:, :128], d1 * scale * gain_ref[:, 128:]


def norm_kernel(x_any, gain_any, out_any, x_all, packed, gain, in_sems, out_sems, gain_sem):
    fetches, sends = [], []
    for n in range(2):
        rows = slice(16 * n, 16 * n + 16)
        fetches.append(pltpu.make_async_copy(x_any.at[rows], x_all.at[rows], in_sems.at[n]))
        fetches[-1].start()
    gain_fetch = pltpu.make_async_copy(gain_any, gain, gain_sem)
    gain_fetch.start()
    gain_fetch.wait()
    for n in range(2):
        fetches[n].wait()
        x = x_all[16 * n : 16 * n + 16].reshape(1024, 256)
        halves = [half.astype(BF16) for half in normed_halves(x, gain)]
        for g in range(2):
            first = 4 * (2 * n + g)
            for t in range(4):
                lanes = slice(128 * t, 128 * t + 128)
                for m in range(2):
                    a = halves[m][512 * g + 64 * t : 512 * g + 64 * t + 64]
                    b = halves[m][512 * g + 64 * t + 256 : 512 * g + 64 * t + 320]
                    packed[first + 2 * m, :, lanes] = beside((a[:, :64], b[:, :64]))
                    packed[first + 2 * m + 1, :, lanes] = beside((a[:, 64:], b[:, 64:]))
        parts = slice(8 * n, 8 * n + 8)
        sends.append(pltpu.make_async_copy(packed.at[parts], out_any.at[parts], out_sems.at[n]))
        sends[-1].start()
    for send in sends:
        send.wait()


def home_norm_kernel(x_ref, gain_ref, out_ref):
    for m, half in enumerate(normed_halves(x_ref[...].reshape(512, 256), gain_ref)):
        out_ref[:, :, 128 * m : 128 * m + 128] = half.astype(BF16).reshape(8, 64, 128)


def home_norm(patches, gain):
    block = pl.BlockSpec((8, 64, 256), lambda g: (g, 0, 0))
    return pl.pallas_call(
        home_norm_kernel,
        grid=(4,),
        in_specs=[block, pl.BlockSpec((1, 256), lambda g: (0, 0))],
        out_specs=block,
        out_shape=pltpu.HBM((32, 64, 256), BF16),
        cost_estimate=pl.CostEstimate(flops=2**24, bytes_accessed=2**21, transcendentals=0),
        compiler_params=pltpu.CompilerParams(vmem_limit_bytes=12 * MIB),
        name="home_norm",
    )(remaining(patches), remaining(gain.reshape(1, 256)))


def norm_and_pack(patches, gain):
    return pl.pallas_call(
        norm_kernel,
        in_specs=[pl.BlockSpec(memory_space=pltpu.HBM)] * 2,
        out_specs=pl.BlockSpec(memory_space=pltpu.HBM),
        out_shape=pltpu.HBM((16, 64, 512), BF16),
        scratch_shapes=[
            pltpu.VMEM((32, 64, 256), BF16),
            pltpu.VMEM((16, 64, 512), BF16),
            pltpu.VMEM((1, 256), F32),
            pltpu.SemaphoreType.DMA((2,)),
            pltpu.SemaphoreType.DMA((2,)),
            pltpu.SemaphoreType.DMA,
        ],
        compiler_params=pltpu.CompilerParams(vmem_limit_bytes=16 * MIB),
        name="norm_pack",
    )(remaining(patches), remaining(gain.reshape(1, 256)))


def final_kernel(base_ref, home_ref, out_any, held, sems):
    low = low_half(64)
    sends = []
    for g in range(4):
        for t in range(4):
            lanes = slice(128 * t, 128 * t + 128)
            for m in range(2):
                u = home_ref[4 * g + 2 * m, :, lanes].astype(F32)
                v = home_ref[4 * g + 2 * m + 1, :, lanes].astype(F32)
                chans, row = slice(128 * m, 128 * m + 128), 8 * g + t
                even, odd = jnp.where(low, u, swap(v)), jnp.where(low, swap(u), v)
                held[row, :, chans] = (base_ref[row, :, chans] + even).astype(BF16)
                held[row + 4, :, chans] = (base_ref[row + 4, :, chans] + odd).astype(BF16)
        rows = slice(8 * g, 8 * g + 8)
        sends.append(pltpu.make_async_copy(held.at[rows], out_any.at[rows], sems.at[g]))
        sends[-1].start()
    for send in sends:
        send.wait()


def unpack_and_add(base, home):
    return pl.pallas_call(
        final_kernel,
        in_specs=[pl.BlockSpec(memory_space=pltpu.VMEM)] * 2,
        out_specs=pl.BlockSpec(memory_space=pltpu.HBM),
        out_shape=pltpu.HBM((32, 64, 256), BF16),
        scratch_shapes=[pltpu.VMEM((32, 64, 256), BF16), pltpu.SemaphoreType.DMA((4,))],
        compiler_params=pltpu.CompilerParams(vmem_limit_bytes=8 * MIB),
        name="unpack_add",
    )(resident(base), resident(home))


def dot(a, b):
    return jnp.dot(a, b, preferred_element_type=F32)


def resident(v):
    return pltpu.with_memory_space_constraint(v, pltpu.VMEM)


def remaining(v):
    return pltpu.with_memory_space_constraint(v, pltpu.HBM)


def stream_dot(table, operand, held, out, sems):
    copies = []
    for m, rows in enumerate((slice(0, 512), slice(512, 896), slice(896, 1024))):
        held[rows, :] = dot(table[rows, :], operand[...]).astype(BF16)
        copies.append(pltpu.make_async_copy(held.at[rows, :], out.at[rows, :], sems.at[m]))
        copies[-1].start()
    for copy in copies:
        copy.wait()


def columns_kernel(table_ref, x_ref, out_any, held, sems):
    stream_dot(table_ref, x_ref, held, out_any, sems)


def columns(table, x):
    return pl.pallas_call(
        columns_kernel,
        in_specs=[pl.BlockSpec(memory_space=pltpu.VMEM)] * 2,
        out_specs=pl.BlockSpec(memory_space=pltpu.HBM),
        out_shape=pltpu.HBM((1024, 512), BF16),
        scratch_shapes=[pltpu.VMEM((1024, 512), BF16), pltpu.SemaphoreType.DMA((3,))],
        cost_estimate=pl.CostEstimate(flops=2**30, bytes_accessed=2**21, transcendentals=0),
        compiler_params=pltpu.CompilerParams(vmem_limit_bytes=12 * MIB),
        name="along_columns",
    )(resident(table), resident(x))


def stencil_kernel(
    x_ref, normed_ref, top_ref, bottom_ref, left_ref, right_ref, taps_ref, out_ref,
    rows, side, left_sum, right_sum,
):
    def tap(i, j):
        return taps_ref[3 * i + j : 3 * i + j + 1, :]

    @pl.when(pl.program_id(0) == 0)
    def _():
        rows[0], rows[33] = top_ref[...], bottom_ref[...]
        rows[1:33] = normed_ref[...]
        for rim_ref, sum_ref, j in ((left_ref, left_sum, 0), (right_ref, right_sum, 2)):
            side[...] = rim_ref[...].astype(F32)
            sum_ref[...] = side[0:32] * tap(0, j) + side[1:33] * tap(1, j) + side[2:34] * tap(2, j)

    column = iota((64, 256), 0)

    def step(r, carry):
        h = 8 * pl.program_id(0) + r
        around = [rows[h + i].astype(F32) for i in range(3)]

        def part(j):
            return around[0] * tap(0, j) + around[1] * tap(1, j) + around[2] * tap(2, j)

        left = jnp.where(column == 0, left_sum[pl.ds(h, 1), :], pltpu.roll(part(0), 1, 0))
        right = jnp.where(column == 63, right_sum[pl.ds(h, 1), :], pltpu.roll(part(2), 63, 0))
        out_ref[h] = x_ref[r].astype(F32) + (left + part(1) + right)
        return carry

    lax.fori_loop(0, 8, step, 0)


def stencil(x, normed, top, bottom, left, right, taps):
    block = pl.BlockSpec((8, 64, 256), lambda g: (g, 0, 0))
    row = pl.BlockSpec((64, 256), lambda g: (0, 0))
    side = pl.BlockSpec((34, 256), lambda g: (0, 0))
    return pl.pallas_call(
        stencil_kernel,
        grid=(4,),
        in_specs=[
            block,
            pl.BlockSpec((32, 64, 256), lambda g: (0, 0, 0)),
            row, row, side, side,
            pl.BlockSpec((9, 256), lambda g: (0, 0)),
        ],
        out_specs=pl.BlockSpec(memory_space=pltpu.VMEM),
        out_shape=pltpu.VMEM((32, 64, 256), F32),
        scratch_shapes=[
            pltpu.VMEM((34, 64, 256), BF16),
            pltpu.VMEM((34, 256), F32),
            pltpu.VMEM((32, 256), F32),
            pltpu.VMEM((32, 256), F32),
        ],
        cost_estimate=pl.CostEstimate(flops=2**24, bytes_accessed=2**22, transcendentals=0),
        compiler_params=pltpu.CompilerParams(vmem_limit_bytes=12 * MIB),
        name="stencil",
    )(*[remaining(v) for v in (x, normed, top, bottom, left, right, taps)])


def butterfly(x, sign):
    re, im = [v[:, :128] for v in x], [v[:, 128:] for v in x]

    def pair(v):
        return v[0] + v[2], v[0] - v[2], v[1] + v[3], v[1] - v[3]

    (er, dr, fr, gr), (ei, di, fi, gi) = pair(re), pair(im)
    plus, minus = (dr - gi, di + gr), (dr + gi, di - gr)
    if sign < 0:
        plus, minus = minus, plus
    return (er + fr, ei + fi), plus, (er - fr, ei - fi), minus


def beside(pair):
    return jnp.concatenate(pair, axis=1)


def middle_kernel(
    z, fwd, cos_any, sin_any, first_any, second_any, last_any, inv_any, out_any,
    cos_ref, sin_ref, first, second, last, inv, held, done, sems, fetch_sems,
):
    fetches = []
    for n, (src, dst) in enumerate(
        (
            (cos_any, cos_ref),
            (sin_any, sin_ref),
            (first_any, first),
            (second_any, second),
            (last_any, last),
            (inv_any, inv),
        )
    ):
        fetches.append(pltpu.make_async_copy(src, dst, fetch_sems.at[n]))
        fetches[-1].start()
    rows = 512 // CHUNKS
    groups = 8 // CHUNKS
    shape = (groups, 4, 16, 128)
    for m in range(CHUNKS):
        u = dot(fwd[2 * rows * m : 2 * rows * (m + 1), :], z[...])
        if m == 0:
            for fetch in fetches[:4]:
                fetch.wait()

        def twiddles(t):
            part = (slice(16 * groups * m, 16 * groups * (m + 1)), slice(128 * t, 128 * t + 128))
            return [ref[part].reshape(groups, 1, 16, 128) for ref in (cos_ref, sin_ref)]

        parts = []
        for t in range(4):
            ur = u[:rows, 128 * t : 128 * t + 128].reshape(shape)
            ui = u[rows:, 128 * t : 128 * t + 128].reshape(shape)
            c, s = twiddles(t)
            vr, vi = (ur * c + ui * s).reshape(rows, 128), (ui * c - ur * s).reshape(rows, 128)
            parts.append(dot(beside((vr.astype(BF16), vi.astype(BF16))), first[256 * t : 256 * t + 256, :]))
        kept = []
        for part in butterfly(parts, -1):
            v = dot(jnp.tanh(beside(part)).astype(BF16), second[...])
            kept.append(jnp.where(v > 0.25, v - 0.25, jnp.where(v < -0.25, v + 0.25, 0.0 * v)))
        if m == 0:
            fetches[4].wait()
        for t, part in enumerate(butterfly(kept, 1)):
            y = dot(beside(part).astype(BF16), last[256 * t : 256 * t + 256, :])
            yr, yi = y[:, :128].reshape(shape), y[:, 128:].reshape(shape)
            c, s = twiddles(t)
            lanes = slice(128 * t, 128 * t + 128)
            held[2 * rows * m : 2 * rows * m + rows, lanes] = (
                (yr * c - yi * s).astype(BF16).reshape(rows, 128)
            )
            held[2 * rows * m + rows : 2 * rows * (m + 1), lanes] = (
                (yi * c + yr * s).astype(BF16).reshape(rows, 128)
            )
    fetches[5].wait()
    stream_dot(inv, held, done, out_any, sems)


def middle(z, fwd, cos, sin, first, second, last, inv):
    vmem, hbm = pl.BlockSpec(memory_space=pltpu.VMEM), pl.BlockSpec(memory_space=pltpu.HBM)
    return pl.pallas_call(
        middle_kernel,
        in_specs=[vmem] * 2 + [hbm] * 6,
        out_specs=hbm,
        out_shape=pltpu.HBM((1024, 512), BF16),
        scratch_shapes=[
            pltpu.VMEM((128, 512), F32),
            pltpu.VMEM((128, 512), F32),
            pltpu.VMEM((1024, 256), BF16),
            pltpu.VMEM((256, 256), BF16),
            pltpu.VMEM((1024, 256), BF16),
            pltpu.VMEM((1024, 1024), BF16),
            pltpu.VMEM((1024, 512), BF16),
            pltpu.VMEM((1024, 512), BF16),
            pltpu.SemaphoreType.DMA((3,)),
            pltpu.SemaphoreType.DMA((6,)),
        ],
        cost_estimate=pl.CostEstimate(flops=3 * 2**30, bytes_accessed=2**21, transcendentals=2**19),
        compiler_params=pltpu.CompilerParams(vmem_limit_bytes=24 * MIB),
        name="filter_rows",
    )(
        resident(z), resident(fwd), *[remaining(v) for v in (cos, sin, first, second, last, inv)]
    )


def local(patches, norm_gain, w_first, w_second, depth_kernel):
    packed = norm_and_pack(patches, norm_gain)
    lines = lax.all_to_all(packed, ("yl", "x"), 0, 0, tiled=True).reshape(1024, 512)

    fwd_w = table(pltpu.VMEM, forward_columns_phases)
    inv_w = table(pltpu.VMEM, backward_columns_phases)
    inv_h = table(pltpu.HBM, backward_rows_phases)
    first, last, second = block_tables(w_first, w_second)
    fwd_h, cos, sin = table(pltpu.VMEM, forward_rows_phases, True, (second, inv_h))

    def neighbours(first, last, axis):
        n = lax.axis_size(axis)
        before = lax.ppermute(last, axis, [(i, (i + 1) % n) for i in range(n)])
        after = lax.ppermute(first, axis, [((i + 1) % n, i) for i in range(n)])
        return before, after

    normed = home_norm(patches, norm_gain)
    lines, normed = lax.optimization_barrier((lines, normed))

    freqs = columns(fwd_w, lines)
    whole = lax.all_to_all(freqs.reshape(128, 8, 512), ("row", "yl"), 0, 0, tiled=True)
    top, bottom = neighbours(normed[0], normed[31], "row")

    filtered = middle(whole.reshape(1024, 512), fwd_h, cos, sin, first, second, last, inv_h)
    filtered, top, bottom, normed = lax.optimization_barrier((filtered, top, bottom, normed))
    back = lax.all_to_all(filtered.reshape(128, 8, 512), ("row", "yl"), 0, 0, tiled=True)
    sides = [
        jnp.concatenate([top[w : w + 1], normed[:, w], bottom[w : w + 1]], axis=0) for w in (0, 63)
    ]
    left, right = neighbours(sides[0], sides[1], ("yl", "x"))
    back, left, right = lax.optimization_barrier((back, left, right))

    spectral = columns(inv_w, back.reshape(1024, 512))
    spectral, left, right = lax.optimization_barrier((spectral, left, right))
    home = lax.all_to_all(spectral.reshape(16, 64, 512), ("yl", "x"), 0, 0, tiled=True)
    base = stencil(patches, normed, top, bottom, left, right, depth_kernel.reshape(9, 256))
    return unpack_and_add(base, home)


def solution(mesh):
    fine = Mesh(np.asarray(mesh.devices).reshape(32, 4, 4), ("row", "yl", "x"))
    return jax.shard_map(
        local,
        mesh=fine,
        in_specs=(P("row", ("yl", "x"), None), P(), P(), P(), P()),
        out_specs=P("row", ("yl", "x"), None),
        check_vma=False,
    )
```

```python
import functools
import math

import jax
import jax.numpy as jnp
import numpy as np
from jax import lax
from jax.experimental import pallas as pl
from jax.experimental.pallas import tpu as pltpu
from jax.sharding import Mesh
from jax.sharding import PartitionSpec as P

TURN = 1024
CHUNKS = 2
MIB = 1024 * 1024
F32 = jnp.float32
BF16 = jnp.bfloat16


def iota(shape, dim):
    return lax.broadcasted_iota(jnp.int32, shape, dim)


def digit(idx, shift, bits):
    return (idx >> shift) & ((1 << bits) - 1)


def cos_sin(idx):
    idx = idx & (TURN - 1)
    quarter = (idx + TURN // 8) >> 8
    x = (idx - (quarter << 8)).astype(F32) * (2.0 * math.pi / TURN)
    y = x * x
    s = x * (1.0 + y * (-1.0 / 6 + y * (1.0 / 120 + y * (-1.0 / 5040 + y * (1.0 / 362880)))))
    c = 1.0 + y * (-1.0 / 2 + y * (1.0 / 24 + y * (-1.0 / 720 + y * (1.0 / 40320))))
    odd = (quarter & 1) == 1
    cos, sin = jnp.where(odd, s, c), jnp.where(odd, c, s)
    turned = (quarter + 1) & 3
    cos = jnp.where(turned >= 2, -cos, cos)
    sin = jnp.where((quarter & 3) >= 2, -sin, sin)
    return cos, sin


SCALE = 1.0 / 32.0


def forward_columns_phases():
    a, b = iota((16, 1024), 0), iota((64, 1024), 0)
    w = iota((64, 1024), 1)
    k = 4 * digit(b, 3, 3) + digit(b, 0, 2)
    return 32 * a * w[:16], k * w + 256 * digit(b, 2, 1), SCALE


def backward_columns_phases():
    a, b, lane = iota((16, 1024), 0), iota((64, 1024), 0), iota((64, 1024), 1)
    k = 4 * (lane >> 3) + digit(lane, 0, 2)
    weight = jnp.where(k == 0, SCALE, 2.0 * SCALE)
    return 64 * a * k[:16], b * k + 256 * digit(lane, 2, 1), weight


def forward_rows_phases():
    a, b, lane = iota((16, 1024), 0), iota((64, 1024), 0), iota((64, 1024), 1)
    qh = 4 * digit(a, 3, 1) + digit(a, 0, 2)
    p, ri = lane >> 3, digit(lane, 2, 1)
    ia = 128 * qh * p[:16] + 256 * (digit(a, 2, 1) - ri[:16])
    weight = jnp.where(digit(b, 4, 2) == digit(lane, 0, 2), SCALE, 0.0)
    return ia, 8 * digit(b, 0, 4) * p, weight


def backward_rows_phases():
    a, b, lane = iota((16, 1024), 0), iota((64, 1024), 0), iota((64, 1024), 1)
    q0 = 16 * (4 * digit(lane, 9, 1) + digit(lane, 6, 2)) + digit(lane, 0, 4)
    ro = digit(lane, 8, 1)
    weight = jnp.where(digit(b, 0, 2) == digit(lane, 4, 2), SCALE, 0.0)
    return 64 * a * q0[:16], 8 * digit(b, 3, 3) * q0 + 256 * (ro - digit(b, 2, 1)), weight


def table_kernel(phases, with_twiddles, stay, waited, *refs):
    refs = refs[waited:]
    out_ref, (ec, es, fc, fs) = refs[0], refs[-4:]
    steps = 16 if stay else 4

    @pl.when(pl.program_id(0) == 0)
    def _():
        ia, ib, weight = phases()
        ec[...], es[...] = cos_sin(ia)
        c, s = cos_sin(ib)
        fc[...], fs[...] = c * weight, s * weight
        if with_twiddles:
            lane = iota((128, 512), 1)
            angle = iota((128, 512), 0) * ((lane >> 7) + 4 * digit(lane, 6, 1))
            refs[1][...], refs[2][...] = cos_sin(angle)

    first = 0 if stay else steps * pl.program_id(0)

    def step(a, carry):
        row = pl.ds(first + a, 1)
        out_ref[pl.ds(pl.multiple_of(64 * a, 64), 64), :] = (
            ec[row, :] * fc[...] - es[row, :] * fs[...]
        ).astype(BF16)
        return carry

    lax.fori_loop(0, steps, step, 0)


def table(space, phases, with_twiddles=False, after=()):
    stay = space == pltpu.VMEM
    whole = pl.BlockSpec(memory_space=pltpu.VMEM)
    twiddle_spec = pl.BlockSpec((128, 512), lambda g: (0, 0))
    out = pl.pallas_call(
        functools.partial(table_kernel, phases, with_twiddles, stay, len(after)),
        grid=(1,) if stay else (4,),
        in_specs=[pl.BlockSpec(memory_space=pltpu.HBM)] * len(after),
        out_specs=[whole if stay else pl.BlockSpec((256, 1024), lambda g: (g, 0))]
        + [twiddle_spec] * (2 * with_twiddles),
        out_shape=[space((1024, 1024), BF16)] + [pltpu.HBM((128, 512), F32)] * (2 * with_twiddles),
        scratch_shapes=[pltpu.VMEM((n, 1024), F32) for n in (16, 16, 64, 64)],
        cost_estimate=pl.CostEstimate(flops=2**23, bytes_accessed=2**21, transcendentals=0),
        compiler_params=pltpu.CompilerParams(vmem_limit_bytes=6 * MIB),
        name=phases.__name__,
    )(*[remaining(v) for v in after])
    return out if with_twiddles else out[0]


def blocks_kernel(first_w, second_w, first_ref, last_ref, second_ref, fc, fs, bc):
    block = lax.axis_index("x")
    low = low_half(64)
    a, lane = iota((16, 256), 0), iota((16, 256), 1)
    t, ri, row_e = a >> 2, digit(a, 1, 1), a & 1
    ro, lane_e = lane >> 7, digit(lane, 6, 1)
    fc[...], fs[...] = cos_sin(128 * lane_e * (t + 4 * row_e) + 256 * (ro - ri))
    bc[...], _unused = cos_sin(128 * row_e * (t + 4 * lane_e) - 256 * (ro - ri))

    def twice(ref, n):
        w = ref[n, block].astype(F32)
        return jnp.concatenate([w, w], axis=1)

    w0, w1 = twice(second_w, 0), twice(second_w, 1)
    zero = jnp.zeros_like(w0)
    for half in range(2):
        def own(v):
            return (jnp.where(low, v, zero) if half == 0 else jnp.where(low, zero, v)).astype(BF16)

        re, im = slice(64 * half, 64 * half + 64), slice(128 + 64 * half, 192 + 64 * half)
        second_ref[re, :128], second_ref[re, 128:] = own(w0), own(w1)
        second_ref[im, :128], second_ref[im, 128:] = own(-w1), own(w0)

    w0, w1 = twice(first_w, 0), twice(first_w, 1)
    eye = jnp.where(iota((64, 128), 0) == (iota((64, 128), 1) & 63), 1.0, 0.0)
    for n in range(16):
        rows = slice(64 * n, 64 * n + 64)
        for lanes in (slice(0, 128), slice(128, 256)):
            first_ref[rows, lanes] = (
                fc[n : n + 1, lanes] * w0 + fs[n : n + 1, lanes] * w1
            ).astype(BF16)
            last_ref[rows, lanes] = (bc[n : n + 1, lanes] * eye).astype(BF16)


def block_tables(w_first, w_second):
    vmem = pl.BlockSpec(memory_space=pltpu.VMEM)
    return pl.pallas_call(
        blocks_kernel,
        grid=(1,),
        in_specs=[vmem, vmem],
        out_specs=[
            pl.BlockSpec((1024, 256), lambda g: (0, 0)),
            pl.BlockSpec((1024, 256), lambda g: (0, 0)),
            pl.BlockSpec((256, 256), lambda g: (0, 0)),
        ],
        out_shape=[pltpu.HBM((n, 256), BF16) for n in (1024, 1024, 256)],
        scratch_shapes=[pltpu.VMEM((16, 256), F32)] * 3,
        cost_estimate=pl.CostEstimate(flops=2**21, bytes_accessed=2**20, transcendentals=0),
        compiler_params=pltpu.CompilerParams(vmem_limit_bytes=6 * MIB),
        name="block_tables",
    )(w_first, w_second)


def low_half(rows):
    return lax.broadcasted_iota(jnp.int32, (rows, 128), 1) < 64


def swap(v):
    return pltpu.roll(v, 64, 1)


def normed_halves(x, gain_ref):
    ones = jnp.ones((256, 128), BF16)
    mean = dot(x, ones) * (1.0 / 256.0)
    d0, d1 = x[:, :128].astype(F32) - mean, x[:, 128:].astype(F32) - mean
    square = d0 * d0 + d1 * d1
    coarse = square.astype(BF16)
    fine = (square - coarse.astype(F32)).astype(BF16)
    var = dot(jnp.concatenate([coarse, fine], axis=1), ones) * (1.0 / 256.0)
    scale = lax.rsqrt(var + 1e-05)
    return d0 * scale * gain_ref[:, :128], d1 * scale * gain_ref[:, 128:]


def norm_kernel(x_any, gain_any, out_any, x_all, packed, gain, in_sems, out_sems, gain_sem):
    fetches, sends = [], []
    for n in range(2):
        rows = slice(16 * n, 16 * n + 16)
        fetches.append(pltpu.make_async_copy(x_any.at[rows], x_all.at[rows], in_sems.at[n]))
        fetches[-1].start()
    gain_fetch = pltpu.make_async_copy(gain_any, gain, gain_sem)
    gain_fetch.start()
    gain_fetch.wait()
    for n in range(2):
        fetches[n].wait()
        x = x_all[16 * n : 16 * n + 16].reshape(1024, 256)
        halves = [half.astype(BF16) for half in normed_halves(x, gain)]
        for g in range(2):
            first = 4 * (2 * n + g)
            for t in range(4):
                lanes = slice(128 * t, 128 * t + 128)
                for m in range(2):
                    a = halves[m][512 * g + 64 * t : 512 * g + 64 * t + 64]
                    b = halves[m][512 * g + 64 * t + 256 : 512 * g + 64 * t + 320]
                    packed[first + 2 * m, :, lanes] = beside((a[:, :64], b[:, :64]))
                    packed[first + 2 * m + 1, :, lanes] = beside((a[:, 64:], b[:, 64:]))
        parts = slice(8 * n, 8 * n + 8)
        sends.append(pltpu.make_async_copy(packed.at[parts], out_any.at[parts], out_sems.at[n]))
        sends[-1].start()
    for send in sends:
        send.wait()


def home_norm_kernel(x_ref, gain_ref, out_ref):
    for m, half in enumerate(normed_halves(x_ref[...].reshape(512, 256), gain_ref)):
        out_ref[:, :, 128 * m : 128 * m + 128] = half.astype(BF16).reshape(8, 64, 128)


def home_norm(patches, gain):
    block = pl.BlockSpec((8, 64, 256), lambda g: (g, 0, 0))
    return pl.pallas_call(
        home_norm_kernel,
        grid=(4,),
        in_specs=[block, pl.BlockSpec((1, 256), lambda g: (0, 0))],
        out_specs=block,
        out_shape=pltpu.HBM((32, 64, 256), BF16),
        cost_estimate=pl.CostEstimate(flops=2**24, bytes_accessed=2**21, transcendentals=0),
        compiler_params=pltpu.CompilerParams(vmem_limit_bytes=12 * MIB),
        name="home_norm",
    )(remaining(patches), remaining(gain.reshape(1, 256)))


def norm_and_pack(patches, gain):
    return pl.pallas_call(
        norm_kernel,
        in_specs=[pl.BlockSpec(memory_space=pltpu.HBM)] * 2,
        out_specs=pl.BlockSpec(memory_space=pltpu.HBM),
        out_shape=pltpu.HBM((16, 64, 512), BF16),
        scratch_shapes=[
            pltpu.VMEM((32, 64, 256), BF16),
            pltpu.VMEM((16, 64, 512), BF16),
            pltpu.VMEM((1, 256), F32),
            pltpu.SemaphoreType.DMA((2,)),
            pltpu.SemaphoreType.DMA((2,)),
            pltpu.SemaphoreType.DMA,
        ],
        compiler_params=pltpu.CompilerParams(vmem_limit_bytes=16 * MIB),
        name="norm_pack",
    )(remaining(patches), remaining(gain.reshape(1, 256)))


def final_kernel(base_ref, home_ref, out_any, held, sems):
    low = low_half(64)
    sends = []
    for g in range(4):
        for t in range(4):
            lanes = slice(128 * t, 128 * t + 128)
            for m in range(2):
                u = home_ref[4 * g + 2 * m, :, lanes].astype(F32)
                v = home_ref[4 * g + 2 * m + 1, :, lanes].astype(F32)
                chans, row = slice(128 * m, 128 * m + 128), 8 * g + t
                even, odd = jnp.where(low, u, swap(v)), jnp.where(low, swap(u), v)
                held[row, :, chans] = (base_ref[row, :, chans] + even).astype(BF16)
                held[row + 4, :, chans] = (base_ref[row + 4, :, chans] + odd).astype(BF16)
        rows = slice(8 * g, 8 * g + 8)
        sends.append(pltpu.make_async_copy(held.at[rows], out_any.at[rows], sems.at[g]))
        sends[-1].start()
    for send in sends:
        send.wait()


def unpack_and_add(base, home):
    return pl.pallas_call(
        final_kernel,
        in_specs=[pl.BlockSpec(memory_space=pltpu.VMEM)] * 2,
        out_specs=pl.BlockSpec(memory_space=pltpu.HBM),
        out_shape=pltpu.HBM((32, 64, 256), BF16),
        scratch_shapes=[pltpu.VMEM((32, 64, 256), BF16), pltpu.SemaphoreType.DMA((4,))],
        compiler_params=pltpu.CompilerParams(vmem_limit_bytes=8 * MIB),
        name="unpack_add",
    )(resident(base), resident(home))


def dot(a, b):
    return jnp.dot(a, b, preferred_element_type=F32)


def resident(v):
    return pltpu.with_memory_space_constraint(v, pltpu.VMEM)


def remaining(v):
    return pltpu.with_memory_space_constraint(v, pltpu.HBM)


def stream_dot(table, operand, held, out, sems):
    copies = []
    for m, rows in enumerate((slice(0, 512), slice(512, 896), slice(896, 1024))):
        held[rows, :] = dot(table[rows, :], operand[...]).astype(BF16)
        copies.append(pltpu.make_async_copy(held.at[rows, :], out.at[rows, :], sems.at[m]))
        copies[-1].start()
    for copy in copies:
        copy.wait()


def columns_kernel(table_ref, x_ref, out_any, held, sems):
    stream_dot(table_ref, x_ref, held, out_any, sems)


def columns(table, x):
    return pl.pallas_call(
        columns_kernel,
        in_specs=[pl.BlockSpec(memory_space=pltpu.VMEM)] * 2,
        out_specs=pl.BlockSpec(memory_space=pltpu.HBM),
        out_shape=pltpu.HBM((1024, 512), BF16),
        scratch_shapes=[pltpu.VMEM((1024, 512), BF16), pltpu.SemaphoreType.DMA((3,))],
        cost_estimate=pl.CostEstimate(flops=2**30, bytes_accessed=2**21, transcendentals=0),
        compiler_params=pltpu.CompilerParams(vmem_limit_bytes=12 * MIB),
        name="along_columns",
    )(resident(table), resident(x))


def stencil_kernel(
    x_ref, normed_ref, top_ref, bottom_ref, left_ref, right_ref, taps_ref, out_ref,
    rows, side, left_sum, right_sum,
):
    def tap(i, j):
        return taps_ref[3 * i + j : 3 * i + j + 1, :]

    @pl.when(pl.program_id(0) == 0)
    def _():
        rows[0], rows[33] = top_ref[...], bottom_ref[...]
        rows[1:33] = normed_ref[...]
        for rim_ref, sum_ref, j in ((left_ref, left_sum, 0), (right_ref, right_sum, 2)):
            side[...] = rim_ref[...].astype(F32)
            sum_ref[...] = side[0:32] * tap(0, j) + side[1:33] * tap(1, j) + side[2:34] * tap(2, j)

    column = iota((64, 256), 0)

    def step(r, carry):
        h = 8 * pl.program_id(0) + r
        around = [rows[h + i].astype(F32) for i in range(3)]

        def part(j):
            return around[0] * tap(0, j) + around[1] * tap(1, j) + around[2] * tap(2, j)

        left = jnp.where(column == 0, left_sum[pl.ds(h, 1), :], pltpu.roll(part(0), 1, 0))
        right = jnp.where(column == 63, right_sum[pl.ds(h, 1), :], pltpu.roll(part(2), 63, 0))
        out_ref[h] = x_ref[r].astype(F32) + (left + part(1) + right)
        return carry

    lax.fori_loop(0, 8, step, 0)


def stencil(x, normed, top, bottom, left, right, taps):
    block = pl.BlockSpec((8, 64, 256), lambda g: (g, 0, 0))
    row = pl.BlockSpec((64, 256), lambda g: (0, 0))
    side = pl.BlockSpec((34, 256), lambda g: (0, 0))
    return pl.pallas_call(
        stencil_kernel,
        grid=(4,),
        in_specs=[
            block,
            pl.BlockSpec((32, 64, 256), lambda g: (0, 0, 0)),
            row, row, side, side,
            pl.BlockSpec((9, 256), lambda g: (0, 0)),
        ],
        out_specs=pl.BlockSpec(memory_space=pltpu.VMEM),
        out_shape=pltpu.VMEM((32, 64, 256), F32),
        scratch_shapes=[
            pltpu.VMEM((34, 64, 256), BF16),
            pltpu.VMEM((34, 256), F32),
            pltpu.VMEM((32, 256), F32),
            pltpu.VMEM((32, 256), F32),
        ],
        cost_estimate=pl.CostEstimate(flops=2**24, bytes_accessed=2**22, transcendentals=0),
        compiler_params=pltpu.CompilerParams(vmem_limit_bytes=12 * MIB),
        name="stencil",
    )(*[remaining(v) for v in (x, normed, top, bottom, left, right, taps)])


def butterfly(x, sign):
    re, im = [v[:, :128] for v in x], [v[:, 128:] for v in x]

    def pair(v):
        return v[0] + v[2], v[0] - v[2], v[1] + v[3], v[1] - v[3]

    (er, dr, fr, gr), (ei, di, fi, gi) = pair(re), pair(im)
    plus, minus = (dr - gi, di + gr), (dr + gi, di - gr)
    if sign < 0:
        plus, minus = minus, plus
    return (er + fr, ei + fi), plus, (er - fr, ei - fi), minus


def beside(pair):
    return jnp.concatenate(pair, axis=1)


def middle_kernel(
    z, fwd, cos_any, sin_any, first_any, second_any, last_any, inv_any, out_any,
    cos_ref, sin_ref, first, second, last, inv, held, done, sems, fetch_sems,
):
    fetches = []
    for n, (src, dst) in enumerate(
        (
            (cos_any, cos_ref),
            (sin_any, sin_ref),
            (first_any, first),
            (second_any, second),
            (last_any, last),
            (inv_any, inv),
        )
    ):
        fetches.append(pltpu.make_async_copy(src, dst, fetch_sems.at[n]))
        fetches[-1].start()
    rows = 512 // CHUNKS
    groups = 8 // CHUNKS
    shape = (groups, 4, 16, 128)
    for m in range(CHUNKS):
        u = dot(fwd[2 * rows * m : 2 * rows * (m + 1), :], z[...])
        if m == 0:
            for fetch in fetches[:4]:
                fetch.wait()

        def twiddles(t):
            part = (slice(16 * groups * m, 16 * groups * (m + 1)), slice(128 * t, 128 * t + 128))
            return [ref[part].reshape(groups, 1, 16, 128) for ref in (cos_ref, sin_ref)]

        parts = []
        for t in range(4):
            ur = u[:rows, 128 * t : 128 * t + 128].reshape(shape)
            ui = u[rows:, 128 * t : 128 * t + 128].reshape(shape)
            c, s = twiddles(t)
            vr, vi = (ur * c + ui * s).reshape(rows, 128), (ui * c - ur * s).reshape(rows, 128)
            parts.append(dot(beside((vr.astype(BF16), vi.astype(BF16))), first[256 * t : 256 * t + 256, :]))
        kept = []
        for part in butterfly(parts, -1):
            v = dot(jnp.tanh(beside(part)).astype(BF16), second[...])
            kept.append(jnp.where(v > 0.25, v - 0.25, jnp.where(v < -0.25, v + 0.25, 0.0 * v)))
        if m == 0:
            fetches[4].wait()
        for t, part in enumerate(butterfly(kept, 1)):
            y = dot(beside(part).astype(BF16), last[256 * t : 256 * t + 256, :])
            yr, yi = y[:, :128].reshape(shape), y[:, 128:].reshape(shape)
            c, s = twiddles(t)
            lanes = slice(128 * t, 128 * t + 128)
            held[2 * rows * m : 2 * rows * m + rows, lanes] = (
                (yr * c - yi * s).astype(BF16).reshape(rows, 128)
            )
            held[2 * rows * m + rows : 2 * rows * (m + 1), lanes] = (
                (yi * c + yr * s).astype(BF16).reshape(rows, 128)
            )
    fetches[5].wait()
    stream_dot(inv, held, done, out_any, sems)


def middle(z, fwd, cos, sin, first, second, last, inv):
    vmem, hbm = pl.BlockSpec(memory_space=pltpu.VMEM), pl.BlockSpec(memory_space=pltpu.HBM)
    return pl.pallas_call(
        middle_kernel,
        in_specs=[vmem] * 2 + [hbm] * 6,
        out_specs=hbm,
        out_shape=pltpu.HBM((1024, 512), BF16),
        scratch_shapes=[
            pltpu.VMEM((128, 512), F32),
            pltpu.VMEM((128, 512), F32),
            pltpu.VMEM((1024, 256), BF16),
            pltpu.VMEM((256, 256), BF16),
            pltpu.VMEM((1024, 256), BF16),
            pltpu.VMEM((1024, 1024), BF16),
            pltpu.VMEM((1024, 512), BF16),
            pltpu.VMEM((1024, 512), BF16),
            pltpu.SemaphoreType.DMA((3,)),
            pltpu.SemaphoreType.DMA((6,)),
        ],
        cost_estimate=pl.CostEstimate(flops=3 * 2**30, bytes_accessed=2**21, transcendentals=2**19),
        compiler_params=pltpu.CompilerParams(vmem_limit_bytes=24 * MIB),
        name="filter_rows",
    )(
        resident(z), resident(fwd), *[remaining(v) for v in (cos, sin, first, second, last, inv)]
    )


def local(patches, norm_gain, w_first, w_second, depth_kernel):
    packed = norm_and_pack(patches, norm_gain)
    lines = lax.all_to_all(packed, ("yl", "x"), 0, 0, tiled=True).reshape(1024, 512)

    fwd_w = table(pltpu.VMEM, forward_columns_phases)
    inv_w = table(pltpu.VMEM, backward_columns_phases)
    inv_h = table(pltpu.HBM, backward_rows_phases)
    first, last, second = block_tables(w_first, w_second)
    fwd_h, cos, sin = table(pltpu.VMEM, forward_rows_phases, True, (second, inv_h))

    def neighbours(first, last, axis):
        n = lax.axis_size(axis)
        before = lax.ppermute(last, axis, [(i, (i + 1) % n) for i in range(n)])
        after = lax.ppermute(first, axis, [((i + 1) % n, i) for i in range(n)])
        return before, after

    lines, here = lax.optimization_barrier((lines, patches))
    normed = home_norm(here, norm_gain)

    freqs = columns(fwd_w, lines)
    whole = lax.all_to_all(freqs.reshape(128, 8, 512), ("row", "yl"), 0, 0, tiled=True)
    top, bottom = neighbours(normed[0], normed[31], "row")

    filtered = middle(whole.reshape(1024, 512), fwd_h, cos, sin, first, second, last, inv_h)
    filtered, top, bottom, normed = lax.optimization_barrier((filtered, top, bottom, normed))
    back = lax.all_to_all(filtered.reshape(128, 8, 512), ("row", "yl"), 0, 0, tiled=True)
    sides = [
        jnp.concatenate([top[w : w + 1], normed[:, w], bottom[w : w + 1]], axis=0) for w in (0, 63)
    ]
    left, right = neighbours(sides[0], sides[1], ("yl", "x"))
    back, left, right = lax.optimization_barrier((back, left, right))

    spectral = columns(inv_w, back.reshape(1024, 512))
    spectral, left, right = lax.optimization_barrier((spectral, left, right))
    home = lax.all_to_all(spectral.reshape(16, 64, 512), ("yl", "x"), 0, 0, tiled=True)
    base = stencil(patches, normed, top, bottom, left, right, depth_kernel.reshape(9, 256))
    return unpack_and_add(base, home)


def solution(mesh):
    fine = Mesh(np.asarray(mesh.devices).reshape(32, 4, 4), ("row", "yl", "x"))
    return jax.shard_map(
        local,
        mesh=fine,
        in_specs=(P("row", ("yl", "x"), None), P(), P(), P(), P()),
        out_specs=P("row", ("yl", "x"), None),
        check_vma=False,
    )
```

```python
import functools
import math

import jax
import jax.numpy as jnp
import numpy as np
from jax import lax
from jax.experimental import pallas as pl
from jax.experimental.pallas import tpu as pltpu
from jax.sharding import Mesh
from jax.sharding import PartitionSpec as P

TURN = 1024
CHUNKS = 2
MIB = 1024 * 1024
F32 = jnp.float32
BF16 = jnp.bfloat16


def iota(shape, dim):
    return lax.broadcasted_iota(jnp.int32, shape, dim)


def digit(idx, shift, bits):
    return (idx >> shift) & ((1 << bits) - 1)


def cos_sin(idx):
    idx = idx & (TURN - 1)
    quarter = (idx + TURN // 8) >> 8
    x = (idx - (quarter << 8)).astype(F32) * (2.0 * math.pi / TURN)
    y = x * x
    s = x * (1.0 + y * (-1.0 / 6 + y * (1.0 / 120 + y * (-1.0 / 5040 + y * (1.0 / 362880)))))
    c = 1.0 + y * (-1.0 / 2 + y * (1.0 / 24 + y * (-1.0 / 720 + y * (1.0 / 40320))))
    odd = (quarter & 1) == 1
    cos, sin = jnp.where(odd, s, c), jnp.where(odd, c, s)
    turned = (quarter + 1) & 3
    cos = jnp.where(turned >= 2, -cos, cos)
    sin = jnp.where((quarter & 3) >= 2, -sin, sin)
    return cos, sin


SCALE = 1.0 / 32.0


def forward_columns_phases():
    a, b = iota((16, 1024), 0), iota((64, 1024), 0)
    w = iota((64, 1024), 1)
    k = 4 * digit(b, 3, 3) + digit(b, 0, 2)
    return 32 * a * w[:16], k * w + 256 * digit(b, 2, 1), SCALE


def backward_columns_phases():
    a, b, lane = iota((16, 1024), 0), iota((64, 1024), 0), iota((64, 1024), 1)
    k = 4 * (lane >> 3) + digit(lane, 0, 2)
    weight = jnp.where(k == 0, SCALE, 2.0 * SCALE)
    return 64 * a * k[:16], b * k + 256 * digit(lane, 2, 1), weight


def forward_rows_phases():
    a, b, lane = iota((16, 1024), 0), iota((64, 1024), 0), iota((64, 1024), 1)
    qh = 4 * digit(a, 3, 1) + digit(a, 0, 2)
    p, ri = lane >> 3, digit(lane, 2, 1)
    ia = 128 * qh * p[:16] + 256 * (digit(a, 2, 1) - ri[:16])
    weight = jnp.where(digit(b, 4, 2) == digit(lane, 0, 2), SCALE, 0.0)
    return ia, 8 * digit(b, 0, 4) * p, weight


def backward_rows_phases():
    a, b, lane = iota((16, 1024), 0), iota((64, 1024), 0), iota((64, 1024), 1)
    q0 = 16 * (4 * digit(lane, 9, 1) + digit(lane, 6, 2)) + digit(lane, 0, 4)
    ro = digit(lane, 8, 1)
    weight = jnp.where(digit(b, 0, 2) == digit(lane, 4, 2), SCALE, 0.0)
    return 64 * a * q0[:16], 8 * digit(b, 3, 3) * q0 + 256 * (ro - digit(b, 2, 1)), weight


def table_kernel(phases, stay, waited, *refs):
    refs = refs[waited:]
    out_ref, (ec, es, fc, fs) = refs[0], refs[-4:]
    steps = 16 if stay else 4

    @pl.when(pl.program_id(0) == 0)
    def _():
        ia, ib, weight = phases()
        ec[...], es[...] = cos_sin(ia)
        c, s = cos_sin(ib)
        fc[...], fs[...] = c * weight, s * weight

    first = 0 if stay else steps * pl.program_id(0)

    def step(a, carry):
        row = pl.ds(first + a, 1)
        out_ref[pl.ds(pl.multiple_of(64 * a, 64), 64), :] = (
            ec[row, :] * fc[...] - es[row, :] * fs[...]
        ).astype(BF16)
        return carry

    lax.fori_loop(0, steps, step, 0)


def table(space, phases, after=()):
    stay = space == pltpu.VMEM
    whole = pl.BlockSpec(memory_space=pltpu.VMEM)
    return pl.pallas_call(
        functools.partial(table_kernel, phases, stay, len(after)),
        grid=(1,) if stay else (4,),
        in_specs=[pl.BlockSpec(memory_space=pltpu.HBM)] * len(after),
        out_specs=whole if stay else pl.BlockSpec((256, 1024), lambda g: (g, 0)),
        out_shape=space((1024, 1024), BF16),
        scratch_shapes=[pltpu.VMEM((n, 1024), F32) for n in (16, 16, 64, 64)],
        cost_estimate=pl.CostEstimate(flops=2**23, bytes_accessed=2**21, transcendentals=0),
        compiler_params=pltpu.CompilerParams(vmem_limit_bytes=6 * MIB),
        name=phases.__name__,
    )(*[remaining(v) for v in after])


def blocks_kernel(first_w, second_w, first_ref, last_ref, second_ref, fc, fs, bc):
    block = lax.axis_index("x")
    low = low_half(64)
    a, lane = iota((16, 256), 0), iota((16, 256), 1)
    t, ri, row_e = a >> 2, digit(a, 1, 1), a & 1
    ro, lane_e = lane >> 7, digit(lane, 6, 1)
    fc[...], fs[...] = cos_sin(128 * lane_e * (t + 4 * row_e) + 256 * (ro - ri))
    bc[...], _unused = cos_sin(128 * row_e * (t + 4 * lane_e) - 256 * (ro - ri))

    def twice(ref, n):
        w = ref[n, block].astype(F32)
        return jnp.concatenate([w, w], axis=1)

    w0, w1 = twice(second_w, 0), twice(second_w, 1)
    zero = jnp.zeros_like(w0)
    for half in range(2):
        def own(v):
            return (jnp.where(low, v, zero) if half == 0 else jnp.where(low, zero, v)).astype(BF16)

        re, im = slice(64 * half, 64 * half + 64), slice(128 + 64 * half, 192 + 64 * half)
        second_ref[re, :128], second_ref[re, 128:] = own(w0), own(w1)
        second_ref[im, :128], second_ref[im, 128:] = own(-w1), own(w0)

    w0, w1 = twice(first_w, 0), twice(first_w, 1)
    eye = jnp.where(iota((64, 128), 0) == (iota((64, 128), 1) & 63), 1.0, 0.0)
    for n in range(16):
        rows = slice(64 * n, 64 * n + 64)
        for lanes in (slice(0, 128), slice(128, 256)):
            first_ref[rows, lanes] = (
                fc[n : n + 1, lanes] * w0 + fs[n : n + 1, lanes] * w1
            ).astype(BF16)
            last_ref[rows, lanes] = (bc[n : n + 1, lanes] * eye).astype(BF16)


def block_tables(w_first, w_second):
    vmem = pl.BlockSpec(memory_space=pltpu.VMEM)
    return pl.pallas_call(
        blocks_kernel,
        grid=(1,),
        in_specs=[vmem, vmem],
        out_specs=[
            pl.BlockSpec((1024, 256), lambda g: (0, 0)),
            pl.BlockSpec((1024, 256), lambda g: (0, 0)),
            pl.BlockSpec((256, 256), lambda g: (0, 0)),
        ],
        out_shape=[pltpu.HBM((n, 256), BF16) for n in (1024, 1024, 256)],
        scratch_shapes=[pltpu.VMEM((16, 256), F32)] * 3,
        cost_estimate=pl.CostEstimate(flops=2**21, bytes_accessed=2**20, transcendentals=0),
        compiler_params=pltpu.CompilerParams(vmem_limit_bytes=6 * MIB),
        name="block_tables",
    )(w_first, w_second)


def low_half(rows):
    return lax.broadcasted_iota(jnp.int32, (rows, 128), 1) < 64


def swap(v):
    return pltpu.roll(v, 64, 1)


def normed_halves(x, gain_ref):
    ones = jnp.ones((256, 128), BF16)
    mean = dot(x, ones) * (1.0 / 256.0)
    d0, d1 = x[:, :128].astype(F32) - mean, x[:, 128:].astype(F32) - mean
    square = d0 * d0 + d1 * d1
    coarse = square.astype(BF16)
    fine = (square - coarse.astype(F32)).astype(BF16)
    var = dot(jnp.concatenate([coarse, fine], axis=1), ones) * (1.0 / 256.0)
    scale = lax.rsqrt(var + 1e-05)
    return d0 * scale * gain_ref[:, :128], d1 * scale * gain_ref[:, 128:]


def norm_kernel(x_any, gain_any, out_any, x_all, packed, gain, in_sems, out_sems, gain_sem):
    fetches, sends = [], []
    for n in range(2):
        rows = slice(16 * n, 16 * n + 16)
        fetches.append(pltpu.make_async_copy(x_any.at[rows], x_all.at[rows], in_sems.at[n]))
        fetches[-1].start()
    gain_fetch = pltpu.make_async_copy(gain_any, gain, gain_sem)
    gain_fetch.start()
    gain_fetch.wait()
    for n in range(2):
        fetches[n].wait()
        x = x_all[16 * n : 16 * n + 16].reshape(1024, 256)
        halves = [half.astype(BF16) for half in normed_halves(x, gain)]
        for g in range(2):
            first = 4 * (2 * n + g)
            for t in range(4):
                lanes = slice(128 * t, 128 * t + 128)
                for m in range(2):
                    a = halves[m][512 * g + 64 * t : 512 * g + 64 * t + 64]
                    b = halves[m][512 * g + 64 * t + 256 : 512 * g + 64 * t + 320]
                    packed[first + 2 * m, :, lanes] = beside((a[:, :64], b[:, :64]))
                    packed[first + 2 * m + 1, :, lanes] = beside((a[:, 64:], b[:, 64:]))
        parts = slice(8 * n, 8 * n + 8)
        sends.append(pltpu.make_async_copy(packed.at[parts], out_any.at[parts], out_sems.at[n]))
        sends[-1].start()
    for send in sends:
        send.wait()


def home_norm_kernel(x_ref, gain_ref, out_ref):
    for m, half in enumerate(normed_halves(x_ref[...].reshape(512, 256), gain_ref)):
        out_ref[:, :, 128 * m : 128 * m + 128] = half.astype(BF16).reshape(8, 64, 128)


def home_norm(patches, gain):
    block = pl.BlockSpec((8, 64, 256), lambda g: (g, 0, 0))
    return pl.pallas_call(
        home_norm_kernel,
        grid=(4,),
        in_specs=[block, pl.BlockSpec((1, 256), lambda g: (0, 0))],
        out_specs=block,
        out_shape=pltpu.HBM((32, 64, 256), BF16),
        cost_estimate=pl.CostEstimate(flops=2**24, bytes_accessed=2**21, transcendentals=0),
        compiler_params=pltpu.CompilerParams(vmem_limit_bytes=12 * MIB),
        name="home_norm",
    )(remaining(patches), remaining(gain.reshape(1, 256)))


def norm_and_pack(patches, gain):
    return pl.pallas_call(
        norm_kernel,
        in_specs=[pl.BlockSpec(memory_space=pltpu.HBM)] * 2,
        out_specs=pl.BlockSpec(memory_space=pltpu.HBM),
        out_shape=pltpu.HBM((16, 64, 512), BF16),
        scratch_shapes=[
            pltpu.VMEM((32, 64, 256), BF16),
            pltpu.VMEM((16, 64, 512), BF16),
            pltpu.VMEM((1, 256), F32),
            pltpu.SemaphoreType.DMA((2,)),
            pltpu.SemaphoreType.DMA((2,)),
            pltpu.SemaphoreType.DMA,
        ],
        compiler_params=pltpu.CompilerParams(vmem_limit_bytes=16 * MIB),
        name="norm_pack",
    )(remaining(patches), remaining(gain.reshape(1, 256)))


def final_kernel(base_ref, home_ref, out_any, held, sems):
    low = low_half(64)
    sends = []
    for g in range(4):
        for t in range(4):
            lanes = slice(128 * t, 128 * t + 128)
            for m in range(2):
                u = home_ref[4 * g + 2 * m, :, lanes].astype(F32)
                v = home_ref[4 * g + 2 * m + 1, :, lanes].astype(F32)
                chans, row = slice(128 * m, 128 * m + 128), 8 * g + t
                even, odd = jnp.where(low, u, swap(v)), jnp.where(low, swap(u), v)
                held[row, :, chans] = (base_ref[row, :, chans] + even).astype(BF16)
                held[row + 4, :, chans] = (base_ref[row + 4, :, chans] + odd).astype(BF16)
        rows = slice(8 * g, 8 * g + 8)
        sends.append(pltpu.make_async_copy(held.at[rows], out_any.at[rows], sems.at[g]))
        sends[-1].start()
    for send in sends:
        send.wait()


def unpack_and_add(base, home):
    return pl.pallas_call(
        final_kernel,
        in_specs=[pl.BlockSpec(memory_space=pltpu.VMEM)] * 2,
        out_specs=pl.BlockSpec(memory_space=pltpu.HBM),
        out_shape=pltpu.HBM((32, 64, 256), BF16),
        scratch_shapes=[pltpu.VMEM((32, 64, 256), BF16), pltpu.SemaphoreType.DMA((4,))],
        compiler_params=pltpu.CompilerParams(vmem_limit_bytes=8 * MIB),
        name="unpack_add",
    )(resident(base), resident(home))


def dot(a, b):
    return jnp.dot(a, b, preferred_element_type=F32)


def resident(v):
    return pltpu.with_memory_space_constraint(v, pltpu.VMEM)


def remaining(v):
    return pltpu.with_memory_space_constraint(v, pltpu.HBM)


def stream_dot(table, operand, held, out, sems):
    copies = []
    for m, rows in enumerate((slice(0, 512), slice(512, 896), slice(896, 1024))):
        held[rows, :] = dot(table[rows, :], operand[...]).astype(BF16)
        copies.append(pltpu.make_async_copy(held.at[rows, :], out.at[rows, :], sems.at[m]))
        copies[-1].start()
    for copy in copies:
        copy.wait()


def columns_kernel(table_ref, x_ref, out_any, held, sems):
    stream_dot(table_ref, x_ref, held, out_any, sems)


def columns(table, x):
    return pl.pallas_call(
        columns_kernel,
        in_specs=[pl.BlockSpec(memory_space=pltpu.VMEM)] * 2,
        out_specs=pl.BlockSpec(memory_space=pltpu.HBM),
        out_shape=pltpu.HBM((1024, 512), BF16),
        scratch_shapes=[pltpu.VMEM((1024, 512), BF16), pltpu.SemaphoreType.DMA((3,))],
        cost_estimate=pl.CostEstimate(flops=2**30, bytes_accessed=2**21, transcendentals=0),
        compiler_params=pltpu.CompilerParams(vmem_limit_bytes=12 * MIB),
        name="along_columns",
    )(resident(table), resident(x))


def stencil_kernel(
    x_ref, normed_ref, top_ref, bottom_ref, left_ref, right_ref, taps_ref, out_ref,
    rows, side, left_sum, right_sum,
):
    def tap(i, j):
        return taps_ref[3 * i + j : 3 * i + j + 1, :]

    @pl.when(pl.program_id(0) == 0)
    def _():
        rows[0], rows[33] = top_ref[...], bottom_ref[...]
        rows[1:33] = normed_ref[...]
        for rim_ref, sum_ref, j in ((left_ref, left_sum, 0), (right_ref, right_sum, 2)):
            side[...] = rim_ref[...].astype(F32)
            sum_ref[...] = side[0:32] * tap(0, j) + side[1:33] * tap(1, j) + side[2:34] * tap(2, j)

    column = iota((64, 256), 0)

    def step(r, carry):
        h = 8 * pl.program_id(0) + r
        around = [rows[h + i].astype(F32) for i in range(3)]

        def part(j):
            return around[0] * tap(0, j) + around[1] * tap(1, j) + around[2] * tap(2, j)

        left = jnp.where(column == 0, left_sum[pl.ds(h, 1), :], pltpu.roll(part(0), 1, 0))
        right = jnp.where(column == 63, right_sum[pl.ds(h, 1), :], pltpu.roll(part(2), 63, 0))
        out_ref[h] = x_ref[r].astype(F32) + (left + part(1) + right)
        return carry

    lax.fori_loop(0, 8, step, 0)


def stencil(x, normed, top, bottom, left, right, taps):
    block = pl.BlockSpec((8, 64, 256), lambda g: (g, 0, 0))
    row = pl.BlockSpec((64, 256), lambda g: (0, 0))
    side = pl.BlockSpec((34, 256), lambda g: (0, 0))
    return pl.pallas_call(
        stencil_kernel,
        grid=(4,),
        in_specs=[
            block,
            pl.BlockSpec((32, 64, 256), lambda g: (0, 0, 0)),
            row, row, side, side,
            pl.BlockSpec((9, 256), lambda g: (0, 0)),
        ],
        out_specs=pl.BlockSpec(memory_space=pltpu.VMEM),
        out_shape=pltpu.VMEM((32, 64, 256), F32),
        scratch_shapes=[
            pltpu.VMEM((34, 64, 256), BF16),
            pltpu.VMEM((34, 256), F32),
            pltpu.VMEM((32, 256), F32),
            pltpu.VMEM((32, 256), F32),
        ],
        cost_estimate=pl.CostEstimate(flops=2**24, bytes_accessed=2**22, transcendentals=0),
        compiler_params=pltpu.CompilerParams(vmem_limit_bytes=12 * MIB),
        name="stencil",
    )(*[remaining(v) for v in (x, normed, top, bottom, left, right, taps)])


def butterfly(x, sign):
    re, im = [v[:, :128] for v in x], [v[:, 128:] for v in x]

    def pair(v):
        return v[0] + v[2], v[0] - v[2], v[1] + v[3], v[1] - v[3]

    (er, dr, fr, gr), (ei, di, fi, gi) = pair(re), pair(im)
    plus, minus = (dr - gi, di + gr), (dr + gi, di - gr)
    if sign < 0:
        plus, minus = minus, plus
    return (er + fr, ei + fi), plus, (er - fr, ei - fi), minus


def beside(pair):
    return jnp.concatenate(pair, axis=1)


def middle_kernel(
    z, fwd, first_any, second_any, last_any, inv_any, out_any,
    cos_ref, sin_ref, first, second, last, inv, held, done, sems, fetch_sems,
):
    fetches = []
    for n, (src, dst) in enumerate(
        (
            (first_any, first),
            (second_any, second),
            (last_any, last),
            (inv_any, inv),
        )
    ):
        fetches.append(pltpu.make_async_copy(src, dst, fetch_sems.at[n]))
        fetches[-1].start()
    lane = iota((128, 512), 1)
    cos_ref[...], sin_ref[...] = cos_sin(
        iota((128, 512), 0) * ((lane >> 7) + 4 * digit(lane, 6, 1))
    )
    rows = 512 // CHUNKS
    groups = 8 // CHUNKS
    shape = (groups, 4, 16, 128)
    for m in range(CHUNKS):
        u = dot(fwd[2 * rows * m : 2 * rows * (m + 1), :], z[...])
        if m == 0:
            for fetch in fetches[:2]:
                fetch.wait()

        def twiddles(t):
            part = (slice(16 * groups * m, 16 * groups * (m + 1)), slice(128 * t, 128 * t + 128))
            return [ref[part].reshape(groups, 1, 16, 128) for ref in (cos_ref, sin_ref)]

        parts = []
        for t in range(4):
            ur = u[:rows, 128 * t : 128 * t + 128].reshape(shape)
            ui = u[rows:, 128 * t : 128 * t + 128].reshape(shape)
            c, s = twiddles(t)
            vr, vi = (ur * c + ui * s).reshape(rows, 128), (ui * c - ur * s).reshape(rows, 128)
            parts.append(dot(beside((vr.astype(BF16), vi.astype(BF16))), first[256 * t : 256 * t + 256, :]))
        kept = []
        for part in butterfly(parts, -1):
            v = dot(jnp.tanh(beside(part)).astype(BF16), second[...])
            kept.append(jnp.where(v > 0.25, v - 0.25, jnp.where(v < -0.25, v + 0.25, 0.0 * v)))
        if m == 0:
            fetches[2].wait()
        for t, part in enumerate(butterfly(kept, 1)):
            y = dot(beside(part).astype(BF16), last[256 * t : 256 * t + 256, :])
            yr, yi = y[:, :128].reshape(shape), y[:, 128:].reshape(shape)
            c, s = twiddles(t)
            lanes = slice(128 * t, 128 * t + 128)
            held[2 * rows * m : 2 * rows * m + rows, lanes] = (
                (yr * c - yi * s).astype(BF16).reshape(rows, 128)
            )
            held[2 * rows * m + rows : 2 * rows * (m + 1), lanes] = (
                (yi * c + yr * s).astype(BF16).reshape(rows, 128)
            )
    fetches[3].wait()
    stream_dot(inv, held, done, out_any, sems)


def middle(z, fwd, first, second, last, inv):
    vmem, hbm = pl.BlockSpec(memory_space=pltpu.VMEM), pl.BlockSpec(memory_space=pltpu.HBM)
    return pl.pallas_call(
        middle_kernel,
        in_specs=[vmem] * 2 + [hbm] * 4,
        out_specs=hbm,
        out_shape=pltpu.HBM((1024, 512), BF16),
        scratch_shapes=[
            pltpu.VMEM((128, 512), F32),
            pltpu.VMEM((128, 512), F32),
            pltpu.VMEM((1024, 256), BF16),
            pltpu.VMEM((256, 256), BF16),
            pltpu.VMEM((1024, 256), BF16),
            pltpu.VMEM((1024, 1024), BF16),
            pltpu.VMEM((1024, 512), BF16),
            pltpu.VMEM((1024, 512), BF16),
            pltpu.SemaphoreType.DMA((3,)),
            pltpu.SemaphoreType.DMA((4,)),
        ],
        cost_estimate=pl.CostEstimate(flops=3 * 2**30, bytes_accessed=2**21, transcendentals=2**19),
        compiler_params=pltpu.CompilerParams(vmem_limit_bytes=24 * MIB),
        name="filter_rows",
    )(
        resident(z), resident(fwd), *[remaining(v) for v in (first, second, last, inv)]
    )


def local(patches, norm_gain, w_first, w_second, depth_kernel):
    packed = norm_and_pack(patches, norm_gain)
    lines = lax.all_to_all(packed, ("yl", "x"), 0, 0, tiled=True).reshape(1024, 512)

    fwd_w = table(pltpu.VMEM, forward_columns_phases)
    inv_w = table(pltpu.VMEM, backward_columns_phases)
    inv_h = table(pltpu.HBM, backward_rows_phases)
    first, last, second = block_tables(w_first, w_second)
    fwd_h = table(pltpu.VMEM, forward_rows_phases, (second, inv_h))

    def neighbours(first, last, axis):
        n = lax.axis_size(axis)
        before = lax.ppermute(last, axis, [(i, (i + 1) % n) for i in range(n)])
        after = lax.ppermute(first, axis, [((i + 1) % n, i) for i in range(n)])
        return before, after

    lines, here = lax.optimization_barrier((lines, patches))
    normed = home_norm(here, norm_gain)

    freqs = columns(fwd_w, lines)
    whole = lax.all_to_all(freqs.reshape(128, 8, 512), ("row", "yl"), 0, 0, tiled=True)
    top, bottom = neighbours(normed[0], normed[31], "row")

    filtered = middle(whole.reshape(1024, 512), fwd_h, first, second, last, inv_h)
    filtered, top, bottom, normed = lax.optimization_barrier((filtered, top, bottom, normed))
    back = lax.all_to_all(filtered.reshape(128, 8, 512), ("row", "yl"), 0, 0, tiled=True)
    sides = [
        jnp.concatenate([top[w : w + 1], normed[:, w], bottom[w : w + 1]], axis=0) for w in (0, 63)
    ]
    left, right = neighbours(sides[0], sides[1], ("yl", "x"))
    back, left, right = lax.optimization_barrier((back, left, right))

    spectral = columns(inv_w, back.reshape(1024, 512))
    spectral, left, right = lax.optimization_barrier((spectral, left, right))
    home = lax.all_to_all(spectral.reshape(16, 64, 512), ("yl", "x"), 0, 0, tiled=True)
    base = stencil(patches, normed, top, bottom, left, right, depth_kernel.reshape(9, 256))
    return unpack_and_add(base, home)


def solution(mesh):
    fine = Mesh(np.asarray(mesh.devices).reshape(32, 4, 4), ("row", "yl", "x"))
    return jax.shard_map(
        local,
        mesh=fine,
        in_specs=(P("row", ("yl", "x"), None), P(), P(), P(), P()),
        out_specs=P("row", ("yl", "x"), None),
        check_vma=False,
    )
```
